256 devices in a mesh: tm: 64 (over y, z_hi, x, core), elem: 4 (over z_lo).
Axes of the slice: x: 4, y: 4, z: 8 (z_hi: 2, z_lo: 4; z = z_hi * 4 + z_lo), core: 2. Of those that a mesh axis runs over, the one named last changes fastest.
Arguments:
- samples: float32 [2, 512, 196608], P(None, 'elem', 'tm'), may hold values from -24 to 24
- shift_bin: int32 [1], replicated, may hold values from 1 to 63
- start_vectors: int32 [2, 512, 64], P(None, 'elem'), may hold values from 0 to 8
- tap_table: int32 [4, 1024], replicated, may hold values from -2048 to 2047
Outputs:
- spectra: float32 [2, 64, 192, 1024], P(None, 'elem', 'tm')
- weights: float32 [2, 512, 64], P(None, 'elem')
The draws below stay inside these ranges and needn't reach their ends.
All inputs are finite; a program needn't handle non-finite values.
Results may differ from the reference program's by a relative error of at most 0.0003.
Values sent between devices are 32-bit elements; how exact they have to be, the bound alone decides.
A program may use at most 128 MiB of HBM per device.

```python
import math
import jax
import jax.numpy as jnp
from jax import lax

ELEMS = 512
BEAMS = 64
CHANNELS = 1024
TAPS = 4
ITERS = 3
SPAN = 3072
SAMPLES = 196608


def draw_samples(key, part):
    keys = jax.random.split(jax.random.fold_in(key, 71), 2)
    noise = jnp.clip(jax.random.normal(keys[0], (2, ELEMS, SAMPLES), jnp.float32), -5.0, 5.0)
    scales = jnp.exp(jax.random.uniform(keys[1], (ELEMS,), jnp.float32, math.log(0.5), math.log(2.0)))
    ramp = 0.6 + 1.2 * jnp.arange(SAMPLES, dtype=jnp.float32) / SAMPLES
    return jnp.clip(noise * scales[None, :, None] * ramp[None, None, :], -24.0, 24.0)


def plant(result, key, least, high):
    longest = result.shape.index(max(result.shape))
    spots = []
    for shift in (0, 1):
        where = [jax.random.randint(jax.random.fold_in(key, axis), (), 0, length) for axis, length in enumerate(result.shape)]
        where[longest] = (where[longest] + shift) % result.shape[longest]
        spots.append(tuple(where))
    return result.at[spots[0]].set(least).at[spots[1]].set(high)


def setup_inputs(seed: int = 0) -> dict:
    key_of = jax.random.split(jax.random.key(seed), 5)
    samples = draw_samples(jax.random.fold_in(key_of[4], 71), 0)
    shift_bin = jax.random.randint(key_of[1], (1,), 1, 64).astype(jnp.int32)
    start_vectors = plant(jax.random.randint(key_of[2], (2, ELEMS, BEAMS), 0, 9), jax.random.fold_in(key_of[2], 1), 0, 8).astype(jnp.int32)
    tap_table = plant(jax.random.randint(key_of[3], (TAPS, CHANNELS), -2048, 2048), jax.random.fold_in(key_of[3], 1), -2048, 2047).astype(jnp.int32)
    return {"samples": samples, "shift_bin": shift_bin, "start_vectors": start_vectors, "tap_table": tap_table}


EPS = 1e-06
HIGH = lax.Precision.HIGHEST

def rotation(shift_bin, offset, count, modulus):
    times = offset + lax.iota(jnp.int32, count)
    folded = shift_bin[0] * times % modulus
    angle = 2.0 * math.pi / modulus * folded.astype(jnp.float32)
    return (jnp.cos(angle), jnp.sin(angle))

def stacked_left(sig_real, sig_imag, cos_table, sin_table):
    mod_real = sig_real * cos_table + sig_imag * sin_table
    mod_imag = sig_imag * cos_table - sig_real * sin_table
    return jnp.concatenate([sig_real, sig_imag, mod_real, mod_imag], 0)

def split_grams(grams, row_count, col_count):

    def block(row_block, col_block):
        return grams[row_block * row_count:(row_block + 1) * row_count, col_block * col_count:(col_block + 1) * col_count]
    return jnp.stack([block(0, 0) + block(1, 1), block(1, 0) - block(0, 1), block(2, 0) + block(3, 1), block(3, 0) - block(2, 1)])

def contract(left_rows, right_rows):
    return lax.dot_general(left_rows, right_rows, (((1,), (1,)), ((), ())), precision=HIGH, preferred_element_type=jnp.float32)

def matmul(left_rows, right_rows):
    return jnp.dot(left_rows, right_rows, precision=HIGH, preferred_element_type=jnp.float32)

def normalize(vector):
    squares = lax.optimization_barrier(jnp.sum(vector * vector, axis=(0, 1)))
    return vector / jnp.sqrt(squares + EPS)

def reference(samples, shift_bin, start_vectors, tap_table):
    total = samples.shape[2]
    elems = samples.shape[1]
    block_len = SPAN
    block_count = total // block_len

    def accumulate(index, grams):
        begin = (index * block_len).astype(jnp.int32)
        piece = lax.dynamic_slice_in_dim(samples, begin, block_len, 2)
        cos_table, sin_table = rotation(shift_bin, begin, block_len, total)
        left_rows = stacked_left(piece[0], piece[1], cos_table, sin_table)
        right_rows = jnp.concatenate([piece[0], piece[1]], 0)
        return grams + contract(left_rows, right_rows)
    grams = lax.fori_loop(0, block_count, accumulate, jnp.zeros((4 * elems, 2 * elems), jnp.float32))
    corr = split_grams(grams, elems, elems)
    plain_real = corr[0] / total
    plain_imag = corr[1] / total
    cyc_scale = 1.0 / math.sqrt(total * elems)
    cyc_real = corr[2] * cyc_scale
    cyc_imag = corr[3] * cyc_scale
    vector = normalize(start_vectors.astype(jnp.float32) - 4.5)
    for iteration in range(ITERS):
        vec_real, vec_imag = (vector[0], vector[1])
        adj_real = matmul(cyc_real.T, vec_real) + matmul(cyc_imag.T, vec_imag)
        adj_imag = matmul(cyc_real.T, vec_imag) - matmul(cyc_imag.T, vec_real)
        out_real = matmul(cyc_real, adj_real) - matmul(cyc_imag, adj_imag) + matmul(plain_real, vec_real) - matmul(plain_imag, vec_imag)
        out_imag = matmul(cyc_real, adj_imag) + matmul(cyc_imag, adj_real) + matmul(plain_real, vec_imag) + matmul(plain_imag, vec_real)
        vector = normalize(jnp.stack([out_real, out_imag]))
    vec_real, vec_imag = (vector[0], vector[1])
    beam_real = matmul(vec_real.T, samples[0]) + matmul(vec_imag.T, samples[1])
    beam_imag = matmul(vec_real.T, samples[1]) - matmul(vec_imag.T, samples[0])
    beam_series = jnp.stack([beam_real, beam_imag])
    rim = (TAPS - 1) * CHANNELS
    padded = jnp.pad(beam_series, ((0, 0), (0, 0), (rim, 0)))
    frames = total // CHANNELS
    shaped = padded.reshape(2, beam_series.shape[1], TAPS - 1 + frames, CHANNELS)
    taps = tap_table.astype(jnp.float32) / 2048.0
    folded = jnp.zeros((2, beam_series.shape[1], frames, CHANNELS), jnp.float32)
    for tap in range(TAPS):
        folded = folded + taps[tap] * shaped[:, :, TAPS - 1 - tap:TAPS - 1 - tap + frames, :]
    spectrum = jnp.fft.fft(folded[0] + 1j * folded[1], axis=-1) / math.sqrt(CHANNELS)
    spectra = jnp.stack([jnp.real(spectrum), jnp.imag(spectrum)]).astype(folded.dtype)
    return (spectra, vector)
```

```python
import functools
import math

import jax
import jax.numpy as jnp
import ml_dtypes
import numpy as np
from jax import lax
from jax.experimental import pallas as pl
from jax.experimental.pallas import tpu as pltpu
from jax.sharding import PartitionSpec as P

ELEMS = 512
BEAMS = 64
CHANNELS = 1024
TAPS = 4
ITERS = 3
SPAN = 3072
SAMPLES = 196608
FRAMES = SPAN // CHANNELS
GROUP = 4
OWN = ELEMS // GROUP
PART = CHANNELS // GROUP
TM = SAMPLES // SPAN
QUARTER = BEAMS // GROUP

EPS = 1e-06
F32 = jnp.float32
BF16 = jnp.bfloat16
MESH = pl.DeviceIdType.MESH
VMEM_LIMIT = 56 * 1024 * 1024

CORR_ROWS = 3 * 4 * ELEMS
HALF = CORR_ROWS // 2
SEG = HALF // 3
AXIS_SIZE = {"x": 4, "y": 4, "z": 8}
ORDERS = (("x", "y", "z"), ("y", "z", "x"), ("z", "x", "y"))


def split(value):
    high = value.astype(BF16)
    return high, (value - high.astype(F32)).astype(BF16)


def dot_nt(left, right):
    return lax.dot_general(left, right, (((1,), (1,)), ((), ())), preferred_element_type=F32)


def dot_nn(left, right):
    return lax.dot_general(left, right, (((1,), (0,)), ((), ())), preferred_element_type=F32)


def cat(*pieces):
    return jnp.concatenate(pieces, axis=1)


def corr_kernel(x_ref, start_ref, cos_ref, sin_ref, x_out, start_out, g_ref, xg, sg, rh, rl, uh, ul,
                send_sem, recv_sem, own_sem, out_sem, s_send, s_recv):
    me = lax.axis_index("elem")
    barrier = pltpu.get_barrier_semaphore()
    for off in range(1, GROUP):
        pl.semaphore_signal(barrier, inc=1, device_id={"elem": lax.rem(me + off, GROUP)}, device_id_type=MESH)
    pl.semaphore_wait(barrier, GROUP - 1)

    def start_copy(off):
        peer = lax.rem(me + off, GROUP)
        return pltpu.make_async_remote_copy(
            src_ref=start_ref, dst_ref=sg.at[pl.ds(pl.multiple_of(me * OWN, OWN), OWN), :],
            send_sem=s_send.at[off], recv_sem=s_recv.at[off], device_id={"elem": peer}, device_id_type=MESH)

    def sample_copy(frame, off):
        peer = lax.rem(me + off, GROUP)
        col = pl.multiple_of(frame * CHANNELS + peer * PART, PART)
        return pltpu.make_async_remote_copy(
            src_ref=x_ref.at[:, :, pl.ds(col, PART)],
            dst_ref=xg.at[frame, :, pl.ds(pl.multiple_of(me * OWN, OWN), OWN), :],
            send_sem=send_sem.at[frame, off], recv_sem=recv_sem.at[frame, off],
            device_id={"elem": peer}, device_id_type=MESH)

    def own_copy(frame):
        col = pl.multiple_of(frame * CHANNELS + me * PART, PART)
        return pltpu.make_async_copy(
            x_ref.at[:, :, pl.ds(col, PART)],
            xg.at[frame, :, pl.ds(pl.multiple_of(me * OWN, OWN), OWN), :], own_sem.at[frame])

    def out_copy(frame):
        return pltpu.make_async_copy(xg.at[frame], x_out.at[frame], out_sem.at[frame])

    for frame in range(FRAMES):
        for off in (2, 1, 3):
            sample_copy(frame, off).start()
        own_copy(frame).start()
    for off in range(1, GROUP):
        start_copy(off).start()
    sg[pl.ds(pl.multiple_of(me * OWN, OWN), OWN), :] = start_ref[...]
    g_ref[...] = jnp.zeros_like(g_ref)

    def one_frame(frame, carry):
        own_copy(frame).wait()
        for off in range(1, GROUP):
            sample_copy(frame, off).wait_recv()
        out_copy(frame).start()
        cos_row = cos_ref[pl.ds(frame, 1), :]
        sin_row = sin_ref[pl.ds(frame, 1), :]

        def prepare(block, carry2):
            rows = pl.ds(pl.multiple_of(block * 128, 128), 128)
            real = xg[frame, 0, rows, :]
            imag = xg[frame, 1, rows, :]
            high, low = split(cat(real, imag))
            rh[rows, :] = high
            rl[rows, :] = low
            high, low = split(cat(real * cos_row + imag * sin_row, imag * cos_row - real * sin_row))
            uh[rows, :] = high
            ul[rows, :] = low
            return carry2

        lax.fori_loop(0, 4, prepare, 0)
        right = cat(rh[...], rl[...], rh[...])

        def left_of(high_ref, low_ref, rows, imag):
            high = high_ref[rows, :]
            low = low_ref[rows, :]
            if imag:
                high = cat(high[:, PART:], -high[:, :PART])
                low = cat(low[:, PART:], -low[:, :PART])
            return cat(high, high, low)

        def cyclic(block, carry2):
            rows = pl.ds(pl.multiple_of(block * 256, 256), 256)
            for imag in (0, 1):
                out = dot_nt(left_of(uh, ul, rows, imag), right)
                for col in range(4):
                    g_ref[1 + imag, col, rows, :] += out[:, col * 128:(col + 1) * 128]
            return carry2

        lax.fori_loop(0, 2, cyclic, 0)
        upper = lax.broadcasted_iota(jnp.int32, (256, 256), 0) <= lax.broadcasted_iota(jnp.int32, (256, 256), 1)
        top = pl.ds(0, 256)
        bottom = pl.ds(256, 256)
        out = dot_nt(left_of(rh, rl, top, 0), right)
        diag = jnp.where(upper, out[:, :256], dot_nt(left_of(rh, rl, top, 1), right[:256]))
        g_ref[0, 0, top, :] += diag[:, :128]
        g_ref[0, 1, top, :] += diag[:, 128:]
        g_ref[0, 2, top, :] += out[:, 256:384]
        g_ref[0, 3, top, :] += out[:, 384:]
        out = dot_nt(left_of(rh, rl, bottom, 1), right)
        diag = jnp.where(upper, dot_nt(left_of(rh, rl, bottom, 0), right[256:]), out[:, 256:])
        g_ref[0, 0, bottom, :] += out[:, :128]
        g_ref[0, 1, bottom, :] += out[:, 128:256]
        g_ref[0, 2, bottom, :] += diag[:, :128]
        g_ref[0, 3, bottom, :] += diag[:, 128:]
        return carry

    lax.fori_loop(0, FRAMES, one_frame, 0)
    for off in range(1, GROUP):
        start_copy(off).wait()
    start_out[...] = sg[...]
    for frame in range(FRAMES):
        out_copy(frame).wait()
        for off in range(1, GROUP):
            sample_copy(frame, off).wait_send()


def gather_and_correlate(samples, start, cos_rows, sin_rows):
    vmem = pl.BlockSpec(memory_space=pltpu.VMEM)
    hbm = pl.BlockSpec(memory_space=pl.ANY)
    return pl.pallas_call(
        corr_kernel,
        out_shape=(
            jax.ShapeDtypeStruct((FRAMES, 2, ELEMS, PART), F32),
            jax.ShapeDtypeStruct((ELEMS, 2 * BEAMS), F32),
            jax.ShapeDtypeStruct((3, 4, ELEMS, 128), F32),
        ),
        in_specs=[hbm, vmem, vmem, vmem],
        out_specs=(hbm, vmem, vmem),
        scratch_shapes=[
            pltpu.VMEM((FRAMES, 2, ELEMS, PART), F32),
            pltpu.VMEM((ELEMS, 2 * BEAMS), F32),
            pltpu.VMEM((ELEMS, 2 * PART), BF16),
            pltpu.VMEM((ELEMS, 2 * PART), BF16),
            pltpu.VMEM((ELEMS, 2 * PART), BF16),
            pltpu.VMEM((ELEMS, 2 * PART), BF16),
            pltpu.SemaphoreType.DMA((FRAMES, GROUP)),
            pltpu.SemaphoreType.DMA((FRAMES, GROUP)),
            pltpu.SemaphoreType.DMA((FRAMES,)),
            pltpu.SemaphoreType.DMA((FRAMES,)),
            pltpu.SemaphoreType.DMA((GROUP,)),
            pltpu.SemaphoreType.DMA((GROUP,)),
        ],
        compiler_params=pltpu.CompilerParams(
            collective_id=0, has_side_effects=True, vmem_limit_bytes=VMEM_LIMIT),
        name="gather_correlate",
    )(samples, start, cos_rows, sin_rows)


def place():
    tm = lax.axis_index("tm")
    elem = lax.axis_index("elem")
    core = lax.rem(tm, 2)
    return {
        "core": core,
        "x": lax.rem(tm // 2, 4),
        "y": tm // 16,
        "z": lax.rem(tm // 8, 2) * 4 + elem,
    }


def device_at(spot, axis, value):
    at = dict(spot)
    at[axis] = value
    tm = ((at["y"] * 2 + at["z"] // 4) * 4 + at["x"]) * 2 + at["core"]
    return {"tm": tm, "elem": lax.rem(at["z"], 4)}


def reduce_kernel(g_ref, o_ref, w_ref, c_ref, *refs):
    slots = refs[:9]
    core_send, core_recv, rs_send, rs_recv, ag_send, ag_recv = refs[9:]
    spot = place()
    barrier = pltpu.get_barrier_semaphore()
    count = 0
    for axis, size in (("core", 2), ("x", 4), ("y", 4), ("z", 8)):
        for off in range(1, size):
            pl.semaphore_signal(
                barrier, inc=1, device_id=device_at(spot, axis, lax.rem(spot[axis] + off, size)),
                device_id_type=MESH)
            count += 1
    pl.semaphore_wait(barrier, count)

    core = spot["core"]
    sibling = device_at(spot, "core", 1 - core)

    def core_rs(part):
        rows = pl.ds(pl.multiple_of((1 - core) * HALF + part * SEG, SEG), SEG)
        return pltpu.make_async_remote_copy(
            src_ref=g_ref.at[rows, :], dst_ref=c_ref.at[pl.ds(part * SEG, SEG), :],
            send_sem=core_send.at[part], recv_sem=core_recv.at[part], device_id=sibling, device_id_type=MESH)

    for part in (2, 0, 1):
        core_rs(part).start()

    def index(part, stage, off):
        return part * 24 + stage * 8 + off

    def lengths(part):
        out = [SEG]
        for axis in ORDERS[part]:
            out.append(out[-1] // AXIS_SIZE[axis])
        return out

    starts = [[part * SEG] for part in range(3)]
    for part in range(3):
        for stage, axis in enumerate(ORDERS[part]):
            starts[part].append(starts[part][-1] + spot[axis] * lengths(part)[stage + 1])

    def rs_copy(part, stage, off):
        axis = ORDERS[part][stage]
        size = AXIS_SIZE[axis]
        length = lengths(part)[stage + 1]
        peer = lax.rem(spot[axis] + off, size)
        source = pl.multiple_of(starts[part][stage] + peer * length, 8)
        return pltpu.make_async_remote_copy(
            src_ref=w_ref.at[pl.ds(source, length), :],
            dst_ref=slots[part * 3 + stage].at[off],
            send_sem=rs_send.at[index(part, stage, off)], recv_sem=rs_recv.at[index(part, stage, off)],
            device_id=device_at(spot, axis, peer), device_id_type=MESH)

    def ag_copy(part, stage, off):
        axis = ORDERS[part][stage]
        size = AXIS_SIZE[axis]
        length = lengths(part)[stage + 1]
        peer = lax.rem(spot[axis] + off, size)
        where = pl.ds(pl.multiple_of(core * HALF + starts[part][stage + 1], 8), length)
        return pltpu.make_async_remote_copy(
            src_ref=o_ref.at[where, :], dst_ref=o_ref.at[where, :],
            send_sem=ag_send.at[index(part, stage, off)], recv_sem=ag_recv.at[index(part, stage, off)],
            device_id=device_at(spot, axis, peer), device_id_type=MESH)

    def core_ag(part):
        rows = pl.ds(pl.multiple_of(core * HALF + part * SEG, SEG), SEG)
        return pltpu.make_async_remote_copy(
            src_ref=o_ref.at[rows, :], dst_ref=o_ref.at[rows, :],
            send_sem=core_send.at[3 + part], recv_sem=core_recv.at[3 + part],
            device_id=sibling, device_id_type=MESH)

    def peers(part, stage):
        return range(1, AXIS_SIZE[ORDERS[part][stage]])

    for part in (2, 0, 1):
        core_rs(part).wait_recv()
        rows = pl.ds(pl.multiple_of(core * HALF + part * SEG, SEG), SEG)
        w_ref[pl.ds(part * SEG, SEG), :] = g_ref[rows, :] + c_ref[pl.ds(part * SEG, SEG), :]
        for off in peers(part, 0):
            rs_copy(part, 0, off).start()
    for stage in range(3):
        for part in (0, 1, 2):
            for off in peers(part, stage):
                rs_copy(part, stage, off).wait_recv()
            length = lengths(part)[stage + 1]
            rows = pl.ds(pl.multiple_of(starts[part][stage + 1], 8), length)
            total = w_ref[rows, :]
            for off in peers(part, stage):
                total = total + slots[part * 3 + stage][off]
            if stage < 2:
                w_ref[rows, :] = total
                for off in peers(part, stage + 1):
                    rs_copy(part, stage + 1, off).start()
            else:
                o_ref[pl.ds(pl.multiple_of(core * HALF + starts[part][3], 8), length), :] = total
                for off in peers(part, 2):
                    ag_copy(part, 2, off).start()
    for stage in (2, 1, 0):
        for part in (0, 1, 2):
            for off in peers(part, stage):
                ag_copy(part, stage, off).wait_recv()
            if stage > 0:
                for off in peers(part, stage - 1):
                    ag_copy(part, stage - 1, off).start()
            else:
                core_ag(part).start()
    for part in range(3):
        core_ag(part).wait_recv()
    for part in range(3):
        core_rs(part).wait_send()
        core_ag(part).wait_send()
        for stage in range(3):
            for off in peers(part, stage):
                rs_copy(part, stage, off).wait_send()
                ag_copy(part, stage, off).wait_send()


def reduce_all(partial):
    vmem = pl.BlockSpec(memory_space=pltpu.VMEM)
    slots = []
    for order in ORDERS:
        length = SEG
        for axis in order:
            length //= AXIS_SIZE[axis]
            slots.append(pltpu.VMEM((AXIS_SIZE[axis], length, 128), F32))
    return pl.pallas_call(
        reduce_kernel,
        out_shape=jax.ShapeDtypeStruct((CORR_ROWS, 128), F32),
        in_specs=[vmem],
        out_specs=vmem,
        scratch_shapes=[
            pltpu.VMEM((HALF, 128), F32),
            pltpu.VMEM((HALF, 128), F32),
            *slots,
            pltpu.SemaphoreType.DMA((6,)),
            pltpu.SemaphoreType.DMA((6,)),
            pltpu.SemaphoreType.DMA((72,)),
            pltpu.SemaphoreType.DMA((72,)),
            pltpu.SemaphoreType.DMA((72,)),
            pltpu.SemaphoreType.DMA((72,)),
        ],
        compiler_params=pltpu.CompilerParams(
            collective_id=1, has_side_effects=True, vmem_limit_bytes=VMEM_LIMIT),
        name="reduce_correlations",
    )(partial.reshape(CORR_ROWS, 128))


def power_kernel(o_ref, start_ref, v_ref, weights_ref, ah, al, bh, bl):
    def wide(index, rows):
        base = index * 4 * ELEMS
        return cat(*[o_ref[pl.ds(base + col * ELEMS + rows, 128), :] for col in range(4)])

    plain_scale = 1.0 / SAMPLES
    cyc_scale = 1.0 / math.sqrt(SAMPLES * ELEMS)

    def full(index):
        return jnp.concatenate([wide(index, rows) for rows in range(0, ELEMS, 128)], axis=0)

    def put(high_ref, low_ref, col, value):
        high, low = split(value)
        high_ref[:, col * ELEMS:(col + 1) * ELEMS] = high
        low_ref[:, col * ELEMS:(col + 1) * ELEMS] = low

    packed = full(0) * plain_scale
    flipped = packed.T
    row_ids = lax.broadcasted_iota(jnp.int32, (ELEMS, ELEMS), 0)
    col_ids = lax.broadcasted_iota(jnp.int32, (ELEMS, ELEMS), 1)
    put(ah, al, 2, jnp.where(row_ids <= col_ids, packed, flipped))
    put(ah, al, 3, jnp.where(row_ids > col_ids, packed, jnp.where(row_ids < col_ids, -flipped, 0.0)))
    cyc_real = full(1) * cyc_scale
    put(ah, al, 0, cyc_real)
    put(bh, bl, 0, cyc_real.T)
    cyc_imag = full(2) * cyc_scale
    put(ah, al, 1, cyc_imag)
    put(bh, bl, 1, -cyc_imag.T)

    lane = lax.broadcasted_iota(jnp.int32, (ELEMS, 2 * BEAMS), 1)

    def turned(vector):
        other = pltpu.roll(vector, BEAMS, 1)
        return jnp.where(lane < BEAMS, -other, other)

    def normalized(vector):
        squares = jnp.sum(vector * vector, axis=0, keepdims=True)
        squares = jnp.broadcast_to(squares, (8, 2 * BEAMS))
        squares = squares + pltpu.roll(squares, BEAMS, 1)
        return vector * (1.0 / jnp.sqrt(squares[:1] + EPS))

    def stacked(vector):
        high, low = split(jnp.concatenate([vector, turned(vector)], axis=0))
        return cat(high, low)

    def product(high, low, right):
        wide_out = dot_nn(high, right)
        return wide_out[:, :2 * BEAMS] + wide_out[:, 2 * BEAMS:] + dot_nn(low, right[:, :2 * BEAMS])

    v_ref[...] = normalized(start_ref[...])

    def step(iteration, carry):
        held = stacked(v_ref[...])
        mid = product(bh[...], bl[...], held)
        right = jnp.concatenate([stacked(mid), held], axis=0)
        v_ref[...] = normalized(product(ah[...], al[...], right))
        return carry

    lax.fori_loop(0, ITERS, step, 0)
    rows = pl.ds(pl.multiple_of(lax.axis_index("elem") * OWN, OWN), OWN)
    mine = v_ref[rows, :]
    weights_ref[0] = mine[:, :BEAMS]
    weights_ref[1] = pltpu.roll(mine, BEAMS, 1)[:, :BEAMS]


def power(total, start):
    vmem = pl.BlockSpec(memory_space=pltpu.VMEM)
    return pl.pallas_call(
        power_kernel,
        out_shape=(
            jax.ShapeDtypeStruct((ELEMS, 2 * BEAMS), F32),
            jax.ShapeDtypeStruct((2, OWN, BEAMS), F32),
        ),
        in_specs=[vmem, vmem],
        out_specs=(vmem, vmem),
        scratch_shapes=[
            pltpu.VMEM((ELEMS, 4 * ELEMS), BF16),
            pltpu.VMEM((ELEMS, 4 * ELEMS), BF16),
            pltpu.VMEM((ELEMS, 2 * ELEMS), BF16),
            pltpu.VMEM((ELEMS, 2 * ELEMS), BF16),
        ],
        compiler_params=pltpu.CompilerParams(vmem_limit_bytes=VMEM_LIMIT),
        name="power_iterations",
    )(total, start)


def dft_tables():
    ids = np.arange(CHANNELS)
    angle = 2.0 * np.pi / CHANNELS * (ids[:, None] * ids[None, :] % CHANNELS)
    out = []
    for table in (np.cos(angle), np.sin(angle)):
        table = (table / math.sqrt(CHANNELS)).astype(np.float32)
        high = table.astype(ml_dtypes.bfloat16)
        out += [high, (table - high.astype(np.float32)).astype(ml_dtypes.bfloat16)]
    return np.stack(out)


def beam_kernel(x_ref, v_ref, tap_ref, table_ref, out_ref, table, own, after, got_own, got_before,
                table_sem, own_send, own_recv, next_send, next_recv):
    tm = lax.axis_index("tm")
    me = lax.axis_index("elem")
    table_copy = pltpu.make_async_copy(table_ref, table, table_sem)
    table_copy.start()
    barrier = pltpu.get_barrier_semaphore()
    for off in range(1, GROUP):
        pl.semaphore_signal(barrier, inc=1, device_id={"elem": lax.rem(me + off, GROUP)}, device_id_type=MESH)

    @pl.when(tm > 0)
    def _():
        for peer in range(GROUP):
            pl.semaphore_signal(barrier, inc=1, device_id={"tm": tm - 1, "elem": peer}, device_id_type=MESH)

    @pl.when(tm < TM - 1)
    def _():
        for peer in range(GROUP):
            pl.semaphore_signal(barrier, inc=1, device_id={"tm": tm + 1, "elem": peer}, device_id_type=MESH)

    vt = v_ref[...].T
    vh, vl = split(vt)
    left = jnp.concatenate([vh, vl], axis=0)
    taps = tap_ref[...].astype(F32) / 2048.0

    beams_real = []
    beams_imag = []
    for frame in range(FRAMES):
        xh, xl = split(cat(x_ref[frame, 0], x_ref[frame, 1]))
        both = dot_nn(left, xh)
        out = both[:2 * BEAMS] + both[2 * BEAMS:] + dot_nn(vh, xl)
        beams_real.append(out[:BEAMS, :PART] + out[BEAMS:, PART:])
        beams_imag.append(out[:BEAMS, PART:] - out[BEAMS:, :PART])
    for kind, beams in enumerate((beams_real, beams_imag)):
        for frame in range(2 * FRAMES):
            total = None
            for tap in range(TAPS):
                if 0 <= frame - tap < FRAMES:
                    term = taps[tap:tap + 1, :] * beams[frame - tap]
                    total = term if total is None else total + term
            if frame < FRAMES:
                own[kind, frame] = total
            else:
                after[kind, frame - FRAMES] = total

    pl.semaphore_wait(
        barrier, GROUP - 1 + GROUP * ((tm > 0).astype(jnp.int32) + (tm < TM - 1).astype(jnp.int32)))

    def next_copy(off):
        peer = lax.rem(me + off, GROUP)
        rows = pl.ds(pl.multiple_of(peer * QUARTER, QUARTER), QUARTER)
        return pltpu.make_async_remote_copy(
            src_ref=after.at[:, :, rows, :], dst_ref=got_before.at[me],
            send_sem=next_send.at[off], recv_sem=next_recv.at[off],
            device_id={"tm": tm + 1, "elem": peer}, device_id_type=MESH)

    def own_copy(off):
        peer = lax.rem(me + off, GROUP)
        rows = pl.ds(pl.multiple_of(peer * QUARTER, QUARTER), QUARTER)
        return pltpu.make_async_remote_copy(
            src_ref=own.at[:, :, rows, :], dst_ref=got_own.at[me],
            send_sem=own_send.at[off], recv_sem=own_recv.at[off],
            device_id={"elem": peer}, device_id_type=MESH)

    @pl.when(tm < TM - 1)
    def _():
        for off in range(GROUP):
            next_copy(off).start()

    for off in (2, 1, 3):
        own_copy(off).start()
    got_own[me] = own[:, :, pl.ds(pl.multiple_of(me * QUARTER, QUARTER), QUARTER), :]
    for off in range(1, GROUP):
        own_copy(off).wait_recv()

    @pl.when(tm > 0)
    def _():
        for off in range(GROUP):
            next_copy(off).wait_recv()
        got_own[...] = got_own[...] + got_before[...]

    table_copy.wait()
    rows = 2 * FRAMES * QUARTER
    wide = cat(*[got_own[part].reshape(rows, PART) for part in range(GROUP)])
    high, low = split(wide)
    left = jnp.concatenate([high, low], axis=0)

    def times(index):
        both = dot_nn(left, table[index])
        return both[:rows] + both[rows:] + dot_nn(high, table[index + 1])

    with_cos = times(0)
    with_sin = times(2)
    half = FRAMES * QUARTER
    out_ref[0] = with_cos[:half] + with_sin[half:]
    out_ref[1] = with_cos[half:] - with_sin[:half]
    for off in range(1, GROUP):
        own_copy(off).wait_send()

    @pl.when(tm < TM - 1)
    def _():
        for off in range(GROUP):
            next_copy(off).wait_send()


def beamform(x_all, vectors, taps, table):
    vmem = pl.BlockSpec(memory_space=pltpu.VMEM)
    hbm = pl.BlockSpec(memory_space=pl.ANY)
    return pl.pallas_call(
        beam_kernel,
        out_shape=jax.ShapeDtypeStruct((2, FRAMES * QUARTER, CHANNELS), F32),
        in_specs=[vmem, vmem, vmem, hbm],
        out_specs=vmem,
        scratch_shapes=[
            pltpu.VMEM((4, CHANNELS, CHANNELS), BF16),
            pltpu.VMEM((2, FRAMES, BEAMS, PART), F32),
            pltpu.VMEM((2, FRAMES, BEAMS, PART), F32),
            pltpu.VMEM((GROUP, 2, FRAMES, QUARTER, PART), F32),
            pltpu.VMEM((GROUP, 2, FRAMES, QUARTER, PART), F32),
            pltpu.SemaphoreType.DMA,
            pltpu.SemaphoreType.DMA((GROUP,)),
            pltpu.SemaphoreType.DMA((GROUP,)),
            pltpu.SemaphoreType.DMA((GROUP,)),
            pltpu.SemaphoreType.DMA((GROUP,)),
        ],
        compiler_params=pltpu.CompilerParams(
            collective_id=2, has_side_effects=True, vmem_limit_bytes=VMEM_LIMIT),
        name="beams_transform",
    )(x_all, vectors, taps, table)


def body(samples, shift_bin, start_vectors, tap_table):
    me = lax.axis_index("elem")
    frame_ids = lax.broadcasted_iota(jnp.int32, (FRAMES, PART), 0)
    chan_ids = lax.broadcasted_iota(jnp.int32, (FRAMES, PART), 1)
    times = lax.axis_index("tm") * SPAN + frame_ids * CHANNELS + me * PART + chan_ids
    folded = shift_bin[0] * times % SAMPLES
    angle = 2.0 * math.pi / SAMPLES * folded.astype(F32)
    start = jnp.concatenate([start_vectors[0], start_vectors[1]], axis=1).astype(F32) - 4.5
    x_all, start_all, partial = gather_and_correlate(samples, start, jnp.cos(angle), jnp.sin(angle))
    total = reduce_all(partial)
    vectors, weights = power(total, start_all)
    taps = lax.dynamic_slice_in_dim(tap_table, me * PART, PART, 1)
    spectra = beamform(x_all, vectors, taps, jnp.asarray(dft_tables()))
    spectra = spectra.reshape(2, FRAMES, QUARTER, CHANNELS).transpose(0, 2, 1, 3)
    return (spectra, weights)


def solution(mesh):
    return jax.shard_map(
        body,
        mesh=mesh,
        in_specs=(P(None, "elem", "tm"), P(), P(None, "elem", None), P()),
        out_specs=(P(None, "elem", "tm", None), P(None, "elem", None)),
        check_vma=False,
    )
```

```python
import math

import jax
import jax.numpy as jnp
import ml_dtypes
import numpy as np
from jax import lax
from jax.experimental import pallas as pl
from jax.experimental.pallas import tpu as pltpu
from jax.sharding import PartitionSpec as P

ELEMS = 512
BEAMS = 64
CHANNELS = 1024
TAPS = 4
ITERS = 3
SPAN = 3072
SAMPLES = 196608
FRAMES = SPAN // CHANNELS
GROUP = 4
OWN = ELEMS // GROUP
PART = CHANNELS // GROUP
TM = SAMPLES // SPAN
QUARTER = BEAMS // GROUP

EPS = 1e-06
F32 = jnp.float32
BF16 = jnp.bfloat16
MESH = pl.DeviceIdType.MESH
VMEM_LIMIT = 56 * 1024 * 1024

CHUNK = 128
CHUNKS = SPAN // GROUP // CHUNK
BLOCK = 128
SIZES = {"core": 2, "x": 4, "y": 4, "z": 8}
PLANE = (("x", "y"), ("y", "x"))


def split(value):
    high = value.astype(BF16)
    return high, (value - high.astype(F32)).astype(BF16)


def dot_nt(left, right):
    return lax.dot_general(left, right, (((1,), (1,)), ((), ())), preferred_element_type=F32)


def dot_nn(left, right):
    return lax.dot_general(left, right, (((1,), (0,)), ((), ())), preferred_element_type=F32)


def cat(*pieces):
    return jnp.concatenate(pieces, axis=1)


def dft_tables():
    ids = np.arange(CHANNELS)
    angle = 2.0 * np.pi / CHANNELS * (ids[:, None] * ids[None, :] % CHANNELS)
    out = []
    for table in (np.cos(angle), np.sin(angle)):
        table = (table / math.sqrt(CHANNELS)).astype(np.float32)
        high = table.astype(ml_dtypes.bfloat16)
        out += [high, (table - high.astype(np.float32)).astype(ml_dtypes.bfloat16)]
    return np.stack(out)


def place():
    tm = lax.axis_index("tm")
    return {
        "core": lax.rem(tm, 2),
        "x": lax.rem(tm // 2, 4),
        "y": tm // 16,
        "z": lax.rem(tm // 8, 2) * 4 + lax.axis_index("elem"),
    }


def device_at(spot, axis, value):
    at = dict(spot)
    at[axis] = value
    tm = ((at["y"] * 2 + at["z"] // 4) * 4 + at["x"]) * 2 + at["core"]
    return {"tm": tm, "elem": lax.rem(at["z"], 4)}


def aligned(start, size):
    return pl.ds(pl.multiple_of(start, size), size)


def kernel(x_ref, start_ref, shift_ref, tap_ref, table_ref, out_ref, weights_ref,
           xg, sg, phase, rh, rl, uh, ul, g, o, pair_got, first_got, second_got, z_got, v_ref, ah, al, bh, bl,
           table, own, after, halo, got, crossed,
           send_sem, recv_sem, own_sem, s_send, s_recv, table_sem,
           pair_send, pair_recv, rs_send, rs_recv, z_send, z_recv, az_send, az_recv, ag_send, ag_recv,
           fw_send, fw_recv, halo_send, halo_recv, cross_send, cross_recv, last_send, last_recv):
    tm = lax.axis_index("tm")
    me = lax.axis_index("elem")
    spot = place()
    core = spot["core"]

    table_copy = pltpu.make_async_copy(table_ref, table, table_sem)
    table_copy.start()

    barrier = pltpu.get_barrier_semaphore()
    count = 0
    for axis, size in SIZES.items():
        for off in range(1, size):
            pl.semaphore_signal(
                barrier, inc=1, device_id=device_at(spot, axis, lax.rem(spot[axis] + off, size)),
                device_id_type=MESH)
            count += 1
    turn = lax.rem(tm, 8)
    near_out = turn != 7
    near_in = turn != 0
    cross_out = jnp.logical_and(turn == 7, tm < TM - 1)
    cross_in = jnp.logical_and(turn == 0, tm > 0)

    @pl.when(near_out)
    def _():
        pl.semaphore_signal(barrier, inc=1, device_id={"tm": tm + 1, "elem": me}, device_id_type=MESH)

    @pl.when(near_in)
    def _():
        pl.semaphore_signal(barrier, inc=1, device_id={"tm": tm - 1, "elem": me}, device_id_type=MESH)

    @pl.when(cross_out)
    def _():
        for peer in range(GROUP):
            pl.semaphore_signal(barrier, inc=1, device_id={"tm": tm + 1, "elem": peer}, device_id_type=MESH)

    @pl.when(cross_in)
    def _():
        for peer in range(GROUP):
            pl.semaphore_signal(barrier, inc=1, device_id={"tm": tm - 1, "elem": peer}, device_id_type=MESH)

    number = lambda flag: flag.astype(jnp.int32)
    pl.semaphore_wait(
        barrier, count + number(near_out) + number(near_in) + GROUP * (number(cross_out) + number(cross_in)))

    def start_copy(off):
        return pltpu.make_async_remote_copy(
            src_ref=sg.at[aligned(me * OWN, OWN), :], dst_ref=sg.at[aligned(me * OWN, OWN), :],
            send_sem=s_send.at[off], recv_sem=s_recv.at[off],
            device_id={"elem": lax.rem(me + off, GROUP)}, device_id_type=MESH)

    def columns(chunk, peer):
        return aligned(chunk // 2 * CHANNELS + peer * PART + lax.rem(chunk, 2) * CHUNK, CHUNK)

    def sample_copy(chunk, off):
        peer = lax.rem(me + off, GROUP)
        return pltpu.make_async_remote_copy(
            src_ref=x_ref.at[:, :, columns(chunk, peer)], dst_ref=xg.at[chunk, :, aligned(me * OWN, OWN), :],
            send_sem=send_sem.at[chunk, off], recv_sem=recv_sem.at[chunk, off],
            device_id={"elem": peer}, device_id_type=MESH)

    def own_copy(chunk):
        return pltpu.make_async_copy(
            x_ref.at[:, :, columns(chunk, me)], xg.at[chunk, :, aligned(me * OWN, OWN), :], own_sem.at[chunk])

    for chunk in range(CHUNKS):
        for off in (2, 1, 3):
            sample_copy(chunk, off).start()
        own_copy(chunk).start()
    sg[aligned(me * OWN, OWN), :] = (start_ref[...].reshape(2 * BEAMS, OWN).astype(F32) - 4.5).T
    for off in range(1, GROUP):
        start_copy(off).start()

    rows8 = lax.broadcasted_iota(jnp.int32, (8, CHUNK), 0)
    lanes = lax.broadcasted_iota(jnp.int32, (8, CHUNK), 1)
    times = tm * SPAN + rows8 // 2 * CHANNELS + me * PART + lax.rem(rows8, 2) * CHUNK + lanes
    turns = (times * shift_ref[0]).astype(F32)
    folded = turns - jnp.floor(turns * (1.0 / SAMPLES)) * SAMPLES
    folded = jnp.where(folded < 0.0, folded + SAMPLES, folded)
    folded = jnp.where(folded >= SAMPLES, folded - SAMPLES, folded)
    angle = 2.0 * math.pi / SAMPLES * folded
    phase[0] = jnp.cos(angle)
    phase[1] = jnp.sin(angle)
    g[...] = jnp.zeros_like(g)

    upper = lax.broadcasted_iota(jnp.int32, (256, 256), 0) <= lax.broadcasted_iota(jnp.int32, (256, 256), 1)

    def left_of(high_ref, low_ref, rows, imag):
        high = high_ref[rows, :]
        low = low_ref[rows, :]
        if imag:
            high = cat(high[:, CHUNK:], -high[:, :CHUNK])
            low = cat(low[:, CHUNK:], -low[:, :CHUNK])
        return cat(high, high, low)

    def add_blocks(kind, first, strip, value):
        for i in range(value.shape[0] // BLOCK):
            for j in range(2):
                row = first + i
                g[(row + j) % 2, strip * 4 + row, kind] += value[
                    i * BLOCK:(i + 1) * BLOCK, j * BLOCK:(j + 1) * BLOCK]

    def arrive(chunk):
        own_copy(chunk).wait()
        for off in range(1, GROUP):
            sample_copy(chunk, off).wait_recv()
        cos_row = phase[0, pl.ds(chunk, 1), :]
        sin_row = phase[1, pl.ds(chunk, 1), :]
        for block in range(4):
            rows = pl.ds(block * BLOCK, BLOCK)
            real = xg[chunk, 0, rows, :]
            imag = xg[chunk, 1, rows, :]
            rh[rows, :], rl[rows, :] = split(cat(real, imag))
            uh[rows, :], ul[rows, :] = split(cat(real * cos_row + imag * sin_row, imag * cos_row - real * sin_row))

    def strip_of(strip):
        cols = pl.ds(strip * 256, 256)
        high = rh[cols, :]
        right = cat(high, rl[cols, :], high)
        every = pl.ds(0, ELEMS)
        for imag in (0, 1):
            add_blocks(1 + imag, 0, strip, dot_nt(left_of(uh, ul, every, imag), right))
        diag = jnp.where(
            upper, dot_nt(left_of(rh, rl, cols, 0), right), dot_nt(left_of(rh, rl, cols, 1), right))
        add_blocks(0, strip * 2, strip, diag)
        other = pl.ds((1 - strip) * 256, 256)
        add_blocks(0, (1 - strip) * 2, strip, dot_nt(left_of(rh, rl, other, 1 - strip), right))

    def one_chunk(chunk, carry):
        arrive(chunk)
        strip_of(0)
        strip_of(1)
        return carry

    lax.fori_loop(0, CHUNKS - 1, one_chunk, 0)

    sibling = device_at(spot, "core", 1 - core)

    def pair_copy(part):
        return pltpu.make_async_remote_copy(
            src_ref=g.at[1 - core, pl.ds(part * 4, 4)], dst_ref=pair_got.at[pl.ds(part * 4, 4)],
            send_sem=pair_send.at[part], recv_sem=pair_recv.at[part], device_id=sibling, device_id_type=MESH)

    def piece(part, stage, first, second):
        if stage == 0:
            return aligned(first * 32, 32)
        return aligned(first * 32 + second * 8, 8)

    def rs_copy(part, stage, off):
        axis = PLANE[part][stage]
        peer = lax.rem(spot[axis] + off, 4)
        first, second = spot[PLANE[part][0]], spot[PLANE[part][1]]
        rows = piece(part, 0, peer, 0) if stage == 0 else piece(part, 1, first, peer)
        dst = (first_got if stage == 0 else second_got).at[part, off]
        return pltpu.make_async_remote_copy(
            src_ref=g.at[core, pl.ds(part * 4, 4), :, rows, :], dst_ref=dst,
            send_sem=rs_send.at[part * 8 + stage * 4 + off], recv_sem=rs_recv.at[part * 8 + stage * 4 + off],
            device_id=device_at(spot, axis, peer), device_id_type=MESH)

    def own_rows(part):
        return piece(part, 1, spot[PLANE[part][0]], spot[PLANE[part][1]])

    def rows_of(z):
        part = z // 4
        plane = (spot["x"] * 32 + spot["y"] * 8) * (1 - part) + (spot["y"] * 32 + spot["x"] * 8) * part
        return aligned(plane, 8)

    def z_copy(off):
        peer = lax.rem(spot["z"] + off, 8)
        return pltpu.make_async_remote_copy(
            src_ref=g.at[core, peer, :, rows_of(peer), :], dst_ref=z_got.at[off],
            send_sem=z_send.at[off], recv_sem=z_recv.at[off],
            device_id=device_at(spot, "z", peer), device_id_type=MESH)

    def az_copy(off):
        mine = spot["z"]
        where = o.at[core, mine, :, rows_of(mine), :]
        return pltpu.make_async_remote_copy(
            src_ref=where, dst_ref=where, send_sem=az_send.at[off], recv_sem=az_recv.at[off],
            device_id=device_at(spot, "z", lax.rem(mine + off, 8)), device_id_type=MESH)

    def ag_copy(part, stage, off):
        axis = PLANE[part][stage]
        peer = lax.rem(spot[axis] + off, 4)
        rows = piece(part, stage, spot[PLANE[part][0]], spot[PLANE[part][1]])
        where = o.at[core, pl.ds(part * 4, 4), :, rows, :]
        return pltpu.make_async_remote_copy(
            src_ref=where, dst_ref=where,
            send_sem=ag_send.at[part * 8 + stage * 4 + off], recv_sem=ag_recv.at[part * 8 + stage * 4 + off],
            device_id=device_at(spot, axis, peer), device_id_type=MESH)

    def forward_copy(part, off):
        origin = lax.rem(spot[PLANE[part][0]] + 4 - off, 4)
        where = o.at[core, pl.ds(part * 4, 4), :, aligned(origin * 32, 32), :]
        return pltpu.make_async_remote_copy(
            src_ref=where, dst_ref=where, send_sem=fw_send.at[part * 4 + off], recv_sem=fw_recv.at[part * 4 + off],
            device_id=sibling, device_id_type=MESH)

    arrive(CHUNKS - 1)
    for part in range(2):
        strip_of(part)
        pair_copy(part).start()
    for part in range(2):
        pair_copy(part).wait_recv()
        for slot in range(part * 4, part * 4 + 4):
            g[core, slot] += pair_got[slot]
        for off in (2, 1, 3):
            rs_copy(part, 0, off).start()
    for part in range(2):
        rows = piece(part, 0, spot[PLANE[part][0]], 0)
        for off in (1, 3, 2):
            rs_copy(part, 0, off).wait_recv()
        g[core, pl.ds(part * 4, 4), :, rows, :] += first_got[part, 1] + first_got[part, 2] + first_got[part, 3]
        for off in (2, 1, 3):
            rs_copy(part, 1, off).start()
    for part in range(2):
        for off in (1, 3, 2):
            rs_copy(part, 1, off).wait_recv()
        g[core, pl.ds(part * 4, 4), :, own_rows(part), :] += (
            second_got[part, 1] + second_got[part, 2] + second_got[part, 3])
    z_order = (4, 3, 5, 2, 6, 1, 7)
    for off in z_order:
        z_copy(off).start()
    mine = spot["z"]
    total = g[core, mine, :, rows_of(mine), :]
    for off in range(1, 8):
        z_copy(off).wait_recv()
    for off in range(1, 8):
        total = total + z_got[off]
    o[core, mine, :, rows_of(mine), :] = total
    for off in z_order:
        az_copy(off).start()
    for off in range(1, 8):
        az_copy(off).wait_recv()
    for part in range(2):
        for off in (2, 1, 3):
            ag_copy(part, 1, off).start()
    for part in range(2):
        for off in (1, 3, 2):
            ag_copy(part, 1, off).wait_recv()
        for off in (2, 1, 3):
            ag_copy(part, 0, off).start()
        forward_copy(part, 0).start()
    for off in (1, 3, 2):
        for part in range(2):
            ag_copy(part, 0, off).wait_recv()
            forward_copy(part, off).start()
    for off in range(1, GROUP):
        start_copy(off).wait_recv()
    for part in range(2):
        for off in range(4):
            forward_copy(part, off).wait_recv()

    plain_scale = 1.0 / SAMPLES
    cyc_scale = 1.0 / math.sqrt(SAMPLES * ELEMS)

    def full(kind):
        return jnp.concatenate(
            [cat(*[o[(i + j) % 2, j // 2 * 4 + i, kind] for j in range(4)]) for i in range(4)], axis=0)

    def put(high_ref, low_ref, col, value):
        high, low = split(value)
        high_ref[:, col * ELEMS:(col + 1) * ELEMS] = high
        low_ref[:, col * ELEMS:(col + 1) * ELEMS] = low

    packed = full(0) * plain_scale
    flipped = packed.T
    row_ids = lax.broadcasted_iota(jnp.int32, (ELEMS, ELEMS), 0)
    col_ids = lax.broadcasted_iota(jnp.int32, (ELEMS, ELEMS), 1)
    put(ah, al, 2, jnp.where(row_ids <= col_ids, packed, flipped))
    put(ah, al, 3, jnp.where(row_ids > col_ids, packed, jnp.where(row_ids < col_ids, -flipped, 0.0)))
    cyc_real = full(1) * cyc_scale
    put(ah, al, 0, cyc_real)
    put(bh, bl, 0, cyc_real.T)
    cyc_imag = full(2) * cyc_scale
    put(ah, al, 1, cyc_imag)
    put(bh, bl, 1, -cyc_imag.T)

    lane = lax.broadcasted_iota(jnp.int32, (ELEMS, 2 * BEAMS), 1)

    def turned(vector):
        other = pltpu.roll(vector, BEAMS, 1)
        return jnp.where(lane < BEAMS, -other, other)

    def normalized(vector):
        squares = jnp.sum(vector * vector, axis=0, keepdims=True)
        squares = jnp.broadcast_to(squares, (8, 2 * BEAMS))
        squares = squares + pltpu.roll(squares, BEAMS, 1)
        return vector * (1.0 / jnp.sqrt(squares[:1] + EPS))

    def stacked(vector):
        high, low = split(jnp.concatenate([vector, turned(vector)], axis=0))
        return cat(high, low)

    def product(high, low, right):
        wide_out = dot_nn(high, right)
        return wide_out[:, :2 * BEAMS] + wide_out[:, 2 * BEAMS:] + dot_nn(low, right[:, :2 * BEAMS])

    v_ref[...] = normalized(sg[...])

    def step(iteration, carry):
        held = stacked(v_ref[...])
        mid = product(bh[...], bl[...], held)
        v_ref[...] = normalized(product(ah[...], al[...], jnp.concatenate([stacked(mid), held], axis=0)))
        return carry

    lax.fori_loop(0, ITERS, step, 0)
    weights_ref[...] = v_ref[aligned(me * OWN, OWN), :].T.reshape(2, BEAMS, OWN)

    vh, vl = split(v_ref[...].T)
    left = jnp.concatenate([vh, vl], axis=0)
    taps = tap_ref[:, aligned(me * PART, PART)].astype(F32) / 2048.0
    beams = ([], [])
    for frame in range(FRAMES):
        pieces = [xg[frame * 2 + half, kind] for kind in range(2) for half in range(2)]
        xh, xl = split(cat(*pieces))
        both = dot_nn(left, xh)
        out = both[:2 * BEAMS] + both[2 * BEAMS:] + dot_nn(vh, xl)
        beams[0].append(out[:BEAMS, :PART] + out[BEAMS:, PART:])
        beams[1].append(out[:BEAMS, PART:] - out[BEAMS:, :PART])

    def filtered(kind, frame):
        total = None
        for tap in range(TAPS):
            if 0 <= frame - tap < FRAMES:
                term = taps[tap:tap + 1, :] * beams[kind][frame - tap]
                total = term if total is None else total + term
        return total

    for kind in range(2):
        for frame in range(FRAMES):
            after[kind, frame] = filtered(kind, frame + FRAMES)

    def quarter(off):
        return aligned(lax.rem(me + off, GROUP) * QUARTER, QUARTER)

    def halo_copy(off):
        rows = quarter(off)
        return pltpu.make_async_remote_copy(
            src_ref=after.at[:, :, rows, :], dst_ref=halo.at[:, :, rows, :],
            send_sem=halo_send.at[off], recv_sem=halo_recv.at[off],
            device_id={"tm": tm + 1, "elem": me}, device_id_type=MESH)

    def cross_copy(off):
        return pltpu.make_async_remote_copy(
            src_ref=after.at[:, :, quarter(off), :], dst_ref=crossed.at[off],
            send_sem=cross_send.at[off], recv_sem=cross_recv.at[off],
            device_id={"tm": tm + 1, "elem": lax.rem(me + off, GROUP)}, device_id_type=MESH)

    def last_copy(off):
        return pltpu.make_async_remote_copy(
            src_ref=own.at[:, :, quarter(off), :], dst_ref=got.at[off],
            send_sem=last_send.at[off], recv_sem=last_recv.at[off],
            device_id={"elem": lax.rem(me + off, GROUP)}, device_id_type=MESH)

    order = (2, 1, 3, 0)

    @pl.when(near_out)
    def _():
        for off in order:
            halo_copy(off).start()

    @pl.when(cross_out)
    def _():
        for off in order:
            cross_copy(off).start()

    for kind in range(2):
        for frame in range(FRAMES):
            own[kind, frame] = filtered(kind, frame)

    for off in order:
        @pl.when(near_in)
        def _():
            halo_copy(off).wait_recv()
            rows = quarter(off)
            own[:, :, rows, :] += halo[:, :, rows, :]

        if off:
            last_copy(off).start()
        else:
            got[0] = own[:, :, quarter(0), :]

    table_copy.wait()
    rows = 2 * FRAMES * QUARTER
    half = FRAMES * QUARTER
    for position, off in enumerate((0, 1, 3, 2)):
        if off:
            last_copy(off).wait_recv()

        @pl.when(cross_in)
        def _():
            cross_copy(off).wait_recv()
            got[off] += crossed[off]

        high, low = split(got[off].reshape(rows, PART))
        left = jnp.concatenate([high, low], axis=0)
        where = aligned(lax.rem(me + GROUP - off, GROUP) * PART, PART)

        def times_table(index):
            both = dot_nn(left, table[index, where, :])
            return both[:rows] + both[rows:] + dot_nn(high, table[index + 1, where, :])

        with_cos = times_table(0)
        with_sin = times_table(2)
        real = with_cos[:half] + with_sin[half:]
        imag = with_cos[half:] - with_sin[:half]
        if position == 0:
            out_ref[0] = real
            out_ref[1] = imag
        else:
            out_ref[0] += real
            out_ref[1] += imag

    for off in range(1, GROUP):
        last_copy(off).wait_send()
        start_copy(off).wait_send()
        for chunk in range(CHUNKS):
            sample_copy(chunk, off).wait_send()
        for part in range(2):
            for stage in range(2):
                rs_copy(part, stage, off).wait_send()
                ag_copy(part, stage, off).wait_send()
    for off in range(1, 8):
        z_copy(off).wait_send()
        az_copy(off).wait_send()
    for part in range(2):
        pair_copy(part).wait_send()
        for off in range(4):
            forward_copy(part, off).wait_send()

    @pl.when(near_out)
    def _():
        for off in order:
            halo_copy(off).wait_send()

    @pl.when(cross_out)
    def _():
        for off in order:
            cross_copy(off).wait_send()


def body(samples, shift_bin, start_vectors, tap_table):
    vmem = pl.BlockSpec(memory_space=pltpu.VMEM)
    smem = pl.BlockSpec(memory_space=pltpu.SMEM)
    hbm = pl.BlockSpec(memory_space=pl.ANY)
    dma = pltpu.SemaphoreType.DMA
    scratch = [
        ((CHUNKS, 2, ELEMS, CHUNK), F32),
        ((ELEMS, 2 * BEAMS), F32),
        ((2, 8, CHUNK), F32),
        ((ELEMS, 2 * CHUNK), BF16),
        ((ELEMS, 2 * CHUNK), BF16),
        ((ELEMS, 2 * CHUNK), BF16),
        ((ELEMS, 2 * CHUNK), BF16),
        ((2, 8, 3, BLOCK, BLOCK), F32),
        ((2, 8, 3, BLOCK, BLOCK), F32),
        ((8, 3, BLOCK, BLOCK), F32),
        ((2, 4, 4, 3, 32, BLOCK), F32),
        ((2, 4, 4, 3, 8, BLOCK), F32),
        ((8, 3, 8, BLOCK), F32),
        ((ELEMS, 2 * BEAMS), F32),
        ((ELEMS, 4 * ELEMS), BF16),
        ((ELEMS, 4 * ELEMS), BF16),
        ((ELEMS, 2 * ELEMS), BF16),
        ((ELEMS, 2 * ELEMS), BF16),
        ((4, CHANNELS, CHANNELS), BF16),
        ((2, FRAMES, BEAMS, PART), F32),
        ((2, FRAMES, BEAMS, PART), F32),
        ((2, FRAMES, BEAMS, PART), F32),
        ((GROUP, 2, FRAMES, QUARTER, PART), F32),
        ((GROUP, 2, FRAMES, QUARTER, PART), F32),
    ]
    semaphores = [
        (CHUNKS, GROUP), (CHUNKS, GROUP), (CHUNKS,), (GROUP,), (GROUP,), None,
        (2,), (2,), (16,), (16,), (8,), (8,), (8,), (8,), (16,), (16,),
        (8,), (8,), (GROUP,), (GROUP,), (GROUP,), (GROUP,), (GROUP,), (GROUP,),
    ]
    spectra, weights = pl.pallas_call(
        kernel,
        out_shape=(
            jax.ShapeDtypeStruct((2, FRAMES * QUARTER, CHANNELS), F32),
            jax.ShapeDtypeStruct((2, BEAMS, OWN), F32),
        ),
        in_specs=[hbm, vmem, smem, vmem, hbm],
        out_specs=(vmem, vmem),
        scratch_shapes=[pltpu.VMEM(*entry) for entry in scratch]
        + [dma if shape is None else dma(shape) for shape in semaphores],
        compiler_params=pltpu.CompilerParams(
            collective_id=0, has_side_effects=True, vmem_limit_bytes=VMEM_LIMIT),
        name="beamformer",
    )(samples, start_vectors.transpose(0, 2, 1), shift_bin, tap_table, jnp.asarray(dft_tables()))
    spectra = spectra.reshape(2, FRAMES, QUARTER, CHANNELS).transpose(0, 2, 1, 3)
    return (spectra, weights.transpose(0, 2, 1))


def solution(mesh):
    return jax.shard_map(
        body,
        mesh=mesh,
        in_specs=(P(None, "elem", "tm"), P(), P(None, "elem", None), P()),
        out_specs=(P(None, "elem", "tm", None), P(None, "elem", None)),
        check_vma=False,
    )
```

```python
import math

import jax
import jax.numpy as jnp
import ml_dtypes
import numpy as np
from jax import lax
from jax.experimental import pallas as pl
from jax.experimental.pallas import tpu as pltpu
from jax.sharding import PartitionSpec as P

ELEMS = 512
BEAMS = 64
CHANNELS = 1024
TAPS = 4
ITERS = 3
SPAN = 3072
SAMPLES = 196608
FRAMES = SPAN // CHANNELS
GROUP = 4
OWN = ELEMS // GROUP
PART = CHANNELS // GROUP
TM = SAMPLES // SPAN
QUARTER = BEAMS // GROUP

EPS = 1e-06
F32 = jnp.float32
BF16 = jnp.bfloat16
MESH = pl.DeviceIdType.MESH
VMEM_LIMIT = 56 * 1024 * 1024

CHUNK = 128
CHUNKS = SPAN // GROUP // CHUNK
BLOCK = 128
SIZES = {"core": 2, "x": 4, "y": 4, "z": 8}
PLANE = (("x", "y"), ("y", "x"))


def split(value):
    high = value.astype(BF16)
    return high, (value - high.astype(F32)).astype(BF16)


def dot_nt(left, right):
    return lax.dot_general(left, right, (((1,), (1,)), ((), ())), preferred_element_type=F32)


def dot_nn(left, right):
    return lax.dot_general(left, right, (((1,), (0,)), ((), ())), preferred_element_type=F32)


def cat(*pieces):
    return jnp.concatenate(pieces, axis=1)


def dft_tables():
    ids = np.arange(CHANNELS)
    angle = 2.0 * np.pi / CHANNELS * (ids[:, None] * ids[None, :] % CHANNELS)
    out = []
    for table in (np.cos(angle), np.sin(angle)):
        table = (table / math.sqrt(CHANNELS)).astype(np.float32)
        high = table.astype(ml_dtypes.bfloat16)
        out += [high, (table - high.astype(np.float32)).astype(ml_dtypes.bfloat16)]
    return np.stack(out)


def place():
    tm = lax.axis_index("tm")
    return {
        "core": lax.rem(tm, 2),
        "x": lax.rem(tm // 2, 4),
        "y": tm // 16,
        "z": lax.rem(tm // 8, 2) * 4 + lax.axis_index("elem"),
    }


def device_at(spot, axis, value):
    at = dict(spot)
    at[axis] = value
    tm = ((at["y"] * 2 + at["z"] // 4) * 4 + at["x"]) * 2 + at["core"]
    return {"tm": tm, "elem": lax.rem(at["z"], 4)}


def aligned(start, size):
    return pl.ds(pl.multiple_of(start, size), size)


def kernel(x_ref, start_hbm, shift_ref, tap_hbm, table_ref, out_ref, weights_ref,
           start_ref, tap_ref, xg, sg, phase, rh, rl, uh, ul, g, o, pair_got, first_got, second_got, z_got, v_ref, ah, al, bh, bl,
           table, own, after, halo, got, crossed,
           send_sem, recv_sem, own_sem, s_send, s_recv, table_sem, input_sem,
           pair_send, pair_recv, rs_send, rs_recv, z_send, z_recv, az_send, az_recv, ag_send, ag_recv,
           fw_send, fw_recv, halo_send, halo_recv, cross_send, cross_recv, last_send, last_recv):
    tm = lax.axis_index("tm")
    me = lax.axis_index("elem")
    spot = place()
    core = spot["core"]

    table_copy = pltpu.make_async_copy(table_ref, table, table_sem)
    start_fetch = pltpu.make_async_copy(start_hbm, start_ref, input_sem.at[0])
    tap_fetch = pltpu.make_async_copy(tap_hbm, tap_ref, input_sem.at[1])
    start_fetch.start()
    tap_fetch.start()

    barrier = pltpu.get_barrier_semaphore()
    count = 0
    for axis, size in SIZES.items():
        for off in range(1, size):
            pl.semaphore_signal(
                barrier, inc=1, device_id=device_at(spot, axis, lax.rem(spot[axis] + off, size)),
                device_id_type=MESH)
            count += 1
    turn = lax.rem(tm, 8)
    near_out = turn != 7
    near_in = turn != 0
    cross_out = jnp.logical_and(turn == 7, tm < TM - 1)
    cross_in = jnp.logical_and(turn == 0, tm > 0)

    @pl.when(near_out)
    def _():
        pl.semaphore_signal(barrier, inc=1, device_id={"tm": tm + 1, "elem": me}, device_id_type=MESH)

    @pl.when(near_in)
    def _():
        pl.semaphore_signal(barrier, inc=1, device_id={"tm": tm - 1, "elem": me}, device_id_type=MESH)

    @pl.when(cross_out)
    def _():
        for peer in range(GROUP):
            pl.semaphore_signal(barrier, inc=1, device_id={"tm": tm + 1, "elem": peer}, device_id_type=MESH)

    @pl.when(cross_in)
    def _():
        for peer in range(GROUP):
            pl.semaphore_signal(barrier, inc=1, device_id={"tm": tm - 1, "elem": peer}, device_id_type=MESH)

    number = lambda flag: flag.astype(jnp.int32)
    pl.semaphore_wait(
        barrier, count + number(near_out) + number(near_in) + GROUP * (number(cross_out) + number(cross_in)))

    def start_copy(off):
        return pltpu.make_async_remote_copy(
            src_ref=sg.at[aligned(me * OWN, OWN), :], dst_ref=sg.at[aligned(me * OWN, OWN), :],
            send_sem=s_send.at[off], recv_sem=s_recv.at[off],
            device_id={"elem": lax.rem(me + off, GROUP)}, device_id_type=MESH)

    def columns(chunk, peer):
        return aligned(chunk // 2 * CHANNELS + peer * PART + lax.rem(chunk, 2) * CHUNK, CHUNK)

    def sample_copy(chunk, off):
        peer = lax.rem(me + off, GROUP)
        return pltpu.make_async_remote_copy(
            src_ref=x_ref.at[:, :, columns(chunk, peer)], dst_ref=xg.at[chunk, :, aligned(me * OWN, OWN), :],
            send_sem=send_sem.at[chunk, off], recv_sem=recv_sem.at[chunk, off],
            device_id={"elem": peer}, device_id_type=MESH)

    def own_copy(chunk):
        return pltpu.make_async_copy(
            x_ref.at[:, :, columns(chunk, me)], xg.at[chunk, :, aligned(me * OWN, OWN), :], own_sem.at[chunk])

    for chunk in range(CHUNKS):
        for off in (2, 1, 3):
            sample_copy(chunk, off).start()
        own_copy(chunk).start()
    table_copy.start()
    start_fetch.wait()
    sg[aligned(me * OWN, OWN), :] = (start_ref[...].reshape(2 * BEAMS, OWN).astype(F32) - 4.5).T
    for off in range(1, GROUP):
        start_copy(off).start()

    rows8 = lax.broadcasted_iota(jnp.int32, (8, CHUNK), 0)
    lanes = lax.broadcasted_iota(jnp.int32, (8, CHUNK), 1)
    times = tm * SPAN + rows8 // 2 * CHANNELS + me * PART + lax.rem(rows8, 2) * CHUNK + lanes
    turns = (times * shift_ref[0]).astype(F32)
    folded = turns - jnp.floor(turns * (1.0 / SAMPLES)) * SAMPLES
    folded = jnp.where(folded < 0.0, folded + SAMPLES, folded)
    folded = jnp.where(folded >= SAMPLES, folded - SAMPLES, folded)
    angle = 2.0 * math.pi / SAMPLES * folded
    phase[0] = jnp.cos(angle)
    phase[1] = jnp.sin(angle)
    g[...] = jnp.zeros_like(g)

    upper = lax.broadcasted_iota(jnp.int32, (256, 256), 0) <= lax.broadcasted_iota(jnp.int32, (256, 256), 1)

    def left_of(high_ref, low_ref, rows, imag):
        high = high_ref[rows, :]
        low = low_ref[rows, :]
        if imag:
            high = cat(high[:, CHUNK:], -high[:, :CHUNK])
            low = cat(low[:, CHUNK:], -low[:, :CHUNK])
        return cat(high, high, low)

    def add_blocks(kind, first, strip, value):
        for i in range(value.shape[0] // BLOCK):
            for j in range(2):
                row = first + i
                g[(row + j) % 2, strip * 4 + row, kind] += value[
                    i * BLOCK:(i + 1) * BLOCK, j * BLOCK:(j + 1) * BLOCK]

    def arrive(chunk):
        own_copy(chunk).wait()
        for off in range(1, GROUP):
            sample_copy(chunk, off).wait_recv()
        cos_row = phase[0, pl.ds(chunk, 1), :]
        sin_row = phase[1, pl.ds(chunk, 1), :]
        for block in range(4):
            rows = pl.ds(block * BLOCK, BLOCK)
            real = xg[chunk, 0, rows, :]
            imag = xg[chunk, 1, rows, :]
            rh[rows, :], rl[rows, :] = split(cat(real, imag))
            uh[rows, :], ul[rows, :] = split(cat(real * cos_row + imag * sin_row, imag * cos_row - real * sin_row))

    def strip_of(strip):
        cols = pl.ds(strip * 256, 256)
        high = rh[cols, :]
        right = cat(high, rl[cols, :], high)
        every = pl.ds(0, ELEMS)
        for imag in (0, 1):
            add_blocks(1 + imag, 0, strip, dot_nt(left_of(uh, ul, every, imag), right))
        diag = jnp.where(
            upper, dot_nt(left_of(rh, rl, cols, 0), right), dot_nt(left_of(rh, rl, cols, 1), right))
        add_blocks(0, strip * 2, strip, diag)
        other = pl.ds((1 - strip) * 256, 256)
        add_blocks(0, (1 - strip) * 2, strip, dot_nt(left_of(rh, rl, other, 1 - strip), right))

    def one_chunk(chunk, carry):
        arrive(chunk)
        strip_of(0)
        strip_of(1)
        return carry

    lax.fori_loop(0, CHUNKS - 1, one_chunk, 0)

    sibling = device_at(spot, "core", 1 - core)

    def pair_copy(part):
        return pltpu.make_async_remote_copy(
            src_ref=g.at[1 - core, pl.ds(part * 4, 4)], dst_ref=pair_got.at[pl.ds(part * 4, 4)],
            send_sem=pair_send.at[part], recv_sem=pair_recv.at[part], device_id=sibling, device_id_type=MESH)

    def piece(part, stage, first, second):
        if stage == 0:
            return aligned(first * 32, 32)
        return aligned(first * 32 + second * 8, 8)

    def rs_copy(part, stage, off):
        axis = PLANE[part][stage]
        peer = lax.rem(spot[axis] + off, 4)
        first, second = spot[PLANE[part][0]], spot[PLANE[part][1]]
        rows = piece(part, 0, peer, 0) if stage == 0 else piece(part, 1, first, peer)
        dst = (first_got if stage == 0 else second_got).at[part, off]
        return pltpu.make_async_remote_copy(
            src_ref=g.at[core, pl.ds(part * 4, 4), :, rows, :], dst_ref=dst,
            send_sem=rs_send.at[part * 8 + stage * 4 + off], recv_sem=rs_recv.at[part * 8 + stage * 4 + off],
            device_id=device_at(spot, axis, peer), device_id_type=MESH)

    def own_rows(part):
        return piece(part, 1, spot[PLANE[part][0]], spot[PLANE[part][1]])

    def rows_of(z):
        part = z // 4
        plane = (spot["x"] * 32 + spot["y"] * 8) * (1 - part) + (spot["y"] * 32 + spot["x"] * 8) * part
        return aligned(plane, 8)

    def z_copy(off):
        peer = lax.rem(spot["z"] + off, 8)
        return pltpu.make_async_remote_copy(
            src_ref=g.at[core, peer, :, rows_of(peer), :], dst_ref=z_got.at[off],
            send_sem=z_send.at[off], recv_sem=z_recv.at[off],
            device_id=device_at(spot, "z", peer), device_id_type=MESH)

    def az_copy(off):
        mine = spot["z"]
        where = o.at[core, mine, :, rows_of(mine), :]
        return pltpu.make_async_remote_copy(
            src_ref=where, dst_ref=where, send_sem=az_send.at[off], recv_sem=az_recv.at[off],
            device_id=device_at(spot, "z", lax.rem(mine + off, 8)), device_id_type=MESH)

    def ag_copy(part, stage, off):
        axis = PLANE[part][stage]
        peer = lax.rem(spot[axis] + off, 4)
        rows = piece(part, stage, spot[PLANE[part][0]], spot[PLANE[part][1]])
        where = o.at[core, pl.ds(part * 4, 4), :, rows, :]
        return pltpu.make_async_remote_copy(
            src_ref=where, dst_ref=where,
            send_sem=ag_send.at[part * 8 + stage * 4 + off], recv_sem=ag_recv.at[part * 8 + stage * 4 + off],
            device_id=device_at(spot, axis, peer), device_id_type=MESH)

    def forward_copy(part, off):
        origin = lax.rem(spot[PLANE[part][0]] + 4 - off, 4)
        where = o.at[core, pl.ds(part * 4, 4), :, aligned(origin * 32, 32), :]
        return pltpu.make_async_remote_copy(
            src_ref=where, dst_ref=where, send_sem=fw_send.at[part * 4 + off], recv_sem=fw_recv.at[part * 4 + off],
            device_id=sibling, device_id_type=MESH)

    arrive(CHUNKS - 1)
    for part in range(2):
        strip_of(part)
        pair_copy(part).start()
    for part in range(2):
        pair_copy(part).wait_recv()
        for slot in range(part * 4, part * 4 + 4):
            g[core, slot] += pair_got[slot]
        for off in (2, 1, 3):
            rs_copy(part, 0, off).start()
    for part in range(2):
        rows = piece(part, 0, spot[PLANE[part][0]], 0)
        for off in (1, 3, 2):
            rs_copy(part, 0, off).wait_recv()
        g[core, pl.ds(part * 4, 4), :, rows, :] += first_got[part, 1] + first_got[part, 2] + first_got[part, 3]
        for off in (2, 1, 3):
            rs_copy(part, 1, off).start()
    for part in range(2):
        for off in (1, 3, 2):
            rs_copy(part, 1, off).wait_recv()
        g[core, pl.ds(part * 4, 4), :, own_rows(part), :] += (
            second_got[part, 1] + second_got[part, 2] + second_got[part, 3])
    z_order = (4, 3, 5, 2, 6, 1, 7)
    for off in z_order:
        z_copy(off).start()
    mine = spot["z"]
    total = g[core, mine, :, rows_of(mine), :]
    for off in range(1, 8):
        z_copy(off).wait_recv()
    for off in range(1, 8):
        total = total + z_got[off]
    o[core, mine, :, rows_of(mine), :] = total
    for off in z_order:
        az_copy(off).start()
    for off in range(1, 8):
        az_copy(off).wait_recv()
    for part in range(2):
        for off in (2, 1, 3):
            ag_copy(part, 1, off).start()
    for part in range(2):
        for off in (1, 3, 2):
            ag_copy(part, 1, off).wait_recv()
        for off in (2, 1, 3):
            ag_copy(part, 0, off).start()
        forward_copy(part, 0).start()
    plain_scale = 1.0 / SAMPLES
    cyc_scale = 1.0 / math.sqrt(SAMPLES * ELEMS)

    def put(high_ref, low_ref, col, value):
        high, low = split(value)
        high_ref[:, col * ELEMS:(col + 1) * ELEMS] = high
        low_ref[:, col * ELEMS:(col + 1) * ELEMS] = low

    def prepare(part, off):
        origin = lax.rem(spot[PLANE[part][0]] + 4 - off, 4)
        rows = aligned(origin * 32, 32)
        lanes = aligned(origin * 128, 128)
        for imag in range(2):
            for j in (part * 2, part * 2 + 1):
                slabs = [o[(i + j) % 2, part * 4 + i, 1 + imag, rows, :] * cyc_scale for i in range(4)]
                slab = jnp.concatenate(slabs, axis=0)
                high, low = split(slab)
                cols = pl.ds(imag * ELEMS + j * BLOCK, BLOCK)
                for i in range(4):
                    there = aligned(i * BLOCK + origin * 32, 32)
                    ah[there, cols] = high[i * 32:(i + 1) * 32]
                    al[there, cols] = low[i * 32:(i + 1) * 32]
                high, low = split(-slab.T if imag else slab.T)
                there = pl.ds(imag * ELEMS + pl.multiple_of(origin * 128, 128), 128)
                bh[j * BLOCK:(j + 1) * BLOCK, there] = high
                bl[j * BLOCK:(j + 1) * BLOCK, there] = low

    for off in (0, 1, 3, 2):
        for part in range(2):
            if off:
                ag_copy(part, 0, off).wait_recv()
                forward_copy(part, off).start()
        for part in range(2):
            forward_copy(part, off).wait_recv()
            prepare(part, off)
    for off in range(1, GROUP):
        start_copy(off).wait_recv()

    packed = plain_scale * jnp.concatenate(
        [cat(*[o[(i + j) % 2, j // 2 * 4 + i, 0] for j in range(4)]) for i in range(4)], axis=0)
    flipped = packed.T
    row_ids = lax.broadcasted_iota(jnp.int32, (ELEMS, ELEMS), 0)
    col_ids = lax.broadcasted_iota(jnp.int32, (ELEMS, ELEMS), 1)
    put(ah, al, 2, jnp.where(row_ids <= col_ids, packed, flipped))
    put(ah, al, 3, jnp.where(row_ids > col_ids, packed, jnp.where(row_ids < col_ids, -flipped, 0.0)))

    lane = lax.broadcasted_iota(jnp.int32, (ELEMS, 2 * BEAMS), 1)

    def turned(vector):
        other = pltpu.roll(vector, BEAMS, 1)
        return jnp.where(lane < BEAMS, -other, other)

    def normalized(vector):
        squares = jnp.sum(vector * vector, axis=0, keepdims=True)
        squares = jnp.broadcast_to(squares, (8, 2 * BEAMS))
        squares = squares + pltpu.roll(squares, BEAMS, 1)
        return vector * (1.0 / jnp.sqrt(squares[:1] + EPS))

    def stacked(vector):
        high, low = split(jnp.concatenate([vector, turned(vector)], axis=0))
        return cat(high, low)

    def product(high, low, right):
        wide_out = dot_nn(high, right)
        return wide_out[:, :2 * BEAMS] + wide_out[:, 2 * BEAMS:] + dot_nn(low, right[:, :2 * BEAMS])

    v_ref[...] = normalized(sg[...])

    def step(iteration, carry):
        held = stacked(v_ref[...])
        shuffled = jnp.concatenate(
            [held[half * ELEMS + i * BLOCK + q * 32:half * ELEMS + i * BLOCK + q * 32 + 32]
             for half in range(2) for q in range(4) for i in range(4)], axis=0)
        mid = product(bh[...], bl[...], shuffled)
        v_ref[...] = normalized(product(ah[...], al[...], jnp.concatenate([stacked(mid), held], axis=0)))
        return carry

    lax.fori_loop(0, ITERS, step, 0)
    weights_ref[...] = v_ref[aligned(me * OWN, OWN), :].T.reshape(2, BEAMS, OWN)

    vh, vl = split(v_ref[...].T)
    left = jnp.concatenate([vh, vl], axis=0)
    tap_fetch.wait()
    taps = tap_ref[:, aligned(me * PART, PART)].astype(F32) / 2048.0
    beams = ([], [])
    for frame in range(FRAMES):
        pieces = [xg[frame * 2 + half, kind] for kind in range(2) for half in range(2)]
        xh, xl = split(cat(*pieces))
        both = dot_nn(left, xh)
        out = both[:2 * BEAMS] + both[2 * BEAMS:] + dot_nn(vh, xl)
        beams[0].append(out[:BEAMS, :PART] + out[BEAMS:, PART:])
        beams[1].append(out[:BEAMS, PART:] - out[BEAMS:, :PART])

    def filtered(kind, frame):
        total = None
        for tap in range(TAPS):
            if 0 <= frame - tap < FRAMES:
                term = taps[tap:tap + 1, :] * beams[kind][frame - tap]
                total = term if total is None else total + term
        return total

    for kind in range(2):
        for frame in range(FRAMES):
            after[kind, frame] = filtered(kind, frame + FRAMES)

    def quarter(off):
        return aligned(lax.rem(me + off, GROUP) * QUARTER, QUARTER)

    def halo_copy(off):
        rows = quarter(off)
        return pltpu.make_async_remote_copy(
            src_ref=after.at[:, :, rows, :], dst_ref=halo.at[:, :, rows, :],
            send_sem=halo_send.at[off], recv_sem=halo_recv.at[off],
            device_id={"tm": tm + 1, "elem": me}, device_id_type=MESH)

    def cross_copy(off):
        return pltpu.make_async_remote_copy(
            src_ref=after.at[:, :, quarter(off), :], dst_ref=crossed.at[off],
            send_sem=cross_send.at[off], recv_sem=cross_recv.at[off],
            device_id={"tm": tm + 1, "elem": lax.rem(me + off, GROUP)}, device_id_type=MESH)

    def last_copy(off):
        return pltpu.make_async_remote_copy(
            src_ref=own.at[:, :, quarter(off), :], dst_ref=got.at[off],
            send_sem=last_send.at[off], recv_sem=last_recv.at[off],
            device_id={"elem": lax.rem(me + off, GROUP)}, device_id_type=MESH)

    order = (2, 1, 3, 0)

    @pl.when(near_out)
    def _():
        for off in order:
            halo_copy(off).start()

    @pl.when(cross_out)
    def _():
        for off in order:
            cross_copy(off).start()

    for kind in range(2):
        for frame in range(FRAMES):
            own[kind, frame] = filtered(kind, frame)

    for off in order:
        @pl.when(near_in)
        def _():
            halo_copy(off).wait_recv()
            rows = quarter(off)
            own[:, :, rows, :] += halo[:, :, rows, :]

        if off:
            last_copy(off).start()
        else:
            got[0] = own[:, :, quarter(0), :]

    table_copy.wait()
    rows = 2 * FRAMES * QUARTER
    half = FRAMES * QUARTER
    for position, off in enumerate((0, 1, 3, 2)):
        if off:
            last_copy(off).wait_recv()

        @pl.when(cross_in)
        def _():
            cross_copy(off).wait_recv()
            got[off] += crossed[off]

        high, low = split(got[off].reshape(rows, PART))
        left = jnp.concatenate([high, low], axis=0)
        where = aligned(lax.rem(me + GROUP - off, GROUP) * PART, PART)

        def times_table(index):
            both = dot_nn(left, table[index, where, :])
            return both[:rows] + both[rows:] + dot_nn(high, table[index + 1, where, :])

        with_cos = times_table(0)
        with_sin = times_table(2)
        real = with_cos[:half] + with_sin[half:]
        imag = with_cos[half:] - with_sin[:half]
        if position == 0:
            out_ref[0] = real
            out_ref[1] = imag
        else:
            out_ref[0] += real
            out_ref[1] += imag

    for off in range(1, GROUP):
        last_copy(off).wait_send()
        start_copy(off).wait_send()
        for chunk in range(CHUNKS):
            sample_copy(chunk, off).wait_send()
        for part in range(2):
            for stage in range(2):
                rs_copy(part, stage, off).wait_send()
                ag_copy(part, stage, off).wait_send()
    for off in range(1, 8):
        z_copy(off).wait_send()
        az_copy(off).wait_send()
    for part in range(2):
        pair_copy(part).wait_send()
        for off in range(4):
            forward_copy(part, off).wait_send()

    @pl.when(near_out)
    def _():
        for off in order:
            halo_copy(off).wait_send()

    @pl.when(cross_out)
    def _():
        for off in order:
            cross_copy(off).wait_send()


def finish_kernel(spectra_ref, weights_ref, spectra_out, weights_out, sems):
    copies = (
        pltpu.make_async_copy(spectra_ref, spectra_out, sems.at[0]),
        pltpu.make_async_copy(weights_ref, weights_out, sems.at[1]),
    )
    for copy in copies:
        copy.start()
    for copy in copies:
        copy.wait()


def body(samples, shift_bin, start_vectors, tap_table):
    vmem = pl.BlockSpec(memory_space=pltpu.VMEM)
    smem = pl.BlockSpec(memory_space=pltpu.SMEM)
    hbm = pl.BlockSpec(memory_space=pl.ANY)
    dma = pltpu.SemaphoreType.DMA
    scratch = [
        ((2, BEAMS, OWN), jnp.int32),
        ((TAPS, CHANNELS), jnp.int32),
        ((CHUNKS, 2, ELEMS, CHUNK), F32),
        ((ELEMS, 2 * BEAMS), F32),
        ((2, 8, CHUNK), F32),
        ((ELEMS, 2 * CHUNK), BF16),
        ((ELEMS, 2 * CHUNK), BF16),
        ((ELEMS, 2 * CHUNK), BF16),
        ((ELEMS, 2 * CHUNK), BF16),
        ((2, 8, 3, BLOCK, BLOCK), F32),
        ((2, 8, 3, BLOCK, BLOCK), F32),
        ((8, 3, BLOCK, BLOCK), F32),
        ((2, 4, 4, 3, 32, BLOCK), F32),
        ((2, 4, 4, 3, 8, BLOCK), F32),
        ((8, 3, 8, BLOCK), F32),
        ((ELEMS, 2 * BEAMS), F32),
        ((ELEMS, 4 * ELEMS), BF16),
        ((ELEMS, 4 * ELEMS), BF16),
        ((ELEMS, 2 * ELEMS), BF16),
        ((ELEMS, 2 * ELEMS), BF16),
        ((4, CHANNELS, CHANNELS), BF16),
        ((2, FRAMES, BEAMS, PART), F32),
        ((2, FRAMES, BEAMS, PART), F32),
        ((2, FRAMES, BEAMS, PART), F32),
        ((GROUP, 2, FRAMES, QUARTER, PART), F32),
        ((GROUP, 2, FRAMES, QUARTER, PART), F32),
    ]
    semaphores = [
        (CHUNKS, GROUP), (CHUNKS, GROUP), (CHUNKS,), (GROUP,), (GROUP,), None, (2,),
        (2,), (2,), (16,), (16,), (8,), (8,), (8,), (8,), (16,), (16,),
        (8,), (8,), (GROUP,), (GROUP,), (GROUP,), (GROUP,), (GROUP,), (GROUP,),
    ]
    spectra, weights = pl.pallas_call(
        kernel,
        out_shape=(
            jax.ShapeDtypeStruct((2, FRAMES * QUARTER, CHANNELS), F32),
            jax.ShapeDtypeStruct((2, BEAMS, OWN), F32),
        ),
        in_specs=[hbm, hbm, smem, hbm, hbm],
        out_specs=(vmem, vmem),
        scratch_shapes=[pltpu.VMEM(*entry) for entry in scratch]
        + [dma if shape is None else dma(shape) for shape in semaphores],
        compiler_params=pltpu.CompilerParams(
            collective_id=0, has_side_effects=True, vmem_limit_bytes=VMEM_LIMIT),
        name="beamformer",
    )(samples, start_vectors.transpose(0, 2, 1), shift_bin, tap_table, jnp.asarray(dft_tables()))
    spectra, weights = pl.pallas_call(
        finish_kernel,
        out_shape=(
            jax.ShapeDtypeStruct((2, FRAMES * QUARTER, CHANNELS), F32),
            jax.ShapeDtypeStruct((2, BEAMS, OWN), F32),
        ),
        in_specs=[hbm, hbm],
        out_specs=(hbm, hbm),
        scratch_shapes=[dma((2,))],
        name="finish",
    )(spectra, weights)
    spectra = spectra.reshape(2, FRAMES, QUARTER, CHANNELS).transpose(0, 2, 1, 3)
    return (spectra, weights.transpose(0, 2, 1))


def solution(mesh):
    return jax.shard_map(
        body,
        mesh=mesh,
        in_specs=(P(None, "elem", "tm"), P(), P(None, "elem", None), P()),
        out_specs=(P(None, "elem", "tm", None), P(None, "elem", None)),
        check_vma=False,
    )
```

```python
import math

import jax
import jax.numpy as jnp
import ml_dtypes
import numpy as np
from jax import lax
from jax.experimental import pallas as pl
from jax.experimental.pallas import tpu as pltpu
from jax.sharding import PartitionSpec as P

ELEMS = 512
BEAMS = 64
CHANNELS = 1024
TAPS = 4
ITERS = 3
SPAN = 3072
SAMPLES = 196608
FRAMES = SPAN // CHANNELS
GROUP = 4
OWN = ELEMS // GROUP
PART = CHANNELS // GROUP
TM = SAMPLES // SPAN
QUARTER = BEAMS // GROUP

EPS = 1e-06
F32 = jnp.float32
BF16 = jnp.bfloat16
MESH = pl.DeviceIdType.MESH
VMEM_LIMIT = 56 * 1024 * 1024

CHUNK = 128
EARLY = 96
LATE = OWN - EARLY
GATE = 4
CHUNKS = SPAN // GROUP // CHUNK
BLOCK = 128
SIZES = {"core": 2, "x": 4, "y": 4, "z": 8}
PLANE = (("x", "y"), ("y", "x"))
SLOTS = (
    ((0, 0), (0, 2), (1, 1), (1, 3), (2, 0), (2, 2), (3, 1), (3, 3)),
    ((0, 1), (1, 0), (0, 3), (3, 0), (1, 2), (2, 1), (2, 3), (3, 2)),
)
SLOT_OF = {block: (parity, slot) for parity in range(2) for slot, block in enumerate(SLOTS[parity])}


def split(value):
    high = value.astype(BF16)
    return high, (value - high.astype(F32)).astype(BF16)


def dot_nt(left, right):
    return lax.dot_general(left, right, (((1,), (1,)), ((), ())), preferred_element_type=F32)


def dot_nn(left, right):
    return lax.dot_general(left, right, (((1,), (0,)), ((), ())), preferred_element_type=F32)


def cat(*pieces):
    return jnp.concatenate(pieces, axis=1)


def dft_tables():
    ids = np.arange(CHANNELS)
    angle = 2.0 * np.pi / CHANNELS * (ids[:, None] * ids[None, :] % CHANNELS)
    out = []
    for table in (np.cos(angle), np.sin(angle)):
        table = (table / math.sqrt(CHANNELS)).astype(np.float32)
        high = table.astype(ml_dtypes.bfloat16)
        out += [high, (table - high.astype(np.float32)).astype(ml_dtypes.bfloat16)]
    return np.stack(out)


def place():
    tm = lax.axis_index("tm")
    return {
        "core": lax.rem(tm, 2),
        "x": lax.rem(tm // 2, 4),
        "y": tm // 16,
        "z": lax.rem(tm // 8, 2) * 4 + lax.axis_index("elem"),
    }


def device_at(spot, axis, value):
    at = dict(spot)
    at[axis] = value
    tm = ((at["y"] * 2 + at["z"] // 4) * 4 + at["x"]) * 2 + at["core"]
    return {"tm": tm, "elem": lax.rem(at["z"], 4)}


def aligned(start, size):
    return pl.ds(pl.multiple_of(start, size), size)


def kernel(x_ref, start_hbm, shift_ref, tap_hbm, table_ref, out_ref, weights_ref,
           start_ref, tap_ref, xg, sg, phase, rh, rl, uh, ul, g, o, pair_got, first_got, second_got, z_got, v_ref, ah, al, bh, bl,
           table, own, after, halo, got, crossed,
           send_sem, recv_sem, own_sem, s_send, s_recv, table_sem, input_sem,
           pair_send, pair_recv, rs_send, rs_recv, z_send, z_recv, az_send, az_recv, ag_send, ag_recv,
           fw_send, fw_recv, halo_send, halo_recv, cross_send, cross_recv, last_send, last_recv):
    tm = lax.axis_index("tm")
    me = lax.axis_index("elem")
    spot = place()
    core = spot["core"]

    table_copy = pltpu.make_async_copy(table_ref, table, table_sem)
    start_fetch = pltpu.make_async_copy(start_hbm, start_ref, input_sem.at[0])
    tap_fetch = pltpu.make_async_copy(tap_hbm, tap_ref, input_sem.at[1])
    start_fetch.start()
    tap_fetch.start()

    barrier = pltpu.get_barrier_semaphore()
    count = 0
    for axis, size in SIZES.items():
        for off in range(1, size):
            pl.semaphore_signal(
                barrier, inc=1, device_id=device_at(spot, axis, lax.rem(spot[axis] + off, size)),
                device_id_type=MESH)
            count += 1
    turn = lax.rem(tm, 8)
    near_out = turn != 7
    near_in = turn != 0
    cross_out = jnp.logical_and(turn == 7, tm < TM - 1)
    cross_in = jnp.logical_and(turn == 0, tm > 0)

    @pl.when(near_out)
    def _():
        pl.semaphore_signal(barrier, inc=1, device_id={"tm": tm + 1, "elem": me}, device_id_type=MESH)

    @pl.when(near_in)
    def _():
        pl.semaphore_signal(barrier, inc=1, device_id={"tm": tm - 1, "elem": me}, device_id_type=MESH)

    @pl.when(cross_out)
    def _():
        for peer in range(GROUP):
            pl.semaphore_signal(barrier, inc=1, device_id={"tm": tm + 1, "elem": peer}, device_id_type=MESH)

    @pl.when(cross_in)
    def _():
        for peer in range(GROUP):
            pl.semaphore_signal(barrier, inc=1, device_id={"tm": tm - 1, "elem": peer}, device_id_type=MESH)

    number = lambda flag: flag.astype(jnp.int32)
    pl.semaphore_wait(
        barrier, count + number(near_out) + number(near_in) + GROUP * (number(cross_out) + number(cross_in)))

    firsts = (0, EARLY)
    counts = (EARLY, LATE)

    def virtual(group):
        return aligned(me * EARLY, EARLY) if group == 0 else aligned(GROUP * EARLY + me * LATE, LATE)

    def start_copy(group, off):
        where = sg.at[virtual(group), :]
        return pltpu.make_async_remote_copy(
            src_ref=where, dst_ref=where,
            send_sem=s_send.at[group * 4 + off], recv_sem=s_recv.at[group * 4 + off],
            device_id={"elem": lax.rem(me + off, GROUP)}, device_id_type=MESH)

    def columns(chunk, peer):
        return aligned(chunk // 2 * CHANNELS + peer * PART + lax.rem(chunk, 2) * CHUNK, CHUNK)

    def sample_copy(group, chunk, off):
        peer = lax.rem(me + off, GROUP)
        return pltpu.make_async_remote_copy(
            src_ref=x_ref.at[:, pl.ds(firsts[group], counts[group]), columns(chunk, peer)],
            dst_ref=xg.at[chunk, :, virtual(group), :],
            send_sem=send_sem.at[group * CHUNKS + chunk, off], recv_sem=recv_sem.at[group * CHUNKS + chunk, off],
            device_id={"elem": peer}, device_id_type=MESH)

    def own_copy(group, chunk):
        return pltpu.make_async_copy(
            x_ref.at[:, pl.ds(firsts[group], counts[group]), columns(chunk, me)],
            xg.at[chunk, :, virtual(group), :], own_sem.at[group * CHUNKS + chunk])

    def send_group(group):
        for chunk in range(CHUNKS):
            for off in (2, 1, 3):
                sample_copy(group, chunk, off).start()
            own_copy(group, chunk).start()

    send_group(0)
    table_copy.start()
    start_fetch.wait()
    starts = (start_ref[...].reshape(2 * BEAMS, OWN).astype(F32) - 4.5).T
    for group in range(2):
        sg[virtual(group), :] = starts[firsts[group]:firsts[group] + counts[group]]
        for off in range(1, GROUP):
            start_copy(group, off).start()

    rows8 = lax.broadcasted_iota(jnp.int32, (8, CHUNK), 0)
    lanes = lax.broadcasted_iota(jnp.int32, (8, CHUNK), 1)
    times = tm * SPAN + rows8 // 2 * CHANNELS + me * PART + lax.rem(rows8, 2) * CHUNK + lanes
    turns = (times * shift_ref[0]).astype(F32)
    folded = turns - jnp.floor(turns * (1.0 / SAMPLES)) * SAMPLES
    folded = jnp.where(folded < 0.0, folded + SAMPLES, folded)
    folded = jnp.where(folded >= SAMPLES, folded - SAMPLES, folded)
    angle = 2.0 * math.pi / SAMPLES * folded
    phase[0] = jnp.cos(angle)
    phase[1] = jnp.sin(angle)
    g[...] = jnp.zeros_like(g)

    def triangle(size):
        return lax.broadcasted_iota(jnp.int32, (size, size), 0) <= lax.broadcasted_iota(jnp.int32, (size, size), 1)

    def left_of(high_ref, low_ref, chunk, rows, imag):
        high = high_ref[chunk, rows, :]
        low = low_ref[chunk, rows, :]
        if imag:
            high = cat(high[:, CHUNK:], -high[:, :CHUNK])
            low = cat(low[:, CHUNK:], -low[:, :CHUNK])
        return cat(high, high, low)

    def right_of(chunk, rows):
        high = rh[chunk, rows, :]
        return cat(high, rl[chunk, rows, :], high)

    def add_blocks(kind, first, first_col, value):
        for i in range(value.shape[0] // BLOCK):
            for j in range(value.shape[1] // BLOCK):
                parity, slot = SLOT_OF[(first + i, first_col + j)]
                g[parity, slot, kind] += value[i * BLOCK:(i + 1) * BLOCK, j * BLOCK:(j + 1) * BLOCK]

    def arrive(group, chunk):
        own_copy(group, chunk).wait()
        for off in range(1, GROUP):
            sample_copy(group, chunk, off).wait_recv()
        cos_row = phase[0, pl.ds(chunk, 1), :]
        sin_row = phase[1, pl.ds(chunk, 1), :]
        for block in ((0, 1, 2), (3,))[group]:
            rows = pl.ds(block * BLOCK, BLOCK)
            real = xg[chunk, 0, rows, :]
            imag = xg[chunk, 1, rows, :]
            rh[chunk, rows, :], rl[chunk, rows, :] = split(cat(real, imag))
            uh[chunk, rows, :], ul[chunk, rows, :] = split(
                cat(real * cos_row + imag * sin_row, imag * cos_row - real * sin_row))

    front = pl.ds(0, 3 * BLOCK)
    back = pl.ds(3 * BLOCK, BLOCK)

    def early_chunk(chunk, carry):
        arrive(0, chunk)
        right = right_of(chunk, front)
        for imag in (0, 1):
            add_blocks(1 + imag, 0, 0, dot_nt(left_of(uh, ul, chunk, front, imag), right))
        add_blocks(0, 0, 0, jnp.where(
            triangle(3 * BLOCK), dot_nt(left_of(rh, rl, chunk, front, 0), right),
            dot_nt(left_of(rh, rl, chunk, front, 1), right)))
        return carry

    def late_chunk(chunk, carry):
        arrive(1, chunk)
        right = right_of(chunk, pl.ds(0, ELEMS))
        last = right_of(chunk, back)
        for imag in (0, 1):
            add_blocks(1 + imag, 3, 0, dot_nt(left_of(uh, ul, chunk, back, imag), right))
            add_blocks(1 + imag, 0, 3, dot_nt(left_of(uh, ul, chunk, front, imag), last))
        add_blocks(0, 0, 3, dot_nt(left_of(rh, rl, chunk, front, 0), last))
        low = dot_nt(left_of(rh, rl, chunk, back, 1), right)
        add_blocks(0, 3, 0, low[:, :3 * BLOCK])
        add_blocks(0, 3, 3, jnp.where(
            triangle(BLOCK), dot_nt(left_of(rh, rl, chunk, back, 0), last), low[:, 3 * BLOCK:]))
        return carry

    sibling = device_at(spot, "core", 1 - core)

    def slots_of(group, part):
        return pl.ds(part * 4 + group * 2, 2)

    def pair_copy(group, part):
        return pltpu.make_async_remote_copy(
            src_ref=g.at[1 - core, slots_of(group, part)], dst_ref=pair_got.at[slots_of(group, part)],
            send_sem=pair_send.at[group * 2 + part], recv_sem=pair_recv.at[group * 2 + part],
            device_id=sibling, device_id_type=MESH)

    def piece(part, stage, first, second):
        if stage == 0:
            return aligned(first * 32, 32)
        return aligned(first * 32 + second * 8, 8)

    def rs_copy(group, part, stage, off):
        axis = PLANE[part][stage]
        peer = lax.rem(spot[axis] + off, 4)
        rows = piece(part, 0, peer, 0) if stage == 0 else piece(part, 1, spot[PLANE[part][0]], peer)
        index = group * 16 + part * 8 + stage * 4 + off
        return pltpu.make_async_remote_copy(
            src_ref=g.at[core, slots_of(group, part), :, rows, :],
            dst_ref=(first_got if stage == 0 else second_got).at[group * 2 + part, off],
            send_sem=rs_send.at[index], recv_sem=rs_recv.at[index],
            device_id=device_at(spot, axis, peer), device_id_type=MESH)

    def rows_of(z):
        part = z // 4
        plane = (spot["x"] * 32 + spot["y"] * 8) * (1 - part) + (spot["y"] * 32 + spot["x"] * 8) * part
        return aligned(plane, 8)

    def z_copy(off):
        peer = lax.rem(spot["z"] + off, 8)
        return pltpu.make_async_remote_copy(
            src_ref=g.at[core, peer, :, rows_of(peer), :], dst_ref=z_got.at[off],
            send_sem=z_send.at[off], recv_sem=z_recv.at[off],
            device_id=device_at(spot, "z", peer), device_id_type=MESH)

    def az_copy(off):
        mine = spot["z"]
        where = o.at[core, mine, :, rows_of(mine), :]
        return pltpu.make_async_remote_copy(
            src_ref=where, dst_ref=where, send_sem=az_send.at[off], recv_sem=az_recv.at[off],
            device_id=device_at(spot, "z", lax.rem(mine + off, 8)), device_id_type=MESH)

    def ag_copy(part, stage, off):
        axis = PLANE[part][stage]
        peer = lax.rem(spot[axis] + off, 4)
        rows = piece(part, stage, spot[PLANE[part][0]], spot[PLANE[part][1]])
        where = o.at[core, pl.ds(part * 4, 4), :, rows, :]
        return pltpu.make_async_remote_copy(
            src_ref=where, dst_ref=where,
            send_sem=ag_send.at[part * 8 + stage * 4 + off], recv_sem=ag_recv.at[part * 8 + stage * 4 + off],
            device_id=device_at(spot, axis, peer), device_id_type=MESH)

    def forward_copy(part, off):
        origin = lax.rem(spot[PLANE[part][0]] + 4 - off, 4)
        where = o.at[core, pl.ds(part * 4, 4), :, aligned(origin * 32, 32), :]
        return pltpu.make_async_remote_copy(
            src_ref=where, dst_ref=where, send_sem=fw_send.at[part * 4 + off], recv_sem=fw_recv.at[part * 4 + off],
            device_id=sibling, device_id_type=MESH)

    def pair_send_out(group):
        for part in range(2):
            pair_copy(group, part).start()

    def pair_add(group):
        for part in range(2):
            pair_copy(group, part).wait_recv()
            for slot in range(part * 4 + group * 2, part * 4 + group * 2 + 2):
                g[core, slot] += pair_got[slot]
            for off in (2, 1, 3):
                rs_copy(group, part, 0, off).start()

    def plane_add(group, stage):
        got_ref = first_got if stage == 0 else second_got
        for part in range(2):
            for off in (1, 3, 2):
                rs_copy(group, part, stage, off).wait_recv()
            rows = piece(part, stage, spot[PLANE[part][0]], spot[PLANE[part][1]])
            which = group * 2 + part
            g[core, slots_of(group, part), :, rows, :] += got_ref[which, 1] + got_ref[which, 2] + got_ref[which, 3]
            if stage == 0:
                for off in (2, 1, 3):
                    rs_copy(group, part, 1, off).start()

    lax.fori_loop(0, GATE + 1, early_chunk, 0)
    send_group(1)
    lax.fori_loop(GATE + 1, CHUNKS, early_chunk, 0)
    pair_send_out(0)
    late_chunk(0, 0)
    pair_add(0)
    lax.fori_loop(1, 4, late_chunk, 0)
    plane_add(0, 0)
    lax.fori_loop(4, CHUNKS, late_chunk, 0)
    pair_send_out(1)
    plane_add(0, 1)
    pair_add(1)
    plane_add(1, 0)
    plane_add(1, 1)
    z_order = (4, 3, 5, 2, 6, 1, 7)
    for off in z_order:
        z_copy(off).start()
    mine = spot["z"]
    total = g[core, mine, :, rows_of(mine), :]
    for off in range(1, 8):
        z_copy(off).wait_recv()
    for off in range(1, 8):
        total = total + z_got[off]
    o[core, mine, :, rows_of(mine), :] = total
    for off in z_order:
        az_copy(off).start()
    for off in range(1, 8):
        az_copy(off).wait_recv()
    for part in range(2):
        for off in (2, 1, 3):
            ag_copy(part, 1, off).start()
    for part in range(2):
        for off in (1, 3, 2):
            ag_copy(part, 1, off).wait_recv()
        for off in (2, 1, 3):
            ag_copy(part, 0, off).start()
        forward_copy(part, 0).start()
    for off in (1, 3, 2):
        for part in range(2):
            ag_copy(part, 0, off).wait_recv()
            forward_copy(part, off).start()
    for off in range(1, GROUP):
        for group in range(2):
            start_copy(group, off).wait_recv()
    for part in range(2):
        for off in range(4):
            forward_copy(part, off).wait_recv()

    plain_scale = 1.0 / SAMPLES
    cyc_scale = 1.0 / math.sqrt(SAMPLES * ELEMS)

    def full(kind):
        return jnp.concatenate(
            [cat(*[o[SLOT_OF[(i, j)] + (kind,)] for j in range(4)]) for i in range(4)], axis=0)

    def put(high_ref, low_ref, col, value):
        high, low = split(value)
        high_ref[:, col * ELEMS:(col + 1) * ELEMS] = high
        low_ref[:, col * ELEMS:(col + 1) * ELEMS] = low

    packed = full(0) * plain_scale
    flipped = packed.T
    row_ids = lax.broadcasted_iota(jnp.int32, (ELEMS, ELEMS), 0)
    col_ids = lax.broadcasted_iota(jnp.int32, (ELEMS, ELEMS), 1)
    put(ah, al, 2, jnp.where(row_ids <= col_ids, packed, flipped))
    put(ah, al, 3, jnp.where(row_ids > col_ids, packed, jnp.where(row_ids < col_ids, -flipped, 0.0)))
    cyc_real = full(1) * cyc_scale
    put(ah, al, 0, cyc_real)
    put(bh, bl, 0, cyc_real.T)
    cyc_imag = full(2) * cyc_scale
    put(ah, al, 1, cyc_imag)
    put(bh, bl, 1, -cyc_imag.T)

    lane = lax.broadcasted_iota(jnp.int32, (ELEMS, 2 * BEAMS), 1)

    def turned(vector):
        other = pltpu.roll(vector, BEAMS, 1)
        return jnp.where(lane < BEAMS, -other, other)

    def normalized(vector):
        squares = jnp.sum(vector * vector, axis=0, keepdims=True)
        squares = jnp.broadcast_to(squares, (8, 2 * BEAMS))
        squares = squares + pltpu.roll(squares, BEAMS, 1)
        return vector * (1.0 / jnp.sqrt(squares[:1] + EPS))

    def stacked(vector):
        high, low = split(jnp.concatenate([vector, turned(vector)], axis=0))
        return cat(high, low)

    def product(high, low, right):
        wide_out = dot_nn(high, right)
        return wide_out[:, :2 * BEAMS] + wide_out[:, 2 * BEAMS:] + dot_nn(low, right[:, :2 * BEAMS])

    v_ref[...] = normalized(sg[...])

    def step(iteration, carry):
        held = stacked(v_ref[...])
        mid = product(bh[...], bl[...], held)
        v_ref[...] = normalized(product(ah[...], al[...], jnp.concatenate([stacked(mid), held], axis=0)))
        return carry

    lax.fori_loop(0, ITERS, step, 0)
    mine = jnp.concatenate([v_ref[virtual(0), :], v_ref[virtual(1), :]], axis=0)
    weights_ref[...] = mine.T.reshape(2, BEAMS, OWN)

    vh, vl = split(v_ref[...].T)
    left = jnp.concatenate([vh, vl], axis=0)
    tap_fetch.wait()
    taps = tap_ref[:, aligned(me * PART, PART)].astype(F32) / 2048.0
    beams = ([], [])
    for frame in range(FRAMES):
        pieces = [xg[frame * 2 + half, kind] for kind in range(2) for half in range(2)]
        xh, xl = split(cat(*pieces))
        both = dot_nn(left, xh)
        out = both[:2 * BEAMS] + both[2 * BEAMS:] + dot_nn(vh, xl)
        beams[0].append(out[:BEAMS, :PART] + out[BEAMS:, PART:])
        beams[1].append(out[:BEAMS, PART:] - out[BEAMS:, :PART])

    def filtered(kind, frame):
        total = None
        for tap in range(TAPS):
            if 0 <= frame - tap < FRAMES:
                term = taps[tap:tap + 1, :] * beams[kind][frame - tap]
                total = term if total is None else total + term
        return total

    for kind in range(2):
        for frame in range(FRAMES):
            after[kind, frame] = filtered(kind, frame + FRAMES)

    def quarter(off):
        return aligned(lax.rem(me + off, GROUP) * QUARTER, QUARTER)

    def halo_copy(off):
        rows = quarter(off)
        return pltpu.make_async_remote_copy(
            src_ref=after.at[:, :, rows, :], dst_ref=halo.at[:, :, rows, :],
            send_sem=halo_send.at[off], recv_sem=halo_recv.at[off],
            device_id={"tm": tm + 1, "elem": me}, device_id_type=MESH)

    def cross_copy(off):
        return pltpu.make_async_remote_copy(
            src_ref=after.at[:, :, quarter(off), :], dst_ref=crossed.at[off],
            send_sem=cross_send.at[off], recv_sem=cross_recv.at[off],
            device_id={"tm": tm + 1, "elem": lax.rem(me + off, GROUP)}, device_id_type=MESH)

    def last_copy(off):
        return pltpu.make_async_remote_copy(
            src_ref=own.at[:, :, quarter(off), :], dst_ref=got.at[off],
            send_sem=last_send.at[off], recv_sem=last_recv.at[off],
            device_id={"elem": lax.rem(me + off, GROUP)}, device_id_type=MESH)

    order = (2, 1, 3, 0)

    @pl.when(near_out)
    def _():
        for off in order:
            halo_copy(off).start()

    @pl.when(cross_out)
    def _():
        for off in order:
            cross_copy(off).start()

    for kind in range(2):
        for frame in range(FRAMES):
            own[kind, frame] = filtered(kind, frame)

    for off in order:
        @pl.when(near_in)
        def _():
            halo_copy(off).wait_recv()
            rows = quarter(off)
            own[:, :, rows, :] += halo[:, :, rows, :]

        if off:
            last_copy(off).start()
        else:
            got[0] = own[:, :, quarter(0), :]

    table_copy.wait()
    rows = 2 * FRAMES * QUARTER
    half = FRAMES * QUARTER
    for position, off in enumerate((0, 1, 3, 2)):
        if off:
            last_copy(off).wait_recv()

        @pl.when(cross_in)
        def _():
            cross_copy(off).wait_recv()
            got[off] += crossed[off]

        high, low = split(got[off].reshape(rows, PART))
        left = jnp.concatenate([high, low], axis=0)
        where = aligned(lax.rem(me + GROUP - off, GROUP) * PART, PART)

        def times_table(index):
            both = dot_nn(left, table[index, where, :])
            return both[:rows] + both[rows:] + dot_nn(high, table[index + 1, where, :])

        with_cos = times_table(0)
        with_sin = times_table(2)
        real = with_cos[:half] + with_sin[half:]
        imag = with_cos[half:] - with_sin[:half]
        if position == 0:
            out_ref[0] = real
            out_ref[1] = imag
        else:
            out_ref[0] += real
            out_ref[1] += imag

    for off in range(1, GROUP):
        last_copy(off).wait_send()
        for group in range(2):
            start_copy(group, off).wait_send()
            for chunk in range(CHUNKS):
                sample_copy(group, chunk, off).wait_send()
        for part in range(2):
            for stage in range(2):
                for group in range(2):
                    rs_copy(group, part, stage, off).wait_send()
                ag_copy(part, stage, off).wait_send()
    for off in range(1, 8):
        z_copy(off).wait_send()
        az_copy(off).wait_send()
    for part in range(2):
        for group in range(2):
            pair_copy(group, part).wait_send()
        for off in range(4):
            forward_copy(part, off).wait_send()

    @pl.when(near_out)
    def _():
        for off in order:
            halo_copy(off).wait_send()

    @pl.when(cross_out)
    def _():
        for off in order:
            cross_copy(off).wait_send()


def finish_kernel(spectra_ref, weights_ref, spectra_out, weights_out):
    spectra_out[...] = spectra_ref[...]
    weights_out[...] = weights_ref[...]


def body(samples, shift_bin, start_vectors, tap_table):
    vmem = pl.BlockSpec(memory_space=pltpu.VMEM)
    smem = pl.BlockSpec(memory_space=pltpu.SMEM)
    hbm = pl.BlockSpec(memory_space=pl.ANY)
    dma = pltpu.SemaphoreType.DMA
    scratch = [
        ((2, BEAMS, OWN), jnp.int32),
        ((TAPS, CHANNELS), jnp.int32),
        ((CHUNKS, 2, ELEMS, CHUNK), F32),
        ((ELEMS, 2 * BEAMS), F32),
        ((2, 8, CHUNK), F32),
        ((CHUNKS, ELEMS, 2 * CHUNK), BF16),
        ((CHUNKS, ELEMS, 2 * CHUNK), BF16),
        ((CHUNKS, ELEMS, 2 * CHUNK), BF16),
        ((CHUNKS, ELEMS, 2 * CHUNK), BF16),
        ((2, 8, 3, BLOCK, BLOCK), F32),
        ((2, 8, 3, BLOCK, BLOCK), F32),
        ((8, 3, BLOCK, BLOCK), F32),
        ((4, 4, 2, 3, 32, BLOCK), F32),
        ((4, 4, 2, 3, 8, BLOCK), F32),
        ((8, 3, 8, BLOCK), F32),
        ((ELEMS, 2 * BEAMS), F32),
        ((ELEMS, 4 * ELEMS), BF16),
        ((ELEMS, 4 * ELEMS), BF16),
        ((ELEMS, 2 * ELEMS), BF16),
        ((ELEMS, 2 * ELEMS), BF16),
        ((4, CHANNELS, CHANNELS), BF16),
        ((2, FRAMES, BEAMS, PART), F32),
        ((2, FRAMES, BEAMS, PART), F32),
        ((2, FRAMES, BEAMS, PART), F32),
        ((GROUP, 2, FRAMES, QUARTER, PART), F32),
        ((GROUP, 2, FRAMES, QUARTER, PART), F32),
    ]
    semaphores = [
        (2 * CHUNKS, GROUP), (2 * CHUNKS, GROUP), (2 * CHUNKS,), (8,), (8,), None, (2,),
        (4,), (4,), (32,), (32,), (8,), (8,), (8,), (8,), (16,), (16,),
        (8,), (8,), (GROUP,), (GROUP,), (GROUP,), (GROUP,), (GROUP,), (GROUP,),
    ]
    spectra, weights = pl.pallas_call(
        kernel,
        out_shape=(
            jax.ShapeDtypeStruct((2, FRAMES * QUARTER, CHANNELS), F32),
            jax.ShapeDtypeStruct((2, BEAMS, OWN), F32),
        ),
        in_specs=[hbm, hbm, smem, hbm, hbm],
        out_specs=(vmem, vmem),
        scratch_shapes=[pltpu.VMEM(*entry) for entry in scratch]
        + [dma if shape is None else dma(shape) for shape in semaphores],
        compiler_params=pltpu.CompilerParams(
            collective_id=0, has_side_effects=True, vmem_limit_bytes=VMEM_LIMIT),
        name="beamformer",
    )(samples, start_vectors.transpose(0, 2, 1), shift_bin, tap_table, jnp.asarray(dft_tables()))
    spectra, weights = pl.pallas_call(
        finish_kernel,
        out_shape=(
            jax.ShapeDtypeStruct((2, FRAMES * QUARTER, CHANNELS), F32),
            jax.ShapeDtypeStruct((2, BEAMS, OWN), F32),
        ),
        in_specs=[vmem, vmem],
        out_specs=(vmem, vmem),
        name="finish",
    )(spectra, weights)
    spectra = spectra.reshape(2, FRAMES, QUARTER, CHANNELS).transpose(0, 2, 1, 3)
    return (spectra, weights.transpose(0, 2, 1))


def solution(mesh):
    return jax.shard_map(
        body,
        mesh=mesh,
        in_specs=(P(None, "elem", "tm"), P(), P(None, "elem", None), P()),
        out_specs=(P(None, "elem", "tm", None), P(None, "elem", None)),
        check_vma=False,
    )
```

```python
import math

import jax
import jax.numpy as jnp
import ml_dtypes
import numpy as np
from jax import lax
from jax.experimental import pallas as pl
from jax.experimental.pallas import tpu as pltpu
from jax.sharding import PartitionSpec as P

ELEMS = 512
BEAMS = 64
CHANNELS = 1024
TAPS = 4
ITERS = 3
SPAN = 3072
SAMPLES = 196608
FRAMES = SPAN // CHANNELS
GROUP = 4
OWN = ELEMS // GROUP
PART = CHANNELS // GROUP
TM = SAMPLES // SPAN
QUARTER = BEAMS // GROUP

EPS = 1e-06
F32 = jnp.float32
BF16 = jnp.bfloat16
MESH = pl.DeviceIdType.MESH
VMEM_LIMIT = 56 * 1024 * 1024

CHUNK = 128
EARLY = 96
LATE = OWN - EARLY
GATE = 4
CHUNKS = SPAN // GROUP // CHUNK
BLOCK = 128
SIZES = {"core": 2, "x": 4, "y": 4, "z": 8}
PLANE = (("x", "y"), ("y", "x"))
SLOTS = (
    ((0, 0), (0, 2), (1, 1), (1, 3), (2, 0), (2, 2), (3, 1), (3, 3)),
    ((0, 1), (1, 0), (0, 3), (3, 0), (1, 2), (2, 1), (2, 3), (3, 2)),
)
SLOT_OF = {block: (parity, slot) for parity in range(2) for slot, block in enumerate(SLOTS[parity])}


def split(value):
    high = value.astype(BF16)
    return high, (value - high.astype(F32)).astype(BF16)


def dot_nt(left, right):
    return lax.dot_general(left, right, (((1,), (1,)), ((), ())), preferred_element_type=F32)


def dot_nn(left, right):
    return lax.dot_general(left, right, (((1,), (0,)), ((), ())), preferred_element_type=F32)


def cat(*pieces):
    return jnp.concatenate(pieces, axis=1)


def dft_tables():
    ids = np.arange(CHANNELS)
    angle = 2.0 * np.pi / CHANNELS * (ids[:, None] * ids[None, :] % CHANNELS)
    out = []
    for table in (np.cos(angle), np.sin(angle)):
        table = (table / math.sqrt(CHANNELS)).astype(np.float32)
        high = table.astype(ml_dtypes.bfloat16)
        out += [high, (table - high.astype(np.float32)).astype(ml_dtypes.bfloat16)]
    return np.stack(out)


def place():
    tm = lax.axis_index("tm")
    return {
        "core": lax.rem(tm, 2),
        "x": lax.rem(tm // 2, 4),
        "y": tm // 16,
        "z": lax.rem(tm // 8, 2) * 4 + lax.axis_index("elem"),
    }


def device_at(spot, axis, value):
    at = dict(spot)
    at[axis] = value
    tm = ((at["y"] * 2 + at["z"] // 4) * 4 + at["x"]) * 2 + at["core"]
    return {"tm": tm, "elem": lax.rem(at["z"], 4)}


def aligned(start, size):
    return pl.ds(pl.multiple_of(start, size), size)


def kernel(x_ref, start_hbm, shift_ref, tap_hbm, table_ref, out_ref, weights_ref,
           start_ref, tap_ref, xg, sg, phase, rh, rl, uh, ul, g, o, pair_got, first_got, second_got, z_got, v_ref, ah, al, bh, bl,
           table, own, after, halo, got, crossed,
           send_sem, recv_sem, own_sem, s_send, s_recv, table_sem, input_sem,
           pair_send, pair_recv, rs_send, rs_recv, z_send, z_recv, az_send, az_recv, ag_send, ag_recv,
           fw_send, fw_recv, halo_send, halo_recv, cross_send, cross_recv, last_send, last_recv):
    tm = lax.axis_index("tm")
    me = lax.axis_index("elem")
    spot = place()
    core = spot["core"]

    table_copy = pltpu.make_async_copy(table_ref, table, table_sem)
    start_fetch = pltpu.make_async_copy(start_hbm, start_ref, input_sem.at[0])
    tap_fetch = pltpu.make_async_copy(tap_hbm, tap_ref, input_sem.at[1])
    start_fetch.start()
    tap_fetch.start()

    barrier = pltpu.get_barrier_semaphore()
    count = 0
    for axis, size in SIZES.items():
        for off in range(1, size):
            pl.semaphore_signal(
                barrier, inc=1, device_id=device_at(spot, axis, lax.rem(spot[axis] + off, size)),
                device_id_type=MESH)
            count += 1
    turn = lax.rem(tm, 8)
    near_out = turn != 7
    near_in = turn != 0
    cross_out = jnp.logical_and(turn == 7, tm < TM - 1)
    cross_in = jnp.logical_and(turn == 0, tm > 0)

    @pl.when(near_out)
    def _():
        pl.semaphore_signal(barrier, inc=1, device_id={"tm": tm + 1, "elem": me}, device_id_type=MESH)

    @pl.when(near_in)
    def _():
        pl.semaphore_signal(barrier, inc=1, device_id={"tm": tm - 1, "elem": me}, device_id_type=MESH)

    @pl.when(cross_out)
    def _():
        for peer in range(GROUP):
            pl.semaphore_signal(barrier, inc=1, device_id={"tm": tm + 1, "elem": peer}, device_id_type=MESH)

    @pl.when(cross_in)
    def _():
        for peer in range(GROUP):
            pl.semaphore_signal(barrier, inc=1, device_id={"tm": tm - 1, "elem": peer}, device_id_type=MESH)

    number = lambda flag: flag.astype(jnp.int32)
    pl.semaphore_wait(
        barrier, count + number(near_out) + number(near_in) + GROUP * (number(cross_out) + number(cross_in)))

    firsts = (0, EARLY)
    counts = (EARLY, LATE)

    def virtual(group):
        return aligned(me * EARLY, EARLY) if group == 0 else aligned(GROUP * EARLY + me * LATE, LATE)

    def start_copy(group, off):
        where = sg.at[virtual(group), :]
        return pltpu.make_async_remote_copy(
            src_ref=where, dst_ref=where,
            send_sem=s_send.at[group * 4 + off], recv_sem=s_recv.at[group * 4 + off],
            device_id={"elem": lax.rem(me + off, GROUP)}, device_id_type=MESH)

    def columns(chunk, peer):
        return aligned(chunk // 2 * CHANNELS + peer * PART + lax.rem(chunk, 2) * CHUNK, CHUNK)

    def sample_copy(group, chunk, off):
        peer = lax.rem(me + off, GROUP)
        return pltpu.make_async_remote_copy(
            src_ref=x_ref.at[:, pl.ds(firsts[group], counts[group]), columns(chunk, peer)],
            dst_ref=xg.at[chunk, :, virtual(group), :],
            send_sem=send_sem.at[group * CHUNKS + chunk, off], recv_sem=recv_sem.at[group * CHUNKS + chunk, off],
            device_id={"elem": peer}, device_id_type=MESH)

    def own_copy(group, chunk):
        return pltpu.make_async_copy(
            x_ref.at[:, pl.ds(firsts[group], counts[group]), columns(chunk, me)],
            xg.at[chunk, :, virtual(group), :], own_sem.at[group * CHUNKS + chunk])

    def send_group(group):
        for chunk in range(CHUNKS):
            for off in (2, 1, 3):
                sample_copy(group, chunk, off).start()
            own_copy(group, chunk).start()

    send_group(0)
    table_copy.start()
    start_fetch.wait()
    starts = (start_ref[...].reshape(2 * BEAMS, OWN).astype(F32) - 4.5).T
    for group in range(2):
        sg[virtual(group), :] = starts[firsts[group]:firsts[group] + counts[group]]
        for off in range(1, GROUP):
            start_copy(group, off).start()

    rows8 = lax.broadcasted_iota(jnp.int32, (8, CHUNK), 0)
    lanes = lax.broadcasted_iota(jnp.int32, (8, CHUNK), 1)
    times = tm * SPAN + rows8 // 2 * CHANNELS + me * PART + lax.rem(rows8, 2) * CHUNK + lanes
    turns = (times * shift_ref[0]).astype(F32)
    folded = turns - jnp.floor(turns * (1.0 / SAMPLES)) * SAMPLES
    folded = jnp.where(folded < 0.0, folded + SAMPLES, folded)
    folded = jnp.where(folded >= SAMPLES, folded - SAMPLES, folded)
    angle = 2.0 * math.pi / SAMPLES * folded
    phase[0] = jnp.cos(angle)
    phase[1] = jnp.sin(angle)
    g[...] = jnp.zeros_like(g)

    def triangle(size):
        return lax.broadcasted_iota(jnp.int32, (size, size), 0) <= lax.broadcasted_iota(jnp.int32, (size, size), 1)

    def left_of(high_ref, low_ref, chunk, rows, imag):
        high = high_ref[chunk, rows, :]
        low = low_ref[chunk, rows, :]
        if imag:
            high = cat(high[:, CHUNK:], -high[:, :CHUNK])
            low = cat(low[:, CHUNK:], -low[:, :CHUNK])
        return cat(high, high, low)

    def right_of(chunk, rows):
        high = rh[chunk, rows, :]
        return cat(high, rl[chunk, rows, :], high)

    def add_blocks(kind, first, first_col, value):
        for i in range(value.shape[0] // BLOCK):
            for j in range(value.shape[1] // BLOCK):
                parity, slot = SLOT_OF[(first + i, first_col + j)]
                g[parity, slot, kind] += value[i * BLOCK:(i + 1) * BLOCK, j * BLOCK:(j + 1) * BLOCK]

    def arrive(group, chunk):
        own_copy(group, chunk).wait()
        for off in range(1, GROUP):
            sample_copy(group, chunk, off).wait_recv()
        cos_row = phase[0, pl.ds(chunk, 1), :]
        sin_row = phase[1, pl.ds(chunk, 1), :]
        for block in ((0, 1, 2), (3,))[group]:
            rows = pl.ds(block * BLOCK, BLOCK)
            real = xg[chunk, 0, rows, :]
            imag = xg[chunk, 1, rows, :]
            rh[chunk, rows, :], rl[chunk, rows, :] = split(cat(real, imag))
            uh[chunk, rows, :], ul[chunk, rows, :] = split(
                cat(real * cos_row + imag * sin_row, imag * cos_row - real * sin_row))

    front = pl.ds(0, 3 * BLOCK)
    back = pl.ds(3 * BLOCK, BLOCK)

    def early_chunk(chunk, carry):
        arrive(0, chunk)
        right = right_of(chunk, front)
        for imag in (0, 1):
            add_blocks(1 + imag, 0, 0, dot_nt(left_of(uh, ul, chunk, front, imag), right))
        add_blocks(0, 0, 0, jnp.where(
            triangle(3 * BLOCK), dot_nt(left_of(rh, rl, chunk, front, 0), right),
            dot_nt(left_of(rh, rl, chunk, front, 1), right)))
        return carry

    def late_chunk(chunk, carry):
        arrive(1, chunk)
        right = right_of(chunk, pl.ds(0, ELEMS))
        last = right_of(chunk, back)
        for imag in (0, 1):
            add_blocks(1 + imag, 3, 0, dot_nt(left_of(uh, ul, chunk, back, imag), right))
            add_blocks(1 + imag, 0, 3, dot_nt(left_of(uh, ul, chunk, front, imag), last))
        add_blocks(0, 0, 3, dot_nt(left_of(rh, rl, chunk, front, 0), last))
        low = dot_nt(left_of(rh, rl, chunk, back, 1), right)
        add_blocks(0, 3, 0, low[:, :3 * BLOCK])
        add_blocks(0, 3, 3, jnp.where(
            triangle(BLOCK), dot_nt(left_of(rh, rl, chunk, back, 0), last), low[:, 3 * BLOCK:]))
        return carry

    sibling = device_at(spot, "core", 1 - core)

    def slots_of(group, part):
        return pl.ds(part * 4 + group * 2, 2)

    def pair_copy(group, part):
        return pltpu.make_async_remote_copy(
            src_ref=g.at[1 - core, slots_of(group, part)], dst_ref=pair_got.at[slots_of(group, part)],
            send_sem=pair_send.at[group * 2 + part], recv_sem=pair_recv.at[group * 2 + part],
            device_id=sibling, device_id_type=MESH)

    def piece(part, stage, first, second):
        if stage == 0:
            return aligned(first * 32, 32)
        return aligned(first * 32 + second * 8, 8)

    def rs_copy(group, part, stage, off):
        axis = PLANE[part][stage]
        peer = lax.rem(spot[axis] + off, 4)
        rows = piece(part, 0, peer, 0) if stage == 0 else piece(part, 1, spot[PLANE[part][0]], peer)
        index = group * 16 + part * 8 + stage * 4 + off
        return pltpu.make_async_remote_copy(
            src_ref=g.at[core, slots_of(group, part), :, rows, :],
            dst_ref=(first_got if stage == 0 else second_got).at[group * 2 + part, off],
            send_sem=rs_send.at[index], recv_sem=rs_recv.at[index],
            device_id=device_at(spot, axis, peer), device_id_type=MESH)

    def rows_of(z):
        part = z // 4
        plane = (spot["x"] * 32 + spot["y"] * 8) * (1 - part) + (spot["y"] * 32 + spot["x"] * 8) * part
        return aligned(plane, 8)

    def z_copy(off):
        peer = lax.rem(spot["z"] + off, 8)
        return pltpu.make_async_remote_copy(
            src_ref=g.at[core, peer, :, rows_of(peer), :], dst_ref=z_got.at[off],
            send_sem=z_send.at[off], recv_sem=z_recv.at[off],
            device_id=device_at(spot, "z", peer), device_id_type=MESH)

    def az_copy(off):
        mine = spot["z"]
        where = o.at[core, mine, :, rows_of(mine), :]
        return pltpu.make_async_remote_copy(
            src_ref=where, dst_ref=where, send_sem=az_send.at[off], recv_sem=az_recv.at[off],
            device_id=device_at(spot, "z", lax.rem(mine + off, 8)), device_id_type=MESH)

    def ag_copy(group, part, stage, off):
        axis = PLANE[part][stage]
        peer = lax.rem(spot[axis] + off, 4)
        rows = piece(part, stage, spot[PLANE[part][0]], spot[PLANE[part][1]])
        where = o.at[core, slots_of(group, part), :, rows, :]
        index = group * 16 + part * 8 + stage * 4 + off
        return pltpu.make_async_remote_copy(
            src_ref=where, dst_ref=where, send_sem=ag_send.at[index], recv_sem=ag_recv.at[index],
            device_id=device_at(spot, axis, peer), device_id_type=MESH)

    def forward_copy(group, part, off):
        origin = lax.rem(spot[PLANE[part][0]] + 4 - off, 4)
        where = o.at[core, slots_of(group, part), :, aligned(origin * 32, 32), :]
        index = group * 8 + part * 4 + off
        return pltpu.make_async_remote_copy(
            src_ref=where, dst_ref=where, send_sem=fw_send.at[index], recv_sem=fw_recv.at[index],
            device_id=sibling, device_id_type=MESH)

    def pair_send_out(group):
        for part in range(2):
            pair_copy(group, part).start()

    def pair_add(group):
        for part in range(2):
            pair_copy(group, part).wait_recv()
            for slot in range(part * 4 + group * 2, part * 4 + group * 2 + 2):
                g[core, slot] += pair_got[slot]
            for off in (2, 1, 3):
                rs_copy(group, part, 0, off).start()

    def plane_add(group, stage):
        got_ref = first_got if stage == 0 else second_got
        for part in range(2):
            for off in (1, 3, 2):
                rs_copy(group, part, stage, off).wait_recv()
            rows = piece(part, stage, spot[PLANE[part][0]], spot[PLANE[part][1]])
            which = group * 2 + part
            g[core, slots_of(group, part), :, rows, :] += got_ref[which, 1] + got_ref[which, 2] + got_ref[which, 3]
            if stage == 0:
                for off in (2, 1, 3):
                    rs_copy(group, part, 1, off).start()

    z_order = (4, 3, 5, 2, 6, 1, 7)
    mine = spot["z"]

    def group_of(z):
        return lax.rem(z // 2, 2)

    def z_start(group):
        for off in z_order:
            @pl.when(group_of(lax.rem(mine + off, 8)) == group)
            def _():
                z_copy(off).start()

    def z_sum(group):
        @pl.when(group_of(mine) == group)
        def _():
            for off in range(1, 8):
                z_copy(off).wait_recv()
            total = g[core, mine, :, rows_of(mine), :]
            for off in range(1, 8):
                total = total + z_got[off]
            o[core, mine, :, rows_of(mine), :] = total
            for off in z_order:
                az_copy(off).start()

    def z_gather(group):
        for off in range(1, 8):
            @pl.when(group_of(lax.rem(mine + 8 - off, 8)) == group)
            def _():
                az_copy(off).wait_recv()
        for part in range(2):
            for off in (2, 1, 3):
                ag_copy(group, part, 1, off).start()

    def ag_middle(group):
        for part in range(2):
            for off in (1, 3, 2):
                ag_copy(group, part, 1, off).wait_recv()
            for off in (2, 1, 3):
                ag_copy(group, part, 0, off).start()
            forward_copy(group, part, 0).start()

    def ag_last(group):
        for off in (1, 3, 2):
            for part in range(2):
                ag_copy(group, part, 0, off).wait_recv()
                forward_copy(group, part, off).start()

    def ag_done(group):
        for part in range(2):
            for off in range(4):
                forward_copy(group, part, off).wait_recv()

    plain_scale = 1.0 / SAMPLES
    cyc_scale = 1.0 / math.sqrt(SAMPLES * ELEMS)

    def put(high_ref, low_ref, row, kind, col, value):
        rows = pl.ds(row * BLOCK, BLOCK)
        cols = pl.ds(kind * ELEMS + col * BLOCK, BLOCK)
        high_ref[rows, cols], low_ref[rows, cols] = split(value)

    def prepare(group):
        for parity in range(2):
            for slot in range(8):
                if slot // 2 % 2 != group:
                    continue
                i, j = SLOTS[parity][slot]
                for imag in (0, 1):
                    block = o[parity, slot, 1 + imag] * cyc_scale
                    put(ah, al, i, imag, j, block)
                    put(bh, bl, j, imag, i, -block.T if imag else block.T)
                block = o[parity, slot, 0] * plain_scale
                turned_block = block.T
                if i < j:
                    put(ah, al, i, 2, j, block)
                    put(ah, al, j, 2, i, turned_block)
                elif i > j:
                    put(ah, al, i, 3, j, block)
                    put(ah, al, j, 3, i, -turned_block)
                else:
                    row_ids = lax.broadcasted_iota(jnp.int32, (BLOCK, BLOCK), 0)
                    col_ids = lax.broadcasted_iota(jnp.int32, (BLOCK, BLOCK), 1)
                    put(ah, al, i, 2, i, jnp.where(row_ids <= col_ids, block, turned_block))
                    put(ah, al, i, 3, i, jnp.where(
                        row_ids > col_ids, block, jnp.where(row_ids < col_ids, -turned_block, 0.0)))

    lax.fori_loop(0, GATE + 1, early_chunk, 0)
    send_group(1)
    lax.fori_loop(GATE + 1, CHUNKS, early_chunk, 0)
    pair_send_out(0)
    late_chunk(0, 0)
    pair_add(0)
    lax.fori_loop(1, 4, late_chunk, 0)
    plane_add(0, 0)
    lax.fori_loop(4, CHUNKS, late_chunk, 0)
    pair_send_out(1)
    plane_add(0, 1)
    z_start(0)
    pair_add(1)
    z_sum(0)
    plane_add(1, 0)
    plane_add(1, 1)
    z_start(1)
    z_gather(0)
    ag_middle(0)
    z_sum(1)
    ag_last(0)
    z_gather(1)
    ag_done(0)
    prepare(0)
    ag_middle(1)
    for off in range(1, GROUP):
        for group in range(2):
            start_copy(group, off).wait_recv()
    ag_last(1)
    ag_done(1)
    prepare(1)

    lane = lax.broadcasted_iota(jnp.int32, (ELEMS, 2 * BEAMS), 1)

    def turned(vector):
        other = pltpu.roll(vector, BEAMS, 1)
        return jnp.where(lane < BEAMS, -other, other)

    def normalized(vector):
        squares = jnp.sum(vector * vector, axis=0, keepdims=True)
        squares = jnp.broadcast_to(squares, (8, 2 * BEAMS))
        squares = squares + pltpu.roll(squares, BEAMS, 1)
        return vector * (1.0 / jnp.sqrt(squares[:1] + EPS))

    def stacked(vector):
        high, low = split(jnp.concatenate([vector, turned(vector)], axis=0))
        return cat(high, low)

    def product(high, low, right):
        wide_out = dot_nn(high, right)
        return wide_out[:, :2 * BEAMS] + wide_out[:, 2 * BEAMS:] + dot_nn(low, right[:, :2 * BEAMS])

    v_ref[...] = normalized(sg[...])

    def step(iteration, carry):
        held = stacked(v_ref[...])
        mid = product(bh[...], bl[...], held)
        v_ref[...] = normalized(product(ah[...], al[...], jnp.concatenate([stacked(mid), held], axis=0)))
        return carry

    lax.fori_loop(0, ITERS, step, 0)
    mine = jnp.concatenate([v_ref[virtual(0), :], v_ref[virtual(1), :]], axis=0)
    weights_ref[...] = mine.T.reshape(2, BEAMS, OWN)

    vh, vl = split(v_ref[...].T)
    left = jnp.concatenate([vh, vl], axis=0)
    tap_fetch.wait()
    taps = tap_ref[:, aligned(me * PART, PART)].astype(F32) / 2048.0
    beams = ([], [])
    for frame in range(FRAMES):
        xh = cat(rh[frame * 2], rh[frame * 2 + 1])
        xl = cat(rl[frame * 2], rl[frame * 2 + 1])
        both = dot_nn(left, xh)
        out = both[:2 * BEAMS] + both[2 * BEAMS:] + dot_nn(vh, xl)
        top, low = out[:BEAMS], out[BEAMS:]
        beams[0].append(cat(*[top[:, c:c + CHUNK] + low[:, c + CHUNK:c + 2 * CHUNK] for c in (0, 2 * CHUNK)]))
        beams[1].append(cat(*[top[:, c + CHUNK:c + 2 * CHUNK] - low[:, c:c + CHUNK] for c in (0, 2 * CHUNK)]))

    def filtered(kind, frame):
        total = None
        for tap in range(TAPS):
            if 0 <= frame - tap < FRAMES:
                term = taps[tap:tap + 1, :] * beams[kind][frame - tap]
                total = term if total is None else total + term
        return total

    for kind in range(2):
        for frame in range(FRAMES):
            after[kind, frame] = filtered(kind, frame + FRAMES)

    def quarter(off):
        return aligned(lax.rem(me + off, GROUP) * QUARTER, QUARTER)

    def halo_copy(off):
        rows = quarter(off)
        return pltpu.make_async_remote_copy(
            src_ref=after.at[:, :, rows, :], dst_ref=halo.at[:, :, rows, :],
            send_sem=halo_send.at[off], recv_sem=halo_recv.at[off],
            device_id={"tm": tm + 1, "elem": me}, device_id_type=MESH)

    def cross_copy(off):
        return pltpu.make_async_remote_copy(
            src_ref=after.at[:, :, quarter(off), :], dst_ref=crossed.at[off],
            send_sem=cross_send.at[off], recv_sem=cross_recv.at[off],
            device_id={"tm": tm + 1, "elem": lax.rem(me + off, GROUP)}, device_id_type=MESH)

    def last_copy(off):
        return pltpu.make_async_remote_copy(
            src_ref=own.at[:, :, quarter(off), :], dst_ref=got.at[off],
            send_sem=last_send.at[off], recv_sem=last_recv.at[off],
            device_id={"elem": lax.rem(me + off, GROUP)}, device_id_type=MESH)

    order = (2, 1, 3, 0)

    @pl.when(near_out)
    def _():
        for off in order:
            halo_copy(off).start()

    @pl.when(cross_out)
    def _():
        for off in order:
            cross_copy(off).start()

    for kind in range(2):
        for frame in range(FRAMES):
            own[kind, frame] = filtered(kind, frame)

    for off in order:
        @pl.when(near_in)
        def _():
            halo_copy(off).wait_recv()
            rows = quarter(off)
            own[:, :, rows, :] += halo[:, :, rows, :]

        if off:
            last_copy(off).start()
        else:
            got[0] = own[:, :, quarter(0), :]

    table_copy.wait()
    rows = 2 * FRAMES * QUARTER
    half = FRAMES * QUARTER
    for position, off in enumerate((0, 1, 3, 2)):
        if off:
            last_copy(off).wait_recv()

        @pl.when(cross_in)
        def _():
            cross_copy(off).wait_recv()
            got[off] += crossed[off]

        high, low = split(got[off].reshape(rows, PART))
        left = jnp.concatenate([high, low], axis=0)
        where = aligned(lax.rem(me + GROUP - off, GROUP) * PART, PART)

        def times_table(index):
            both = dot_nn(left, table[index, where, :])
            return both[:rows] + both[rows:] + dot_nn(high, table[index + 1, where, :])

        with_cos = times_table(0)
        with_sin = times_table(2)
        real = with_cos[:half] + with_sin[half:]
        imag = with_cos[half:] - with_sin[:half]
        if position == 0:
            out_ref[0] = real
            out_ref[1] = imag
        else:
            out_ref[0] += real
            out_ref[1] += imag

    for off in range(1, GROUP):
        last_copy(off).wait_send()
        for group in range(2):
            start_copy(group, off).wait_send()
            for chunk in range(CHUNKS):
                sample_copy(group, chunk, off).wait_send()
        for part in range(2):
            for stage in range(2):
                for group in range(2):
                    rs_copy(group, part, stage, off).wait_send()
                    ag_copy(group, part, stage, off).wait_send()
    for off in range(1, 8):
        z_copy(off).wait_send()
        az_copy(off).wait_send()
    for part in range(2):
        for group in range(2):
            pair_copy(group, part).wait_send()
        for off in range(4):
            for group in range(2):
                forward_copy(group, part, off).wait_send()

    @pl.when(near_out)
    def _():
        for off in order:
            halo_copy(off).wait_send()

    @pl.when(cross_out)
    def _():
        for off in order:
            cross_copy(off).wait_send()


def finish_kernel(spectra_ref, weights_ref, spectra_out, weights_out):
    spectra_out[...] = spectra_ref[...]
    weights_out[...] = weights_ref[...]


def body(samples, shift_bin, start_vectors, tap_table):
    vmem = pl.BlockSpec(memory_space=pltpu.VMEM)
    smem = pl.BlockSpec(memory_space=pltpu.SMEM)
    hbm = pl.BlockSpec(memory_space=pl.ANY)
    dma = pltpu.SemaphoreType.DMA
    scratch = [
        ((2, BEAMS, OWN), jnp.int32),
        ((TAPS, CHANNELS), jnp.int32),
        ((CHUNKS, 2, ELEMS, CHUNK), F32),
        ((ELEMS, 2 * BEAMS), F32),
        ((2, 8, CHUNK), F32),
        ((CHUNKS, ELEMS, 2 * CHUNK), BF16),
        ((CHUNKS, ELEMS, 2 * CHUNK), BF16),
        ((CHUNKS, ELEMS, 2 * CHUNK), BF16),
        ((CHUNKS, ELEMS, 2 * CHUNK), BF16),
        ((2, 8, 3, BLOCK, BLOCK), F32),
        ((2, 8, 3, BLOCK, BLOCK), F32),
        ((8, 3, BLOCK, BLOCK), F32),
        ((4, 4, 2, 3, 32, BLOCK), F32),
        ((4, 4, 2, 3, 8, BLOCK), F32),
        ((8, 3, 8, BLOCK), F32),
        ((ELEMS, 2 * BEAMS), F32),
        ((ELEMS, 4 * ELEMS), BF16),
        ((ELEMS, 4 * ELEMS), BF16),
        ((ELEMS, 2 * ELEMS), BF16),
        ((ELEMS, 2 * ELEMS), BF16),
        ((4, CHANNELS, CHANNELS), BF16),
        ((2, FRAMES, BEAMS, PART), F32),
        ((2, FRAMES, BEAMS, PART), F32),
        ((2, FRAMES, BEAMS, PART), F32),
        ((GROUP, 2, FRAMES, QUARTER, PART), F32),
        ((GROUP, 2, FRAMES, QUARTER, PART), F32),
    ]
    semaphores = [
        (2 * CHUNKS, GROUP), (2 * CHUNKS, GROUP), (2 * CHUNKS,), (8,), (8,), None, (2,),
        (4,), (4,), (32,), (32,), (8,), (8,), (8,), (8,), (32,), (32,),
        (16,), (16,), (GROUP,), (GROUP,), (GROUP,), (GROUP,), (GROUP,), (GROUP,),
    ]
    spectra, weights = pl.pallas_call(
        kernel,
        out_shape=(
            jax.ShapeDtypeStruct((2, FRAMES * QUARTER, CHANNELS), F32),
            jax.ShapeDtypeStruct((2, BEAMS, OWN), F32),
        ),
        in_specs=[hbm, hbm, smem, hbm, hbm],
        out_specs=(vmem, vmem),
        scratch_shapes=[pltpu.VMEM(*entry) for entry in scratch]
        + [dma if shape is None else dma(shape) for shape in semaphores],
        compiler_params=pltpu.CompilerParams(
            collective_id=0, has_side_effects=True, vmem_limit_bytes=VMEM_LIMIT),
        name="beamformer",
    )(samples, start_vectors.transpose(0, 2, 1), shift_bin, tap_table, jnp.asarray(dft_tables()))
    spectra, weights = pl.pallas_call(
        finish_kernel,
        out_shape=(
            jax.ShapeDtypeStruct((2, FRAMES * QUARTER, CHANNELS), F32),
            jax.ShapeDtypeStruct((2, BEAMS, OWN), F32),
        ),
        in_specs=[vmem, vmem],
        out_specs=(vmem, vmem),
        name="finish",
    )(spectra, weights)
    spectra = spectra.reshape(2, FRAMES, QUARTER, CHANNELS).transpose(0, 2, 1, 3)
    return (spectra, weights.transpose(0, 2, 1))


def solution(mesh):
    return jax.shard_map(
        body,
        mesh=mesh,
        in_specs=(P(None, "elem", "tm"), P(), P(None, "elem", None), P()),
        out_specs=(P(None, "elem", "tm", None), P(None, "elem", None)),
        check_vma=False,
    )
```

```python
import math

import jax
import jax.numpy as jnp
import ml_dtypes
import numpy as np
from jax import lax
from jax.experimental import pallas as pl
from jax.experimental.pallas import tpu as pltpu
from jax.sharding import PartitionSpec as P

ELEMS = 512
BEAMS = 64
CHANNELS = 1024
TAPS = 4
ITERS = 3
SPAN = 3072
SAMPLES = 196608
FRAMES = SPAN // CHANNELS
GROUP = 4
OWN = ELEMS // GROUP
PART = CHANNELS // GROUP
TM = SAMPLES // SPAN
QUARTER = BEAMS // GROUP

EPS = 1e-06
F32 = jnp.float32
BF16 = jnp.bfloat16
MESH = pl.DeviceIdType.MESH
VMEM_LIMIT = 46 * 1024 * 1024

CHUNK = 128
EARLY = 96
LATE = OWN - EARLY
CHUNKS = SPAN // GROUP // CHUNK
BLOCK = 128
SIZES = {"core": 2, "x": 4, "y": 4, "z": 8}
PLANE = (("x", "y"), ("y", "x"))
SLOTS = (
    ((0, 0), (0, 2), (1, 1), (1, 3), (2, 0), (2, 2), (3, 1), (3, 3)),
    ((0, 1), (1, 0), (0, 3), (3, 0), (1, 2), (2, 1), (2, 3), (3, 2)),
)
SLOT_OF = {block: (parity, slot) for parity in range(2) for slot, block in enumerate(SLOTS[parity])}


def split(value):
    high = value.astype(BF16)
    return high, (value - high.astype(F32)).astype(BF16)


def dot_nt(left, right):
    return lax.dot_general(left, right, (((1,), (1,)), ((), ())), preferred_element_type=F32)


def dot_nn(left, right):
    return lax.dot_general(left, right, (((1,), (0,)), ((), ())), preferred_element_type=F32)


def cat(*pieces):
    return jnp.concatenate(pieces, axis=1)


def dft_tables():
    ids = np.arange(CHANNELS)
    angle = 2.0 * np.pi / CHANNELS * (ids[:, None] * ids[None, :] % CHANNELS)
    out = []
    for table in (np.cos(angle), np.sin(angle)):
        table = (table / math.sqrt(CHANNELS)).astype(np.float32)
        high = table.astype(ml_dtypes.bfloat16)
        out += [high, (table - high.astype(np.float32)).astype(ml_dtypes.bfloat16)]
    return np.stack(out)


def place():
    tm = lax.axis_index("tm")
    return {
        "core": lax.rem(tm, 2),
        "x": lax.rem(tm // 2, 4),
        "y": tm // 16,
        "z": lax.rem(tm // 8, 2) * 4 + lax.axis_index("elem"),
    }


def device_at(spot, axis, value):
    at = dict(spot)
    at[axis] = value
    tm = ((at["y"] * 2 + at["z"] // 4) * 4 + at["x"]) * 2 + at["core"]
    return {"tm": tm, "elem": lax.rem(at["z"], 4)}


def aligned(start, size):
    return pl.ds(pl.multiple_of(start, size), size)


def kernel(x_ref, start_hbm, shift_ref, tap_hbm, table_ref, out_ref, weights_ref,
           start_ref, tap_ref, xg, sg, phase, rh, rl, uh, ul, g, o, pair_got, first_got, second_got, z_got, v_ref, ah, al, bh, bl,
           table, own, after, halo, got, crossed,
           send_sem, recv_sem, own_sem, s_send, s_recv, table_sem, input_sem,
           pair_send, pair_recv, rs_send, rs_recv, z_send, z_recv, az_send, az_recv, ag_send, ag_recv,
           fw_send, fw_recv, halo_send, halo_recv, cross_send, cross_recv, last_send, last_recv):
    tm = lax.axis_index("tm")
    me = lax.axis_index("elem")
    spot = place()
    core = spot["core"]

    table_copy = pltpu.make_async_copy(table_ref, table, table_sem)
    start_fetch = pltpu.make_async_copy(start_hbm, start_ref, input_sem.at[0])
    tap_fetch = pltpu.make_async_copy(tap_hbm, tap_ref, input_sem.at[1])
    start_fetch.start()
    tap_fetch.start()

    barrier = pltpu.get_barrier_semaphore()
    count = 0
    for axis, size in SIZES.items():
        for off in range(1, size):
            pl.semaphore_signal(
                barrier, inc=1, device_id=device_at(spot, axis, lax.rem(spot[axis] + off, size)),
                device_id_type=MESH)
            count += 1
    turn = lax.rem(tm, 8)
    near_out = turn != 7
    near_in = turn != 0
    cross_out = jnp.logical_and(turn == 7, tm < TM - 1)
    cross_in = jnp.logical_and(turn == 0, tm > 0)

    @pl.when(near_out)
    def _():
        pl.semaphore_signal(barrier, inc=1, device_id={"tm": tm + 1, "elem": me}, device_id_type=MESH)

    @pl.when(near_in)
    def _():
        pl.semaphore_signal(barrier, inc=1, device_id={"tm": tm - 1, "elem": me}, device_id_type=MESH)

    @pl.when(cross_out)
    def _():
        for peer in range(GROUP):
            pl.semaphore_signal(barrier, inc=1, device_id={"tm": tm + 1, "elem": peer}, device_id_type=MESH)

    @pl.when(cross_in)
    def _():
        for peer in range(GROUP):
            pl.semaphore_signal(barrier, inc=1, device_id={"tm": tm - 1, "elem": peer}, device_id_type=MESH)

    number = lambda flag: flag.astype(jnp.int32)
    pl.semaphore_wait(
        barrier, count + number(near_out) + number(near_in) + GROUP * (number(cross_out) + number(cross_in)))

    firsts = (0, EARLY)
    counts = (EARLY, LATE)

    def virtual(group):
        return aligned(me * EARLY, EARLY) if group == 0 else aligned(GROUP * EARLY + me * LATE, LATE)

    def start_copy(group, off):
        where = sg.at[virtual(group), :]
        return pltpu.make_async_remote_copy(
            src_ref=where, dst_ref=where,
            send_sem=s_send.at[group * 4 + off], recv_sem=s_recv.at[group * 4 + off],
            device_id={"elem": lax.rem(me + off, GROUP)}, device_id_type=MESH)

    def columns(chunk, peer):
        return aligned(chunk // 2 * CHANNELS + peer * PART + lax.rem(chunk, 2) * CHUNK, CHUNK)

    def sample_copy(group, chunk, off):
        peer = lax.rem(me + off, GROUP)
        return pltpu.make_async_remote_copy(
            src_ref=x_ref.at[:, pl.ds(firsts[group], counts[group]), columns(chunk, peer)],
            dst_ref=xg.at[chunk, :, virtual(group), :],
            send_sem=send_sem.at[group * CHUNKS + chunk, off], recv_sem=recv_sem.at[group * CHUNKS + chunk, off],
            device_id={"elem": peer}, device_id_type=MESH)

    def own_copy(group, chunk):
        return pltpu.make_async_copy(
            x_ref.at[:, pl.ds(firsts[group], counts[group]), columns(chunk, me)],
            xg.at[chunk, :, virtual(group), :], own_sem.at[group * CHUNKS + chunk])

    def send_group(group):
        for chunk in range(CHUNKS):
            for off in (2, 1, 3):
                sample_copy(group, chunk, off).start()
            own_copy(group, chunk).start()

    send_group(0)
    send_group(1)
    table_copy.start()
    start_fetch.wait()
    starts = (start_ref[...].reshape(2 * BEAMS, OWN).astype(F32) - 4.5).T
    for group in range(2):
        sg[virtual(group), :] = starts[firsts[group]:firsts[group] + counts[group]]

    rows8 = lax.broadcasted_iota(jnp.int32, (8, CHUNK), 0)
    lanes = lax.broadcasted_iota(jnp.int32, (8, CHUNK), 1)
    times = tm * SPAN + rows8 // 2 * CHANNELS + me * PART + lax.rem(rows8, 2) * CHUNK + lanes
    turns = (times * shift_ref[0]).astype(F32)
    folded = turns - jnp.floor(turns * (1.0 / SAMPLES)) * SAMPLES
    folded = jnp.where(folded < 0.0, folded + SAMPLES, folded)
    folded = jnp.where(folded >= SAMPLES, folded - SAMPLES, folded)
    angle = 2.0 * math.pi / SAMPLES * folded
    phase[0] = jnp.cos(angle)
    phase[1] = jnp.sin(angle)
    g[...] = jnp.zeros_like(g)

    def triangle(size):
        return lax.broadcasted_iota(jnp.int32, (size, size), 0) <= lax.broadcasted_iota(jnp.int32, (size, size), 1)

    def left_of(high_ref, low_ref, chunk, rows, imag):
        high = high_ref[chunk, rows, :]
        low = low_ref[chunk, rows, :]
        if imag:
            high = cat(high[:, CHUNK:], -high[:, :CHUNK])
            low = cat(low[:, CHUNK:], -low[:, :CHUNK])
        return cat(high, high, low)

    def right_of(chunk, rows):
        high = rh[chunk, rows, :]
        return cat(high, rl[chunk, rows, :], high)

    def add_blocks(kind, first, first_col, value):
        for i in range(value.shape[0] // BLOCK):
            for j in range(value.shape[1] // BLOCK):
                parity, slot = SLOT_OF[(first + i, first_col + j)]
                g[parity, slot, kind] += value[i * BLOCK:(i + 1) * BLOCK, j * BLOCK:(j + 1) * BLOCK]

    def arrive(group, chunk):
        own_copy(group, chunk).wait()
        for off in range(1, GROUP):
            sample_copy(group, chunk, off).wait_recv()
        cos_row = phase[0, pl.ds(chunk, 1), :]
        sin_row = phase[1, pl.ds(chunk, 1), :]
        for block in ((0, 1, 2), (3,))[group]:
            rows = pl.ds(block * BLOCK, BLOCK)
            real = xg[chunk, 0, rows, :]
            imag = xg[chunk, 1, rows, :]
            rh[chunk, rows, :], rl[chunk, rows, :] = split(cat(real, imag))
            uh[chunk, rows, :], ul[chunk, rows, :] = split(
                cat(real * cos_row + imag * sin_row, imag * cos_row - real * sin_row))

    front = pl.ds(0, 3 * BLOCK)
    back = pl.ds(3 * BLOCK, BLOCK)

    def early_chunk(chunk, carry):
        arrive(0, chunk)
        right = right_of(chunk, front)
        for imag in (0, 1):
            add_blocks(1 + imag, 0, 0, dot_nt(left_of(uh, ul, chunk, front, imag), right))
        add_blocks(0, 0, 0, jnp.where(
            triangle(3 * BLOCK), dot_nt(left_of(rh, rl, chunk, front, 0), right),
            dot_nt(left_of(rh, rl, chunk, front, 1), right)))
        return carry

    def late_chunk(chunk, carry):
        arrive(1, chunk)
        right = right_of(chunk, pl.ds(0, ELEMS))
        last = right_of(chunk, back)
        for imag in (0, 1):
            add_blocks(1 + imag, 3, 0, dot_nt(left_of(uh, ul, chunk, back, imag), right))
            add_blocks(1 + imag, 0, 3, dot_nt(left_of(uh, ul, chunk, front, imag), last))
        add_blocks(0, 0, 3, dot_nt(left_of(rh, rl, chunk, front, 0), last))
        low = dot_nt(left_of(rh, rl, chunk, back, 1), right)
        add_blocks(0, 3, 0, low[:, :3 * BLOCK])
        add_blocks(0, 3, 3, jnp.where(
            triangle(BLOCK), dot_nt(left_of(rh, rl, chunk, back, 0), last), low[:, 3 * BLOCK:]))
        return carry

    sibling = device_at(spot, "core", 1 - core)

    def slots_of(group, part):
        return pl.ds(part * 4 + group * 2, 2)

    def pair_copy(group, part):
        return pltpu.make_async_remote_copy(
            src_ref=g.at[1 - core, slots_of(group, part)], dst_ref=pair_got.at[slots_of(group, part)],
            send_sem=pair_send.at[group * 2 + part], recv_sem=pair_recv.at[group * 2 + part],
            device_id=sibling, device_id_type=MESH)

    def piece(part, stage, first, second):
        if stage == 0:
            return aligned(first * 32, 32)
        return aligned(first * 32 + second * 8, 8)

    def rs_copy(group, part, stage, off):
        axis = PLANE[part][stage]
        peer = lax.rem(spot[axis] + off, 4)
        rows = piece(part, 0, peer, 0) if stage == 0 else piece(part, 1, spot[PLANE[part][0]], peer)
        index = group * 16 + part * 8 + stage * 4 + off
        return pltpu.make_async_remote_copy(
            src_ref=g.at[core, slots_of(group, part), :, rows, :],
            dst_ref=(first_got if stage == 0 else second_got).at[group * 2 + part, off],
            send_sem=rs_send.at[index], recv_sem=rs_recv.at[index],
            device_id=device_at(spot, axis, peer), device_id_type=MESH)

    def rows_of(z):
        part = z // 4
        plane = (spot["x"] * 32 + spot["y"] * 8) * (1 - part) + (spot["y"] * 32 + spot["x"] * 8) * part
        return aligned(plane, 8)

    def z_copy(off):
        peer = lax.rem(spot["z"] + off, 8)
        return pltpu.make_async_remote_copy(
            src_ref=g.at[core, peer, :, rows_of(peer), :], dst_ref=z_got.at[off],
            send_sem=z_send.at[off], recv_sem=z_recv.at[off],
            device_id=device_at(spot, "z", peer), device_id_type=MESH)

    def az_copy(off):
        mine = spot["z"]
        where = o.at[core, mine, :, rows_of(mine), :]
        return pltpu.make_async_remote_copy(
            src_ref=where, dst_ref=where, send_sem=az_send.at[off], recv_sem=az_recv.at[off],
            device_id=device_at(spot, "z", lax.rem(mine + off, 8)), device_id_type=MESH)

    def ag_copy(group, part, stage, off):
        axis = PLANE[part][stage]
        peer = lax.rem(spot[axis] + off, 4)
        rows = piece(part, stage, spot[PLANE[part][0]], spot[PLANE[part][1]])
        where = o.at[core, slots_of(group, part), :, rows, :]
        index = group * 16 + part * 8 + stage * 4 + off
        return pltpu.make_async_remote_copy(
            src_ref=where, dst_ref=where, send_sem=ag_send.at[index], recv_sem=ag_recv.at[index],
            device_id=device_at(spot, axis, peer), device_id_type=MESH)

    def forward_copy(group, part, off):
        origin = lax.rem(spot[PLANE[part][0]] + 4 - off, 4)
        where = o.at[core, slots_of(group, part), :, aligned(origin * 32, 32), :]
        index = group * 8 + part * 4 + off
        return pltpu.make_async_remote_copy(
            src_ref=where, dst_ref=where, send_sem=fw_send.at[index], recv_sem=fw_recv.at[index],
            device_id=sibling, device_id_type=MESH)

    def pair_send_out(group):
        for part in range(2):
            pair_copy(group, part).start()

    def pair_add(group):
        for part in range(2):
            pair_copy(group, part).wait_recv()
            for slot in range(part * 4 + group * 2, part * 4 + group * 2 + 2):
                g[core, slot] += pair_got[slot]
            for off in (2, 1, 3):
                rs_copy(group, part, 0, off).start()

    def plane_add(group, stage):
        got_ref = first_got if stage == 0 else second_got
        for part in range(2):
            for off in (1, 3, 2):
                rs_copy(group, part, stage, off).wait_recv()
            rows = piece(part, stage, spot[PLANE[part][0]], spot[PLANE[part][1]])
            which = group * 2 + part
            g[core, slots_of(group, part), :, rows, :] += got_ref[which, 1] + got_ref[which, 2] + got_ref[which, 3]
            if stage == 0:
                for off in (2, 1, 3):
                    rs_copy(group, part, 1, off).start()

    z_order = (4, 3, 5, 2, 6, 1, 7)
    mine = spot["z"]

    def group_of(z):
        return lax.rem(z // 2, 2)

    def z_start(group):
        for off in z_order:
            @pl.when(group_of(lax.rem(mine + off, 8)) == group)
            def _():
                z_copy(off).start()

    def z_sum(group):
        @pl.when(group_of(mine) == group)
        def _():
            for off in range(1, 8):
                z_copy(off).wait_recv()
            total = g[core, mine, :, rows_of(mine), :]
            for off in range(1, 8):
                total = total + z_got[off]
            o[core, mine, :, rows_of(mine), :] = total
            for off in z_order:
                az_copy(off).start()

    def z_gather(group):
        for off in range(1, 8):
            @pl.when(group_of(lax.rem(mine + 8 - off, 8)) == group)
            def _():
                az_copy(off).wait_recv()
        for part in range(2):
            for off in (2, 1, 3):
                ag_copy(group, part, 1, off).start()

    def ag_middle(group):
        for part in range(2):
            for off in (1, 3, 2):
                ag_copy(group, part, 1, off).wait_recv()
            for off in (2, 1, 3):
                ag_copy(group, part, 0, off).start()
            forward_copy(group, part, 0).start()

    def ag_last(group):
        for off in (1, 3, 2):
            for part in range(2):
                ag_copy(group, part, 0, off).wait_recv()
                forward_copy(group, part, off).start()

    def ag_done(group):
        for part in range(2):
            for off in range(4):
                forward_copy(group, part, off).wait_recv()

    plain_scale = 1.0 / SAMPLES
    cyc_scale = 1.0 / math.sqrt(SAMPLES * ELEMS)

    def put(high_ref, low_ref, row, kind, col, value):
        rows = pl.ds(row * BLOCK, BLOCK)
        cols = pl.ds(kind * ELEMS + col * BLOCK, BLOCK)
        high_ref[rows, cols], low_ref[rows, cols] = split(value)

    def prepare(group):
        for parity in range(2):
            for slot in range(8):
                if slot // 2 % 2 != group:
                    continue
                i, j = SLOTS[parity][slot]
                for imag in (0, 1):
                    block = o[parity, slot, 1 + imag] * cyc_scale
                    put(ah, al, i, imag, j, block)
                    put(bh, bl, j, imag, i, -block.T if imag else block.T)
                block = o[parity, slot, 0] * plain_scale
                turned_block = block.T
                if i < j:
                    put(ah, al, i, 2, j, block)
                    put(ah, al, j, 2, i, turned_block)
                elif i > j:
                    put(ah, al, i, 3, j, block)
                    put(ah, al, j, 3, i, -turned_block)
                else:
                    row_ids = lax.broadcasted_iota(jnp.int32, (BLOCK, BLOCK), 0)
                    col_ids = lax.broadcasted_iota(jnp.int32, (BLOCK, BLOCK), 1)
                    put(ah, al, i, 2, i, jnp.where(row_ids <= col_ids, block, turned_block))
                    put(ah, al, i, 3, i, jnp.where(
                        row_ids > col_ids, block, jnp.where(row_ids < col_ids, -turned_block, 0.0)))

    lax.fori_loop(0, CHUNKS, early_chunk, 0)
    pair_send_out(0)
    late_chunk(0, 0)
    pair_add(0)
    lax.fori_loop(1, 4, late_chunk, 0)
    plane_add(0, 0)
    lax.fori_loop(4, CHUNKS, late_chunk, 0)
    pair_send_out(1)
    plane_add(0, 1)
    z_start(0)
    for group in range(2):
        for off in range(1, GROUP):
            start_copy(group, off).start()
    pair_add(1)
    z_sum(0)
    plane_add(1, 0)
    plane_add(1, 1)
    z_start(1)
    z_gather(0)
    ag_middle(0)
    z_sum(1)
    ag_last(0)
    z_gather(1)
    ag_done(0)
    ag_middle(1)
    prepare(0)
    for off in range(1, GROUP):
        for group in range(2):
            start_copy(group, off).wait_recv()
    ag_last(1)
    ag_done(1)
    prepare(1)

    lane = lax.broadcasted_iota(jnp.int32, (ELEMS, 2 * BEAMS), 1)

    def turned(vector):
        other = pltpu.roll(vector, BEAMS, 1)
        return jnp.where(lane < BEAMS, -other, other)

    def normalized(vector):
        squares = jnp.sum(vector * vector, axis=0, keepdims=True)
        squares = jnp.broadcast_to(squares, (8, 2 * BEAMS))
        squares = squares + pltpu.roll(squares, BEAMS, 1)
        return vector * (1.0 / jnp.sqrt(squares[:1] + EPS))

    def stacked(vector):
        high, low = split(jnp.concatenate([vector, turned(vector)], axis=0))
        return cat(high, low)

    def product(high, low, right):
        wide_out = dot_nn(high, right)
        return wide_out[:, :2 * BEAMS] + wide_out[:, 2 * BEAMS:] + dot_nn(low, right[:, :2 * BEAMS])

    v_ref[...] = normalized(sg[...])

    def step(iteration, carry):
        held = stacked(v_ref[...])
        mid = product(bh[...], bl[...], held)
        v_ref[...] = normalized(product(ah[...], al[...], jnp.concatenate([stacked(mid), held], axis=0)))
        return carry

    lax.fori_loop(0, ITERS, step, 0)
    mine = jnp.concatenate([v_ref[virtual(0), :], v_ref[virtual(1), :]], axis=0)
    weights_ref[...] = mine.T.reshape(2, BEAMS, OWN)

    vh, vl = split(v_ref[...].T)
    left = jnp.concatenate([vh, vl], axis=0)
    tap_fetch.wait()
    taps = tap_ref[:, aligned(me * PART, PART)].astype(F32) / 2048.0
    beams = ([], [])
    for frame in range(FRAMES):
        xh = cat(rh[frame * 2], rh[frame * 2 + 1])
        xl = cat(rl[frame * 2], rl[frame * 2 + 1])
        both = dot_nn(left, xh)
        out = both[:2 * BEAMS] + both[2 * BEAMS:] + dot_nn(vh, xl)
        top, low = out[:BEAMS], out[BEAMS:]
        beams[0].append(cat(*[top[:, c:c + CHUNK] + low[:, c + CHUNK:c + 2 * CHUNK] for c in (0, 2 * CHUNK)]))
        beams[1].append(cat(*[top[:, c + CHUNK:c + 2 * CHUNK] - low[:, c:c + CHUNK] for c in (0, 2 * CHUNK)]))

    def filtered(kind, frame):
        total = None
        for tap in range(TAPS):
            if 0 <= frame - tap < FRAMES:
                term = taps[tap:tap + 1, :] * beams[kind][frame - tap]
                total = term if total is None else total + term
        return total

    for kind in range(2):
        for frame in range(FRAMES):
            after[kind, frame] = filtered(kind, frame + FRAMES)

    def quarter(off):
        return aligned(lax.rem(me + off, GROUP) * QUARTER, QUARTER)

    def halo_copy(off):
        rows = quarter(off)
        return pltpu.make_async_remote_copy(
            src_ref=after.at[:, :, rows, :], dst_ref=halo.at[:, :, rows, :],
            send_sem=halo_send.at[off], recv_sem=halo_recv.at[off],
            device_id={"tm": tm + 1, "elem": me}, device_id_type=MESH)

    def cross_copy(off):
        return pltpu.make_async_remote_copy(
            src_ref=after.at[:, :, quarter(off), :], dst_ref=crossed.at[off],
            send_sem=cross_send.at[off], recv_sem=cross_recv.at[off],
            device_id={"tm": tm + 1, "elem": lax.rem(me + off, GROUP)}, device_id_type=MESH)

    def last_copy(off):
        return pltpu.make_async_remote_copy(
            src_ref=own.at[:, :, quarter(off), :], dst_ref=got.at[off],
            send_sem=last_send.at[off], recv_sem=last_recv.at[off],
            device_id={"elem": lax.rem(me + off, GROUP)}, device_id_type=MESH)

    order = (2, 1, 3, 0)

    @pl.when(near_out)
    def _():
        for off in order:
            halo_copy(off).start()

    @pl.when(cross_out)
    def _():
        for off in order:
            cross_copy(off).start()

    for kind in range(2):
        for frame in range(FRAMES):
            own[kind, frame] = filtered(kind, frame)

    for off in order:
        @pl.when(near_in)
        def _():
            halo_copy(off).wait_recv()
            rows = quarter(off)
            own[:, :, rows, :] += halo[:, :, rows, :]

        if off:
            last_copy(off).start()
        else:
            got[0] = own[:, :, quarter(0), :]

    table_copy.wait()
    rows = 2 * FRAMES * QUARTER
    half = FRAMES * QUARTER
    for position, off in enumerate((0, 1, 3, 2)):
        if off:
            last_copy(off).wait_recv()

        @pl.when(cross_in)
        def _():
            cross_copy(off).wait_recv()
            got[off] += crossed[off]

        high, low = split(got[off].reshape(rows, PART))
        left = jnp.concatenate([high, low], axis=0)
        where = aligned(lax.rem(me + GROUP - off, GROUP) * PART, PART)

        def times_table(index):
            both = dot_nn(left, table[index, where, :])
            return both[:rows] + both[rows:] + dot_nn(high, table[index + 1, where, :])

        with_cos = times_table(0)
        with_sin = times_table(2)
        real = with_cos[:half] + with_sin[half:]
        imag = with_cos[half:] - with_sin[:half]
        if position == 0:
            out_ref[0] = real
            out_ref[1] = imag
        else:
            out_ref[0] += real
            out_ref[1] += imag

    for off in range(1, GROUP):
        last_copy(off).wait_send()
        for group in range(2):
            start_copy(group, off).wait_send()
            for chunk in range(CHUNKS):
                sample_copy(group, chunk, off).wait_send()
        for part in range(2):
            for stage in range(2):
                for group in range(2):
                    rs_copy(group, part, stage, off).wait_send()
                    ag_copy(group, part, stage, off).wait_send()
    for off in range(1, 8):
        z_copy(off).wait_send()
        az_copy(off).wait_send()
    for part in range(2):
        for group in range(2):
            pair_copy(group, part).wait_send()
        for off in range(4):
            for group in range(2):
                forward_copy(group, part, off).wait_send()

    @pl.when(near_out)
    def _():
        for off in order:
            halo_copy(off).wait_send()

    @pl.when(cross_out)
    def _():
        for off in order:
            cross_copy(off).wait_send()


def finish_kernel(spectra_ref, weights_ref, spectra_out, weights_out):
    spectra_out[...] = spectra_ref[...]
    weights_out[...] = weights_ref[...]


def body(samples, shift_bin, start_vectors, tap_table):
    vmem = pl.BlockSpec(memory_space=pltpu.VMEM)
    smem = pl.BlockSpec(memory_space=pltpu.SMEM)
    hbm = pl.BlockSpec(memory_space=pl.ANY)
    dma = pltpu.SemaphoreType.DMA
    scratch = [
        ((2, BEAMS, OWN), jnp.int32),
        ((TAPS, CHANNELS), jnp.int32),
        ((CHUNKS, 2, ELEMS, CHUNK), F32),
        ((ELEMS, 2 * BEAMS), F32),
        ((2, 8, CHUNK), F32),
        ((CHUNKS, ELEMS, 2 * CHUNK), BF16),
        ((CHUNKS, ELEMS, 2 * CHUNK), BF16),
        ((CHUNKS, ELEMS, 2 * CHUNK), BF16),
        ((CHUNKS, ELEMS, 2 * CHUNK), BF16),
        ((2, 8, 3, BLOCK, BLOCK), F32),
        ((2, 8, 3, BLOCK, BLOCK), F32),
        ((8, 3, BLOCK, BLOCK), F32),
        ((4, 4, 2, 3, 32, BLOCK), F32),
        ((4, 4, 2, 3, 8, BLOCK), F32),
        ((8, 3, 8, BLOCK), F32),
        ((ELEMS, 2 * BEAMS), F32),
        ((ELEMS, 4 * ELEMS), BF16),
        ((ELEMS, 4 * ELEMS), BF16),
        ((ELEMS, 2 * ELEMS), BF16),
        ((ELEMS, 2 * ELEMS), BF16),
        ((4, CHANNELS, CHANNELS), BF16),
        ((2, FRAMES, BEAMS, PART), F32),
        ((2, FRAMES, BEAMS, PART), F32),
        ((2, FRAMES, BEAMS, PART), F32),
        ((GROUP, 2, FRAMES, QUARTER, PART), F32),
        ((GROUP, 2, FRAMES, QUARTER, PART), F32),
    ]
    semaphores = [
        (2 * CHUNKS, GROUP), (2 * CHUNKS, GROUP), (2 * CHUNKS,), (8,), (8,), None, (2,),
        (4,), (4,), (32,), (32,), (8,), (8,), (8,), (8,), (32,), (32,),
        (16,), (16,), (GROUP,), (GROUP,), (GROUP,), (GROUP,), (GROUP,), (GROUP,),
    ]
    spectra, weights = pl.pallas_call(
        kernel,
        out_shape=(
            jax.ShapeDtypeStruct((2, FRAMES * QUARTER, CHANNELS), F32),
            jax.ShapeDtypeStruct((2, BEAMS, OWN), F32),
        ),
        in_specs=[hbm, hbm, smem, hbm, hbm],
        out_specs=(vmem, vmem),
        scratch_shapes=[pltpu.VMEM(*entry) for entry in scratch]
        + [dma if shape is None else dma(shape) for shape in semaphores],
        compiler_params=pltpu.CompilerParams(
            collective_id=0, has_side_effects=True, vmem_limit_bytes=VMEM_LIMIT),
        name="beamformer",
    )(samples, start_vectors.transpose(0, 2, 1), shift_bin, tap_table, jnp.asarray(dft_tables()))
    spectra, weights = pl.pallas_call(
        finish_kernel,
        out_shape=(
            jax.ShapeDtypeStruct((2, FRAMES * QUARTER, CHANNELS), F32),
            jax.ShapeDtypeStruct((2, BEAMS, OWN), F32),
        ),
        in_specs=[vmem, vmem],
        out_specs=(vmem, vmem),
        compiler_params=pltpu.CompilerParams(vmem_limit_bytes=4 * 1024 * 1024),
        name="finish",
    )(spectra, weights)
    spectra = spectra.reshape(2, FRAMES, QUARTER, CHANNELS).transpose(0, 2, 1, 3)
    return (spectra, weights.transpose(0, 2, 1))


def solution(mesh):
    return jax.shard_map(
        body,
        mesh=mesh,
        in_specs=(P(None, "elem", "tm"), P(), P(None, "elem", None), P()),
        out_specs=(P(None, "elem", "tm", None), P(None, "elem", None)),
        check_vma=False,
    )
```

```python
import math

import jax
import jax.numpy as jnp
import ml_dtypes
import numpy as np
from jax import lax
from jax.experimental import pallas as pl
from jax.experimental.pallas import tpu as pltpu
from jax.sharding import PartitionSpec as P

ELEMS = 512
BEAMS = 64
CHANNELS = 1024
TAPS = 4
ITERS = 3
SPAN = 3072
SAMPLES = 196608
FRAMES = SPAN // CHANNELS
GROUP = 4
OWN = ELEMS // GROUP
PART = CHANNELS // GROUP
TM = SAMPLES // SPAN
QUARTER = BEAMS // GROUP

EPS = 1e-06
F32 = jnp.float32
BF16 = jnp.bfloat16
MESH = pl.DeviceIdType.MESH
VMEM_LIMIT = 46 * 1024 * 1024

CHUNK = 128
EARLY = 96
LATE = OWN - EARLY
CHUNKS = SPAN // GROUP // CHUNK
BLOCK = 128
SIZES = {"core": 2, "x": 4, "y": 4, "z": 8}
PLANE = (("x", "y"), ("y", "x"))
SLOTS = (
    ((0, 0), (0, 2), (1, 1), (1, 3), (2, 0), (2, 2), (3, 1), (3, 3)),
    ((0, 1), (1, 0), (0, 3), (3, 0), (1, 2), (2, 1), (2, 3), (3, 2)),
)
SLOT_OF = {block: (parity, slot) for parity in range(2) for slot, block in enumerate(SLOTS[parity])}


def split(value):
    high = value.astype(BF16)
    return high, (value - high.astype(F32)).astype(BF16)


def dot_nt(left, right):
    return lax.dot_general(left, right, (((1,), (1,)), ((), ())), preferred_element_type=F32)


def dot_nn(left, right):
    return lax.dot_general(left, right, (((1,), (0,)), ((), ())), preferred_element_type=F32)


def cat(*pieces):
    return jnp.concatenate(pieces, axis=1)


def dft_tables():
    ids = np.arange(CHANNELS)
    angle = 2.0 * np.pi / CHANNELS * (ids[:, None] * ids[None, :] % CHANNELS)
    out = []
    for table in (np.cos(angle), np.sin(angle)):
        table = (table / math.sqrt(CHANNELS)).astype(np.float32)
        high = table.astype(ml_dtypes.bfloat16)
        out += [high, (table - high.astype(np.float32)).astype(ml_dtypes.bfloat16)]
    return np.stack(out)


def place():
    tm = lax.axis_index("tm")
    return {
        "core": lax.rem(tm, 2),
        "x": lax.rem(tm // 2, 4),
        "y": tm // 16,
        "z": lax.rem(tm // 8, 2) * 4 + lax.axis_index("elem"),
    }


def device_at(spot, axis, value):
    at = dict(spot)
    at[axis] = value
    tm = ((at["y"] * 2 + at["z"] // 4) * 4 + at["x"]) * 2 + at["core"]
    return {"tm": tm, "elem": lax.rem(at["z"], 4)}


def aligned(start, size):
    return pl.ds(pl.multiple_of(start, size), size)


def kernel(x_ref, start_hbm, shift_ref, tap_hbm, table_ref, out_ref, weights_ref,
           start_ref, tap_ref, xg, sg, phase, rh, rl, uh, ul, g, o, pair_got, first_got, second_got, z_got, v_ref, ah, al, bh, bl,
           table, own, after, halo, got, crossed,
           send_sem, recv_sem, own_sem, s_send, s_recv, table_sem, input_sem,
           pair_send, pair_recv, rs_send, rs_recv, z_send, z_recv, az_send, az_recv, ag_send, ag_recv,
           fw_send, fw_recv, halo_send, halo_recv, cross_send, cross_recv, last_send, last_recv):
    tm = lax.axis_index("tm")
    me = lax.axis_index("elem")
    spot = place()
    core = spot["core"]

    table_copy = pltpu.make_async_copy(table_ref, table, table_sem)
    start_fetch = pltpu.make_async_copy(start_hbm, start_ref, input_sem.at[0])
    tap_fetch = pltpu.make_async_copy(tap_hbm, tap_ref, input_sem.at[1])
    start_fetch.start()
    tap_fetch.start()

    barrier = pltpu.get_barrier_semaphore()
    count = 0
    for axis, size in SIZES.items():
        for off in range(1, size):
            pl.semaphore_signal(
                barrier, inc=1, device_id=device_at(spot, axis, lax.rem(spot[axis] + off, size)),
                device_id_type=MESH)
            count += 1
    turn = lax.rem(tm, 8)
    near_out = turn != 7
    near_in = turn != 0
    cross_out = jnp.logical_and(turn == 7, tm < TM - 1)
    cross_in = jnp.logical_and(turn == 0, tm > 0)

    @pl.when(near_out)
    def _():
        pl.semaphore_signal(barrier, inc=1, device_id={"tm": tm + 1, "elem": me}, device_id_type=MESH)

    @pl.when(near_in)
    def _():
        pl.semaphore_signal(barrier, inc=1, device_id={"tm": tm - 1, "elem": me}, device_id_type=MESH)

    @pl.when(cross_out)
    def _():
        for peer in range(GROUP):
            pl.semaphore_signal(barrier, inc=1, device_id={"tm": tm + 1, "elem": peer}, device_id_type=MESH)

    @pl.when(cross_in)
    def _():
        for peer in range(GROUP):
            pl.semaphore_signal(barrier, inc=1, device_id={"tm": tm - 1, "elem": peer}, device_id_type=MESH)

    number = lambda flag: flag.astype(jnp.int32)
    pl.semaphore_wait(
        barrier, count + number(near_out) + number(near_in) + GROUP * (number(cross_out) + number(cross_in)))

    firsts = (0, EARLY)
    counts = (EARLY, LATE)

    def virtual(group):
        return aligned(me * EARLY, EARLY) if group == 0 else aligned(GROUP * EARLY + me * LATE, LATE)

    def start_copy(group, off):
        where = sg.at[virtual(group), :]
        return pltpu.make_async_remote_copy(
            src_ref=where, dst_ref=where,
            send_sem=s_send.at[group * 4 + off], recv_sem=s_recv.at[group * 4 + off],
            device_id={"elem": lax.rem(me + off, GROUP)}, device_id_type=MESH)

    def columns(chunk, peer):
        return aligned(chunk // 2 * CHANNELS + peer * PART + lax.rem(chunk, 2) * CHUNK, CHUNK)

    def sample_copy(group, chunk, off):
        peer = lax.rem(me + off, GROUP)
        return pltpu.make_async_remote_copy(
            src_ref=x_ref.at[:, pl.ds(firsts[group], counts[group]), columns(chunk, peer)],
            dst_ref=xg.at[chunk, :, virtual(group), :],
            send_sem=send_sem.at[group * CHUNKS + chunk, off], recv_sem=recv_sem.at[group * CHUNKS + chunk, off],
            device_id={"elem": peer}, device_id_type=MESH)

    def own_copy(group, chunk):
        return pltpu.make_async_copy(
            x_ref.at[:, pl.ds(firsts[group], counts[group]), columns(chunk, me)],
            xg.at[chunk, :, virtual(group), :], own_sem.at[group * CHUNKS + chunk])

    def send_group(group):
        for chunk in range(CHUNKS):
            for off in (2, 1, 3):
                sample_copy(group, chunk, off).start()
            own_copy(group, chunk).start()

    send_group(0)
    send_group(1)
    table_copy.start()
    start_fetch.wait()
    starts = (start_ref[...].reshape(2 * BEAMS, OWN).astype(F32) - 4.5).T
    for group in range(2):
        sg[virtual(group), :] = starts[firsts[group]:firsts[group] + counts[group]]

    rows8 = lax.broadcasted_iota(jnp.int32, (8, CHUNK), 0)
    lanes = lax.broadcasted_iota(jnp.int32, (8, CHUNK), 1)
    times = tm * SPAN + rows8 // 2 * CHANNELS + me * PART + lax.rem(rows8, 2) * CHUNK + lanes
    turns = (times * shift_ref[0]).astype(F32)
    folded = turns - jnp.floor(turns * (1.0 / SAMPLES)) * SAMPLES
    folded = jnp.where(folded < 0.0, folded + SAMPLES, folded)
    folded = jnp.where(folded >= SAMPLES, folded - SAMPLES, folded)
    angle = 2.0 * math.pi / SAMPLES * folded
    phase[0] = jnp.cos(angle)
    phase[1] = jnp.sin(angle)
    g[...] = jnp.zeros_like(g)

    def triangle(size):
        return lax.broadcasted_iota(jnp.int32, (size, size), 0) <= lax.broadcasted_iota(jnp.int32, (size, size), 1)

    def left_of(high_ref, low_ref, chunk, rows, imag):
        high = high_ref[chunk, rows, :]
        low = low_ref[chunk, rows, :]
        if imag:
            high = cat(high[:, CHUNK:], -high[:, :CHUNK])
            low = cat(low[:, CHUNK:], -low[:, :CHUNK])
        return cat(high, high, low)

    def right_of(chunk, rows):
        high = rh[chunk, rows, :]
        return cat(high, rl[chunk, rows, :], high)

    def add_blocks(kind, first, first_col, value):
        for i in range(value.shape[0] // BLOCK):
            for j in range(value.shape[1] // BLOCK):
                parity, slot = SLOT_OF[(first + i, first_col + j)]
                g[parity, slot, kind] += value[i * BLOCK:(i + 1) * BLOCK, j * BLOCK:(j + 1) * BLOCK]

    def arrive(group, chunk):
        own_copy(group, chunk).wait()
        for off in range(1, GROUP):
            sample_copy(group, chunk, off).wait_recv()
        cos_row = phase[0, pl.ds(chunk, 1), :]
        sin_row = phase[1, pl.ds(chunk, 1), :]
        for block in ((0, 1, 2), (3,))[group]:
            rows = pl.ds(block * BLOCK, BLOCK)
            real = xg[chunk, 0, rows, :]
            imag = xg[chunk, 1, rows, :]
            rh[chunk, rows, :], rl[chunk, rows, :] = split(cat(real, imag))
            uh[chunk, rows, :], ul[chunk, rows, :] = split(
                cat(real * cos_row + imag * sin_row, imag * cos_row - real * sin_row))

    front = pl.ds(0, 3 * BLOCK)
    back = pl.ds(3 * BLOCK, BLOCK)

    def early_chunk(chunk, carry):
        arrive(0, chunk)
        right = right_of(chunk, front)
        for imag in (0, 1):
            add_blocks(1 + imag, 0, 0, dot_nt(left_of(uh, ul, chunk, front, imag), right))
        add_blocks(0, 0, 0, jnp.where(
            triangle(3 * BLOCK), dot_nt(left_of(rh, rl, chunk, front, 0), right),
            dot_nt(left_of(rh, rl, chunk, front, 1), right)))
        return carry

    def late_chunk(chunk, carry):
        arrive(1, chunk)
        right = right_of(chunk, pl.ds(0, ELEMS))
        last = right_of(chunk, back)
        for imag in (0, 1):
            add_blocks(1 + imag, 3, 0, dot_nt(left_of(uh, ul, chunk, back, imag), right))
            add_blocks(1 + imag, 0, 3, dot_nt(left_of(uh, ul, chunk, front, imag), last))
        add_blocks(0, 0, 3, dot_nt(left_of(rh, rl, chunk, front, 0), last))
        low = dot_nt(left_of(rh, rl, chunk, back, 1), right)
        add_blocks(0, 3, 0, low[:, :3 * BLOCK])
        add_blocks(0, 3, 3, jnp.where(
            triangle(BLOCK), dot_nt(left_of(rh, rl, chunk, back, 0), last), low[:, 3 * BLOCK:]))
        return carry

    sibling = device_at(spot, "core", 1 - core)

    def slots_of(group, part):
        return pl.ds(part * 4 + group * 2, 2)

    def pair_copy(group, part):
        return pltpu.make_async_remote_copy(
            src_ref=g.at[1 - core, slots_of(group, part)], dst_ref=pair_got.at[slots_of(group, part)],
            send_sem=pair_send.at[group * 2 + part], recv_sem=pair_recv.at[group * 2 + part],
            device_id=sibling, device_id_type=MESH)

    def piece(part, stage, first, second):
        if stage == 0:
            return aligned(first * 32, 32)
        return aligned(first * 32 + second * 8, 8)

    def rs_copy(group, part, stage, off):
        axis = PLANE[part][stage]
        peer = lax.rem(spot[axis] + off, 4)
        rows = piece(part, 0, peer, 0) if stage == 0 else piece(part, 1, spot[PLANE[part][0]], peer)
        index = group * 16 + part * 8 + stage * 4 + off
        return pltpu.make_async_remote_copy(
            src_ref=g.at[core, slots_of(group, part), :, rows, :],
            dst_ref=(first_got if stage == 0 else second_got).at[group * 2 + part, off],
            send_sem=rs_send.at[index], recv_sem=rs_recv.at[index],
            device_id=device_at(spot, axis, peer), device_id_type=MESH)

    def rows_of(z):
        part = z // 4
        plane = (spot["x"] * 32 + spot["y"] * 8) * (1 - part) + (spot["y"] * 32 + spot["x"] * 8) * part
        return aligned(plane, 8)

    def z_copy(off):
        peer = lax.rem(spot["z"] + off, 8)
        return pltpu.make_async_remote_copy(
            src_ref=g.at[core, peer, :, rows_of(peer), :], dst_ref=z_got.at[off],
            send_sem=z_send.at[off], recv_sem=z_recv.at[off],
            device_id=device_at(spot, "z", peer), device_id_type=MESH)

    def az_copy(off):
        mine = spot["z"]
        where = o.at[core, mine, :, rows_of(mine), :]
        return pltpu.make_async_remote_copy(
            src_ref=where, dst_ref=where, send_sem=az_send.at[off], recv_sem=az_recv.at[off],
            device_id=device_at(spot, "z", lax.rem(mine + off, 8)), device_id_type=MESH)

    def ag_copy(group, part, stage, off):
        axis = PLANE[part][stage]
        peer = lax.rem(spot[axis] + off, 4)
        rows = piece(part, stage, spot[PLANE[part][0]], spot[PLANE[part][1]])
        where = o.at[core, slots_of(group, part), :, rows, :]
        index = group * 16 + part * 8 + stage * 4 + off
        return pltpu.make_async_remote_copy(
            src_ref=where, dst_ref=where, send_sem=ag_send.at[index], recv_sem=ag_recv.at[index],
            device_id=device_at(spot, axis, peer), device_id_type=MESH)

    def forward_copy(group, part, off):
        origin = lax.rem(spot[PLANE[part][0]] + 4 - off, 4)
        where = o.at[core, slots_of(group, part), :, aligned(origin * 32, 32), :]
        index = group * 8 + part * 4 + off
        return pltpu.make_async_remote_copy(
            src_ref=where, dst_ref=where, send_sem=fw_send.at[index], recv_sem=fw_recv.at[index],
            device_id=sibling, device_id_type=MESH)

    def pair_send_out(group):
        for part in range(2):
            pair_copy(group, part).start()

    def pair_add(group):
        for part in range(2):
            pair_copy(group, part).wait_recv()
            for slot in range(part * 4 + group * 2, part * 4 + group * 2 + 2):
                g[core, slot] += pair_got[slot]
            for off in (2, 1, 3):
                rs_copy(group, part, 0, off).start()

    def plane_add(group, stage):
        got_ref = first_got if stage == 0 else second_got
        for part in range(2):
            for off in (1, 3, 2):
                rs_copy(group, part, stage, off).wait_recv()
            rows = piece(part, stage, spot[PLANE[part][0]], spot[PLANE[part][1]])
            which = group * 2 + part
            g[core, slots_of(group, part), :, rows, :] += got_ref[which, 1] + got_ref[which, 2] + got_ref[which, 3]
            if stage == 0:
                for off in (2, 1, 3):
                    rs_copy(group, part, 1, off).start()

    z_order = (4, 3, 5, 2, 6, 1, 7)
    mine = spot["z"]

    def group_of(z):
        return lax.rem(z // 2, 2)

    def z_start(group):
        for off in z_order:
            @pl.when(group_of(lax.rem(mine + off, 8)) == group)
            def _():
                z_copy(off).start()

    def z_sum(group):
        @pl.when(group_of(mine) == group)
        def _():
            for off in range(1, 8):
                z_copy(off).wait_recv()
            total = g[core, mine, :, rows_of(mine), :]
            for off in range(1, 8):
                total = total + z_got[off]
            o[core, mine, :, rows_of(mine), :] = total
            for off in z_order:
                az_copy(off).start()

    def z_gather(group):
        for off in range(1, 8):
            @pl.when(group_of(lax.rem(mine + 8 - off, 8)) == group)
            def _():
                az_copy(off).wait_recv()
        for part in range(2):
            for off in (2, 1, 3):
                ag_copy(group, part, 1, off).start()

    def ag_middle(group):
        for part in range(2):
            for off in (1, 3, 2):
                ag_copy(group, part, 1, off).wait_recv()
            for off in (2, 1, 3):
                ag_copy(group, part, 0, off).start()
            forward_copy(group, part, 0).start()

    def ag_last(group):
        for off in (1, 3, 2):
            for part in range(2):
                ag_copy(group, part, 0, off).wait_recv()
                forward_copy(group, part, off).start()

    def ag_done(group):
        for part in range(2):
            for off in range(4):
                forward_copy(group, part, off).wait_recv()

    plain_scale = 1.0 / SAMPLES
    cyc_scale = 1.0 / math.sqrt(SAMPLES * ELEMS)

    def put(high_ref, low_ref, row, kind, col, value):
        rows = pl.ds(row * BLOCK, BLOCK)
        cols = pl.ds(kind * ELEMS + col * BLOCK, BLOCK)
        high_ref[rows, cols], low_ref[rows, cols] = split(value)

    def prepare(group):
        for parity in range(2):
            for slot in range(8):
                if slot // 2 % 2 != group:
                    continue
                i, j = SLOTS[parity][slot]
                for imag in (0, 1):
                    block = o[parity, slot, 1 + imag] * cyc_scale
                    put(ah, al, i, imag, j, block)
                    put(bh, bl, j, imag, i, -block.T if imag else block.T)
                block = o[parity, slot, 0] * plain_scale
                turned_block = block.T
                if i < j:
                    put(ah, al, i, 2, j, block)
                    put(ah, al, j, 2, i, turned_block)
                elif i > j:
                    put(ah, al, i, 3, j, block)
                    put(ah, al, j, 3, i, -turned_block)
                else:
                    row_ids = lax.broadcasted_iota(jnp.int32, (BLOCK, BLOCK), 0)
                    col_ids = lax.broadcasted_iota(jnp.int32, (BLOCK, BLOCK), 1)
                    put(ah, al, i, 2, i, jnp.where(row_ids <= col_ids, block, turned_block))
                    put(ah, al, i, 3, i, jnp.where(
                        row_ids > col_ids, block, jnp.where(row_ids < col_ids, -turned_block, 0.0)))

    lax.fori_loop(0, CHUNKS, early_chunk, 0)
    pair_send_out(0)
    late_chunk(0, 0)
    pair_add(0)
    lax.fori_loop(1, 4, late_chunk, 0)
    plane_add(0, 0)
    lax.fori_loop(4, CHUNKS, late_chunk, 0)
    pair_send_out(1)
    plane_add(0, 1)
    z_start(0)
    for group in range(2):
        for off in range(1, GROUP):
            start_copy(group, off).start()
    pair_add(1)
    z_sum(0)
    plane_add(1, 0)
    plane_add(1, 1)
    z_start(1)
    z_gather(0)
    ag_middle(0)
    z_sum(1)
    ag_last(0)
    z_gather(1)
    ag_done(0)
    ag_middle(1)
    prepare(0)
    for off in range(1, GROUP):
        for group in range(2):
            start_copy(group, off).wait_recv()
    ag_last(1)
    ag_done(1)
    prepare(1)

    lane = lax.broadcasted_iota(jnp.int32, (ELEMS, 2 * BEAMS), 1)

    def turned(vector):
        other = pltpu.roll(vector, BEAMS, 1)
        return jnp.where(lane < BEAMS, -other, other)

    def normalized(vector):
        squares = jnp.sum(vector * vector, axis=0, keepdims=True)
        squares = jnp.broadcast_to(squares, (8, 2 * BEAMS))
        squares = squares + pltpu.roll(squares, BEAMS, 1)
        return vector * (1.0 / jnp.sqrt(squares[:1] + EPS))

    def stacked(vector):
        high, low = split(jnp.concatenate([vector, turned(vector)], axis=0))
        return cat(high, low)

    def product(high, low, right):
        wide_out = dot_nn(high, right)
        return wide_out[:, :2 * BEAMS] + wide_out[:, 2 * BEAMS:] + dot_nn(low, right[:, :2 * BEAMS])

    v_ref[...] = normalized(sg[...])

    def step(iteration, carry):
        held = stacked(v_ref[...])
        mid = product(bh[...], bl[...], held)
        v_ref[...] = normalized(product(ah[...], al[...], jnp.concatenate([stacked(mid), held], axis=0)))
        return carry

    lax.fori_loop(0, ITERS, step, 0)
    mine = jnp.concatenate([v_ref[virtual(0), :], v_ref[virtual(1), :]], axis=0)
    weights_ref[...] = mine.T.reshape(2, BEAMS, OWN)

    vh, vl = split(v_ref[...].T)
    left = jnp.concatenate([vh, vl], axis=0)
    tap_fetch.wait()
    taps = tap_ref[:, aligned(me * PART, PART)].astype(F32) / 2048.0
    beams = ([], [])
    for frame in range(FRAMES):
        xh = cat(rh[frame * 2], rh[frame * 2 + 1])
        xl = cat(rl[frame * 2], rl[frame * 2 + 1])
        both = dot_nn(left, xh)
        out = both[:2 * BEAMS] + both[2 * BEAMS:] + dot_nn(vh, xl)
        top, low = out[:BEAMS], out[BEAMS:]
        beams[0].append(cat(*[top[:, c:c + CHUNK] + low[:, c + CHUNK:c + 2 * CHUNK] for c in (0, 2 * CHUNK)]))
        beams[1].append(cat(*[top[:, c + CHUNK:c + 2 * CHUNK] - low[:, c:c + CHUNK] for c in (0, 2 * CHUNK)]))

    def filtered(kind, frame):
        total = None
        for tap in range(TAPS):
            if 0 <= frame - tap < FRAMES:
                term = taps[tap:tap + 1, :] * beams[kind][frame - tap]
                total = term if total is None else total + term
        return total

    for kind in range(2):
        for frame in range(FRAMES):
            after[kind, frame] = filtered(kind, frame + FRAMES)

    def quarter(off):
        return aligned(lax.rem(me + off, GROUP) * QUARTER, QUARTER)

    def halo_copy(off):
        rows = quarter(off)
        return pltpu.make_async_remote_copy(
            src_ref=after.at[:, :, rows, :], dst_ref=halo.at[:, :, rows, :],
            send_sem=halo_send.at[off], recv_sem=halo_recv.at[off],
            device_id={"tm": tm + 1, "elem": me}, device_id_type=MESH)

    def cross_copy(off):
        return pltpu.make_async_remote_copy(
            src_ref=after.at[:, :, quarter(off), :], dst_ref=crossed.at[off],
            send_sem=cross_send.at[off], recv_sem=cross_recv.at[off],
            device_id={"tm": tm + 1, "elem": lax.rem(me + off, GROUP)}, device_id_type=MESH)

    def last_copy(off):
        return pltpu.make_async_remote_copy(
            src_ref=own.at[:, :, quarter(off), :], dst_ref=got.at[off],
            send_sem=last_send.at[off], recv_sem=last_recv.at[off],
            device_id={"elem": lax.rem(me + off, GROUP)}, device_id_type=MESH)

    order = (2, 1, 3, 0)

    @pl.when(near_out)
    def _():
        for off in order:
            halo_copy(off).start()

    @pl.when(cross_out)
    def _():
        for off in order:
            cross_copy(off).start()

    for kind in range(2):
        for frame in range(FRAMES):
            own[kind, frame] = filtered(kind, frame)

    for off in order:
        @pl.when(near_in)
        def _():
            halo_copy(off).wait_recv()
            rows = quarter(off)
            own[:, :, rows, :] += halo[:, :, rows, :]

        if off:
            last_copy(off).start()
        else:
            got[0] = own[:, :, quarter(0), :]

    table_copy.wait()
    rows = 2 * FRAMES * QUARTER
    half = FRAMES * QUARTER
    for position, off in enumerate((0, 1, 3, 2)):
        if off:
            last_copy(off).wait_recv()

        @pl.when(cross_in)
        def _():
            cross_copy(off).wait_recv()
            got[off] += crossed[off]

        high, low = split(got[off].reshape(rows, PART))
        left = jnp.concatenate([high, low], axis=0)
        where = aligned(lax.rem(me + GROUP - off, GROUP) * PART, PART)

        def times_table(index):
            both = dot_nn(left, table[index, where, :])
            return both[:rows] + both[rows:] + dot_nn(high, table[index + 1, where, :])

        with_cos = times_table(0)
        with_sin = times_table(2)
        real = with_cos[:half] + with_sin[half:]
        imag = with_cos[half:] - with_sin[:half]
        if position == 0:
            out_ref[0] = real
            out_ref[1] = imag
        else:
            out_ref[0] += real
            out_ref[1] += imag

    for off in range(1, GROUP):
        last_copy(off).wait_send()
        for group in range(2):
            start_copy(group, off).wait_send()
            for chunk in range(CHUNKS):
                sample_copy(group, chunk, off).wait_send()
        for part in range(2):
            for stage in range(2):
                for group in range(2):
                    rs_copy(group, part, stage, off).wait_send()
                    ag_copy(group, part, stage, off).wait_send()
    for off in range(1, 8):
        z_copy(off).wait_send()
        az_copy(off).wait_send()
    for part in range(2):
        for group in range(2):
            pair_copy(group, part).wait_send()
        for off in range(4):
            for group in range(2):
                forward_copy(group, part, off).wait_send()

    @pl.when(near_out)
    def _():
        for off in order:
            halo_copy(off).wait_send()

    @pl.when(cross_out)
    def _():
        for off in order:
            cross_copy(off).wait_send()


def finish_kernel(spectra_ref, weights_ref, spectra_out, weights_out):
    spectra_out[...] = spectra_ref[...]
    weights_out[...] = weights_ref[...]


def body(samples, shift_bin, start_vectors, tap_table):
    vmem = pl.BlockSpec(memory_space=pltpu.VMEM)
    smem = pl.BlockSpec(memory_space=pltpu.SMEM)
    hbm = pl.BlockSpec(memory_space=pl.ANY)
    dma = pltpu.SemaphoreType.DMA
    scratch = [
        ((2, BEAMS, OWN), jnp.int32),
        ((TAPS, CHANNELS), jnp.int32),
        ((CHUNKS, 2, ELEMS, CHUNK), F32),
        ((ELEMS, 2 * BEAMS), F32),
        ((2, 8, CHUNK), F32),
        ((CHUNKS, ELEMS, 2 * CHUNK), BF16),
        ((CHUNKS, ELEMS, 2 * CHUNK), BF16),
        ((CHUNKS, ELEMS, 2 * CHUNK), BF16),
        ((CHUNKS, ELEMS, 2 * CHUNK), BF16),
        ((2, 8, 3, BLOCK, BLOCK), F32),
        ((2, 8, 3, BLOCK, BLOCK), F32),
        ((8, 3, BLOCK, BLOCK), F32),
        ((4, 4, 2, 3, 32, BLOCK), F32),
        ((4, 4, 2, 3, 8, BLOCK), F32),
        ((8, 3, 8, BLOCK), F32),
        ((ELEMS, 2 * BEAMS), F32),
        ((ELEMS, 4 * ELEMS), BF16),
        ((ELEMS, 4 * ELEMS), BF16),
        ((ELEMS, 2 * ELEMS), BF16),
        ((ELEMS, 2 * ELEMS), BF16),
        ((4, CHANNELS, CHANNELS), BF16),
        ((2, FRAMES, BEAMS, PART), F32),
        ((2, FRAMES, BEAMS, PART), F32),
        ((2, FRAMES, BEAMS, PART), F32),
        ((GROUP, 2, FRAMES, QUARTER, PART), F32),
        ((GROUP, 2, FRAMES, QUARTER, PART), F32),
    ]
    semaphores = [
        (2 * CHUNKS, GROUP), (2 * CHUNKS, GROUP), (2 * CHUNKS,), (8,), (8,), None, (2,),
        (4,), (4,), (32,), (32,), (8,), (8,), (8,), (8,), (32,), (32,),
        (16,), (16,), (GROUP,), (GROUP,), (GROUP,), (GROUP,), (GROUP,), (GROUP,),
    ]
    spectra, weights = pl.pallas_call(
        kernel,
        out_shape=(
            jax.ShapeDtypeStruct((2, FRAMES * QUARTER, CHANNELS), F32),
            jax.ShapeDtypeStruct((2, BEAMS, OWN), F32),
        ),
        in_specs=[hbm, hbm, smem, hbm, hbm],
        out_specs=(vmem, vmem),
        scratch_shapes=[pltpu.VMEM(*entry) for entry in scratch]
        + [dma if shape is None else dma(shape) for shape in semaphores],
        compiler_params=pltpu.CompilerParams(
            collective_id=0, has_side_effects=True, vmem_limit_bytes=VMEM_LIMIT),
        name="beamformer",
    )(*[pltpu.with_memory_space_constraint(value, pltpu.HBM) for value in (samples, start_vectors.transpose(0, 2, 1))],
      shift_bin, pltpu.with_memory_space_constraint(tap_table, pltpu.HBM), jnp.asarray(dft_tables()))
    spectra, weights = pl.pallas_call(
        finish_kernel,
        out_shape=(
            jax.ShapeDtypeStruct((2, FRAMES * QUARTER, CHANNELS), F32),
            jax.ShapeDtypeStruct((2, BEAMS, OWN), F32),
        ),
        in_specs=[vmem, vmem],
        out_specs=(vmem, vmem),
        compiler_params=pltpu.CompilerParams(vmem_limit_bytes=4 * 1024 * 1024),
        name="finish",
    )(spectra, weights)
    spectra = spectra.reshape(2, FRAMES, QUARTER, CHANNELS).transpose(0, 2, 1, 3)
    return (spectra, weights.transpose(0, 2, 1))


def solution(mesh):
    return jax.shard_map(
        body,
        mesh=mesh,
        in_specs=(P(None, "elem", "tm"), P(), P(None, "elem", None), P()),
        out_specs=(P(None, "elem", "tm", None), P(None, "elem", None)),
        check_vma=False,
    )
```

```python
import math

import jax
import jax.numpy as jnp
import ml_dtypes
import numpy as np
from jax import lax
from jax.experimental import pallas as pl
from jax.experimental.pallas import tpu as pltpu
from jax.sharding import PartitionSpec as P

ELEMS = 512
BEAMS = 64
CHANNELS = 1024
TAPS = 4
ITERS = 3
SPAN = 3072
SAMPLES = 196608
FRAMES = SPAN // CHANNELS
GROUP = 4
OWN = ELEMS // GROUP
PART = CHANNELS // GROUP
TM = SAMPLES // SPAN
QUARTER = BEAMS // GROUP

EPS = 1e-06
F32 = jnp.float32
BF16 = jnp.bfloat16
MESH = pl.DeviceIdType.MESH
VMEM_LIMIT = 46 * 1024 * 1024

CHUNK = 128
EARLY = 96
LATE = OWN - EARLY
CHUNKS = SPAN // GROUP // CHUNK
BLOCK = 128
SIZES = {"core": 2, "x": 4, "y": 4, "z": 8}
PLANE = (("x", "y"), ("y", "x"))
SLOTS = (
    ((0, 0), (0, 2), (1, 1), (1, 3), (2, 0), (2, 2), (3, 1), (3, 3)),
    ((0, 1), (1, 0), (0, 3), (2, 3), (1, 2), (2, 1), (3, 0), (3, 2)),
)
SLOT_OF = {block: (parity, slot) for parity in range(2) for slot, block in enumerate(SLOTS[parity])}


def split(value):
    high = value.astype(BF16)
    return high, (value - high.astype(F32)).astype(BF16)


def dot_nt(left, right):
    return lax.dot_general(left, right, (((1,), (1,)), ((), ())), preferred_element_type=F32)


def dot_nn(left, right):
    return lax.dot_general(left, right, (((1,), (0,)), ((), ())), preferred_element_type=F32)


def cat(*pieces):
    return jnp.concatenate(pieces, axis=1)


def dft_tables():
    ids = np.arange(CHANNELS)
    angle = 2.0 * np.pi / CHANNELS * (ids[:, None] * ids[None, :] % CHANNELS)
    out = []
    for table in (np.cos(angle), np.sin(angle)):
        table = (table / math.sqrt(CHANNELS)).astype(np.float32)
        high = table.astype(ml_dtypes.bfloat16)
        out += [high, (table - high.astype(np.float32)).astype(ml_dtypes.bfloat16)]
    return np.stack(out)


def place():
    tm = lax.axis_index("tm")
    return {
        "core": lax.rem(tm, 2),
        "x": lax.rem(tm // 2, 4),
        "y": tm // 16,
        "z": lax.rem(tm // 8, 2) * 4 + lax.axis_index("elem"),
    }


def device_at(spot, axis, value):
    at = dict(spot)
    at[axis] = value
    tm = ((at["y"] * 2 + at["z"] // 4) * 4 + at["x"]) * 2 + at["core"]
    return {"tm": tm, "elem": lax.rem(at["z"], 4)}


def aligned(start, size):
    return pl.ds(pl.multiple_of(start, size), size)


def kernel(x_ref, start_hbm, shift_ref, tap_hbm, table_ref, out_ref, weights_ref,
           start_ref, tap_ref, xg, sg, phase, rh, rl, uh, ul, g, o, pair_got, first_got, second_got, z_got, v_ref, ah, al, bh, bl,
           table, own, after, halo, got, crossed,
           send_sem, recv_sem, own_sem, s_send, s_recv, table_sem, input_sem,
           pair_send, pair_recv, rs_send, rs_recv, z_send, z_recv, az_send, az_recv, ag_send, ag_recv,
           fw_send, fw_recv, halo_send, halo_recv, cross_send, cross_recv, last_send, last_recv):
    tm = lax.axis_index("tm")
    me = lax.axis_index("elem")
    spot = place()
    core = spot["core"]

    table_copy = pltpu.make_async_copy(table_ref, table, table_sem)
    start_fetch = pltpu.make_async_copy(start_hbm, start_ref, input_sem.at[0])
    tap_fetch = pltpu.make_async_copy(tap_hbm, tap_ref, input_sem.at[1])
    start_fetch.start()
    tap_fetch.start()

    barrier = pltpu.get_barrier_semaphore()
    count = 0
    for axis, size in SIZES.items():
        for off in range(1, size):
            pl.semaphore_signal(
                barrier, inc=1, device_id=device_at(spot, axis, lax.rem(spot[axis] + off, size)),
                device_id_type=MESH)
            count += 1
    turn = lax.rem(tm, 8)
    near_out = turn != 7
    near_in = turn != 0
    cross_out = jnp.logical_and(turn == 7, tm < TM - 1)
    cross_in = jnp.logical_and(turn == 0, tm > 0)

    @pl.when(near_out)
    def _():
        pl.semaphore_signal(barrier, inc=1, device_id={"tm": tm + 1, "elem": me}, device_id_type=MESH)

    @pl.when(near_in)
    def _():
        pl.semaphore_signal(barrier, inc=1, device_id={"tm": tm - 1, "elem": me}, device_id_type=MESH)

    @pl.when(cross_out)
    def _():
        for peer in range(GROUP):
            pl.semaphore_signal(barrier, inc=1, device_id={"tm": tm + 1, "elem": peer}, device_id_type=MESH)

    @pl.when(cross_in)
    def _():
        for peer in range(GROUP):
            pl.semaphore_signal(barrier, inc=1, device_id={"tm": tm - 1, "elem": peer}, device_id_type=MESH)

    number = lambda flag: flag.astype(jnp.int32)
    pl.semaphore_wait(
        barrier, count + number(near_out) + number(near_in) + GROUP * (number(cross_out) + number(cross_in)))

    firsts = (0, EARLY)
    counts = (EARLY, LATE)

    def virtual(group):
        return aligned(me * EARLY, EARLY) if group == 0 else aligned(GROUP * EARLY + me * LATE, LATE)

    def start_copy(group, off):
        where = sg.at[virtual(group), :]
        return pltpu.make_async_remote_copy(
            src_ref=where, dst_ref=where,
            send_sem=s_send.at[group * 4 + off], recv_sem=s_recv.at[group * 4 + off],
            device_id={"elem": lax.rem(me + off, GROUP)}, device_id_type=MESH)

    def columns(chunk, peer):
        return aligned(chunk // 2 * CHANNELS + peer * PART + lax.rem(chunk, 2) * CHUNK, CHUNK)

    def sample_copy(group, chunk, off):
        peer = lax.rem(me + off, GROUP)
        return pltpu.make_async_remote_copy(
            src_ref=x_ref.at[:, pl.ds(firsts[group], counts[group]), columns(chunk, peer)],
            dst_ref=xg.at[chunk, :, virtual(group), :],
            send_sem=send_sem.at[group * CHUNKS + chunk, off], recv_sem=recv_sem.at[group * CHUNKS + chunk, off],
            device_id={"elem": peer}, device_id_type=MESH)

    def own_copy(group, chunk):
        return pltpu.make_async_copy(
            x_ref.at[:, pl.ds(firsts[group], counts[group]), columns(chunk, me)],
            xg.at[chunk, :, virtual(group), :], own_sem.at[group * CHUNKS + chunk])

    def send_group(group):
        for chunk in range(CHUNKS):
            for off in (2, 1, 3):
                sample_copy(group, chunk, off).start()
            own_copy(group, chunk).start()

    send_group(0)
    send_group(1)
    table_copy.start()
    start_fetch.wait()
    starts = (start_ref[...].reshape(2 * BEAMS, OWN).astype(F32) - 4.5).T
    for group in range(2):
        sg[virtual(group), :] = starts[firsts[group]:firsts[group] + counts[group]]

    rows8 = lax.broadcasted_iota(jnp.int32, (8, CHUNK), 0)
    lanes = lax.broadcasted_iota(jnp.int32, (8, CHUNK), 1)
    times = tm * SPAN + rows8 // 2 * CHANNELS + me * PART + lax.rem(rows8, 2) * CHUNK + lanes
    turns = (times * shift_ref[0]).astype(F32)
    folded = turns - jnp.floor(turns * (1.0 / SAMPLES)) * SAMPLES
    folded = jnp.where(folded < 0.0, folded + SAMPLES, folded)
    folded = jnp.where(folded >= SAMPLES, folded - SAMPLES, folded)
    angle = 2.0 * math.pi / SAMPLES * folded
    phase[0] = jnp.cos(angle)
    phase[1] = jnp.sin(angle)
    g[...] = jnp.zeros_like(g)

    def triangle(size):
        return lax.broadcasted_iota(jnp.int32, (size, size), 0) <= lax.broadcasted_iota(jnp.int32, (size, size), 1)

    def left_of(high_ref, low_ref, chunk, rows, imag):
        high = high_ref[chunk, rows, :]
        low = low_ref[chunk, rows, :]
        if imag:
            high = cat(high[:, CHUNK:], -high[:, :CHUNK])
            low = cat(low[:, CHUNK:], -low[:, :CHUNK])
        return cat(high, high, low)

    def right_of(chunk, rows):
        high = rh[chunk, rows, :]
        return cat(high, rl[chunk, rows, :], high)

    def add_blocks(kind, first, first_col, value):
        for i in range(value.shape[0] // BLOCK):
            for j in range(value.shape[1] // BLOCK):
                parity, slot = SLOT_OF[(first + i, first_col + j)]
                g[parity, slot, kind] += value[i * BLOCK:(i + 1) * BLOCK, j * BLOCK:(j + 1) * BLOCK]

    def arrive(group, chunk):
        own_copy(group, chunk).wait()
        for off in range(1, GROUP):
            sample_copy(group, chunk, off).wait_recv()
        cos_row = phase[0, pl.ds(chunk, 1), :]
        sin_row = phase[1, pl.ds(chunk, 1), :]
        for block in ((0, 1, 2), (3,))[group]:
            rows = pl.ds(block * BLOCK, BLOCK)
            real = xg[chunk, 0, rows, :]
            imag = xg[chunk, 1, rows, :]
            rh[chunk, rows, :], rl[chunk, rows, :] = split(cat(real, imag))
            uh[chunk, rows, :], ul[chunk, rows, :] = split(
                cat(real * cos_row + imag * sin_row, imag * cos_row - real * sin_row))

    front = pl.ds(0, 3 * BLOCK)
    back = pl.ds(3 * BLOCK, BLOCK)

    def early_chunk(chunk, carry):
        arrive(0, chunk)
        out = dot_nt(jnp.concatenate(
            [left_of(uh, ul, chunk, front, 0), left_of(uh, ul, chunk, front, 1),
             left_of(rh, rl, chunk, front, 0), left_of(rh, rl, chunk, front, 1)], axis=0), right_of(chunk, front))
        size = 3 * BLOCK
        add_blocks(1, 0, 0, out[:size])
        add_blocks(2, 0, 0, out[size:2 * size])
        add_blocks(0, 0, 0, jnp.where(triangle(size), out[2 * size:3 * size], out[3 * size:]))
        return carry

    def late_columns(chunk):
        last = right_of(chunk, back)
        out = dot_nt(jnp.concatenate(
            [left_of(rh, rl, chunk, front, 0), left_of(uh, ul, chunk, front, 0), left_of(uh, ul, chunk, front, 1),
             left_of(rh, rl, chunk, back, 0)], axis=0), last)
        for kind in range(3):
            add_blocks(kind, 0, 3, out[kind * 3 * BLOCK:(kind + 1) * 3 * BLOCK])
        return out[9 * BLOCK:]

    def late_rows(chunk, corner):
        out = dot_nt(jnp.concatenate(
            [left_of(rh, rl, chunk, back, 1), left_of(uh, ul, chunk, back, 0), left_of(uh, ul, chunk, back, 1)],
            axis=0), right_of(chunk, pl.ds(0, ELEMS)))
        add_blocks(0, 3, 0, out[:BLOCK, :3 * BLOCK])
        add_blocks(0, 3, 3, jnp.where(triangle(BLOCK), corner, out[:BLOCK, 3 * BLOCK:]))
        for kind in (1, 2):
            add_blocks(kind, 3, 0, out[kind * BLOCK:(kind + 1) * BLOCK])

    def late_chunk(chunk, carry):
        arrive(1, chunk)
        late_rows(chunk, late_columns(chunk))
        return carry

    sibling = device_at(spot, "core", 1 - core)

    def slots_of(group, part):
        return pl.ds(part * 4 + group * 2, 2)

    def pair_copy(group, part):
        return pltpu.make_async_remote_copy(
            src_ref=g.at[1 - core, slots_of(group, part)], dst_ref=pair_got.at[slots_of(group, part)],
            send_sem=pair_send.at[group * 2 + part], recv_sem=pair_recv.at[group * 2 + part],
            device_id=sibling, device_id_type=MESH)

    def piece(part, stage, first, second):
        if stage == 0:
            return aligned(first * 32, 32)
        return aligned(first * 32 + second * 8, 8)

    def rs_copy(group, part, stage, off):
        axis = PLANE[part][stage]
        peer = lax.rem(spot[axis] + off, 4)
        rows = piece(part, 0, peer, 0) if stage == 0 else piece(part, 1, spot[PLANE[part][0]], peer)
        index = group * 16 + part * 8 + stage * 4 + off
        return pltpu.make_async_remote_copy(
            src_ref=g.at[core, slots_of(group, part), :, rows, :],
            dst_ref=(first_got if stage == 0 else second_got).at[group * 2 + part, off],
            send_sem=rs_send.at[index], recv_sem=rs_recv.at[index],
            device_id=device_at(spot, axis, peer), device_id_type=MESH)

    def rows_of(z):
        part = z // 4
        plane = (spot["x"] * 32 + spot["y"] * 8) * (1 - part) + (spot["y"] * 32 + spot["x"] * 8) * part
        return aligned(plane, 8)

    def z_copy(off):
        peer = lax.rem(spot["z"] + off, 8)
        return pltpu.make_async_remote_copy(
            src_ref=g.at[core, peer, :, rows_of(peer), :], dst_ref=z_got.at[off],
            send_sem=z_send.at[off], recv_sem=z_recv.at[off],
            device_id=device_at(spot, "z", peer), device_id_type=MESH)

    def az_copy(off):
        mine = spot["z"]
        where = o.at[core, mine, :, rows_of(mine), :]
        return pltpu.make_async_remote_copy(
            src_ref=where, dst_ref=where, send_sem=az_send.at[off], recv_sem=az_recv.at[off],
            device_id=device_at(spot, "z", lax.rem(mine + off, 8)), device_id_type=MESH)

    def ag_copy(group, part, stage, off):
        axis = PLANE[part][stage]
        peer = lax.rem(spot[axis] + off, 4)
        rows = piece(part, stage, spot[PLANE[part][0]], spot[PLANE[part][1]])
        where = o.at[core, slots_of(group, part), :, rows, :]
        index = group * 16 + part * 8 + stage * 4 + off
        return pltpu.make_async_remote_copy(
            src_ref=where, dst_ref=where, send_sem=ag_send.at[index], recv_sem=ag_recv.at[index],
            device_id=device_at(spot, axis, peer), device_id_type=MESH)

    def forward_copy(group, part, off):
        origin = lax.rem(spot[PLANE[part][0]] + 4 - off, 4)
        where = o.at[core, slots_of(group, part), :, aligned(origin * 32, 32), :]
        index = group * 8 + part * 4 + off
        return pltpu.make_async_remote_copy(
            src_ref=where, dst_ref=where, send_sem=fw_send.at[index], recv_sem=fw_recv.at[index],
            device_id=sibling, device_id_type=MESH)

    def pair_send_out(group):
        for part in range(2):
            pair_copy(group, part).start()

    def pair_add(group):
        for part in range(2):
            pair_copy(group, part).wait_recv()
            for slot in range(part * 4 + group * 2, part * 4 + group * 2 + 2):
                g[core, slot] += pair_got[slot]
            for off in (2, 1, 3):
                rs_copy(group, part, 0, off).start()

    def plane_add(group, stage):
        got_ref = first_got if stage == 0 else second_got
        for part in range(2):
            for off in (1, 3, 2):
                rs_copy(group, part, stage, off).wait_recv()
            rows = piece(part, stage, spot[PLANE[part][0]], spot[PLANE[part][1]])
            which = group * 2 + part
            g[core, slots_of(group, part), :, rows, :] += got_ref[which, 1] + got_ref[which, 2] + got_ref[which, 3]
            if stage == 0:
                for off in (2, 1, 3):
                    rs_copy(group, part, 1, off).start()

    z_order = (4, 3, 5, 2, 6, 1, 7)
    mine = spot["z"]

    def group_of(z):
        return lax.rem(z // 2, 2)

    def z_start(group):
        for off in z_order:
            @pl.when(group_of(lax.rem(mine + off, 8)) == group)
            def _():
                z_copy(off).start()

    def z_sum(group):
        @pl.when(group_of(mine) == group)
        def _():
            for off in range(1, 8):
                z_copy(off).wait_recv()
            total = g[core, mine, :, rows_of(mine), :]
            for off in range(1, 8):
                total = total + z_got[off]
            o[core, mine, :, rows_of(mine), :] = total
            for off in z_order:
                az_copy(off).start()

    def z_gather(group):
        for off in range(1, 8):
            @pl.when(group_of(lax.rem(mine + 8 - off, 8)) == group)
            def _():
                az_copy(off).wait_recv()
        for part in range(2):
            for off in (2, 1, 3):
                ag_copy(group, part, 1, off).start()

    def ag_middle(group):
        for part in range(2):
            for off in (1, 3, 2):
                ag_copy(group, part, 1, off).wait_recv()
            for off in (2, 1, 3):
                ag_copy(group, part, 0, off).start()
            forward_copy(group, part, 0).start()

    def ag_last(group):
        for off in (1, 3, 2):
            for part in range(2):
                ag_copy(group, part, 0, off).wait_recv()
                forward_copy(group, part, off).start()

    def ag_done(group):
        for part in range(2):
            for off in range(4):
                forward_copy(group, part, off).wait_recv()

    plain_scale = 1.0 / SAMPLES
    cyc_scale = 1.0 / math.sqrt(SAMPLES * ELEMS)

    def put(high_ref, low_ref, row, kind, col, value):
        rows = pl.ds(row * BLOCK, BLOCK)
        cols = pl.ds(kind * ELEMS + col * BLOCK, BLOCK)
        high_ref[rows, cols], low_ref[rows, cols] = split(value)

    def prepare(group):
        for parity in range(2):
            for slot in range(8):
                if slot // 2 % 2 != group:
                    continue
                i, j = SLOTS[parity][slot]
                for imag in (0, 1):
                    block = o[parity, slot, 1 + imag] * cyc_scale
                    put(ah, al, i, imag, j, block)
                    put(bh, bl, j, imag, i, -block.T if imag else block.T)
                block = o[parity, slot, 0] * plain_scale
                turned_block = block.T
                if i < j:
                    put(ah, al, i, 2, j, block)
                    put(ah, al, j, 2, i, turned_block)
                elif i > j:
                    put(ah, al, i, 3, j, block)
                    put(ah, al, j, 3, i, -turned_block)
                else:
                    row_ids = lax.broadcasted_iota(jnp.int32, (BLOCK, BLOCK), 0)
                    col_ids = lax.broadcasted_iota(jnp.int32, (BLOCK, BLOCK), 1)
                    put(ah, al, i, 2, i, jnp.where(row_ids <= col_ids, block, turned_block))
                    put(ah, al, i, 3, i, jnp.where(
                        row_ids > col_ids, block, jnp.where(row_ids < col_ids, -turned_block, 0.0)))

    lax.fori_loop(0, CHUNKS, early_chunk, 0)
    pair_send_out(0)
    late_chunk(0, 0)
    pair_add(0)
    lax.fori_loop(1, 4, late_chunk, 0)
    plane_add(0, 0)
    lax.fori_loop(4, CHUNKS - 1, late_chunk, 0)
    arrive(1, CHUNKS - 1)
    corner = late_columns(CHUNKS - 1)
    pair_copy(1, 0).start()
    late_rows(CHUNKS - 1, corner)
    pair_copy(1, 1).start()
    pair_add(1)
    plane_add(0, 1)
    z_start(0)
    for group in range(2):
        for off in range(1, GROUP):
            start_copy(group, off).start()
    z_sum(0)
    plane_add(1, 0)
    plane_add(1, 1)
    z_start(1)
    z_gather(0)
    ag_middle(0)
    z_sum(1)
    ag_last(0)
    z_gather(1)
    ag_done(0)
    ag_middle(1)
    prepare(0)
    for off in range(1, GROUP):
        for group in range(2):
            start_copy(group, off).wait_recv()
    ag_last(1)
    ag_done(1)
    prepare(1)

    lane = lax.broadcasted_iota(jnp.int32, (ELEMS, 2 * BEAMS), 1)

    def turned(vector):
        other = pltpu.roll(vector, BEAMS, 1)
        return jnp.where(lane < BEAMS, -other, other)

    def normalized(vector):
        squares = jnp.sum(vector * vector, axis=0, keepdims=True)
        squares = jnp.broadcast_to(squares, (8, 2 * BEAMS))
        squares = squares + pltpu.roll(squares, BEAMS, 1)
        return vector * (1.0 / jnp.sqrt(squares[:1] + EPS))

    def stacked(vector):
        high, low = split(jnp.concatenate([vector, turned(vector)], axis=0))
        return cat(high, low)

    def product(high, low, right):
        wide_out = dot_nn(high, right)
        return wide_out[:, :2 * BEAMS] + wide_out[:, 2 * BEAMS:] + dot_nn(low, right[:, :2 * BEAMS])

    v_ref[...] = normalized(sg[...])

    def step(iteration, carry):
        held = stacked(v_ref[...])
        mid = product(bh[...], bl[...], held)
        v_ref[...] = normalized(product(ah[...], al[...], jnp.concatenate([stacked(mid), held], axis=0)))
        return carry

    lax.fori_loop(0, ITERS, step, 0)
    mine = jnp.concatenate([v_ref[virtual(0), :], v_ref[virtual(1), :]], axis=0)
    weights_ref[...] = mine.T.reshape(2, BEAMS, OWN)

    vh, vl = split(v_ref[...].T)
    left = jnp.concatenate([vh, vl], axis=0)
    tap_fetch.wait()
    taps = tap_ref[:, aligned(me * PART, PART)].astype(F32) / 2048.0
    beams = ([], [])
    for frame in range(FRAMES):
        xh = cat(rh[frame * 2], rh[frame * 2 + 1])
        xl = cat(rl[frame * 2], rl[frame * 2 + 1])
        both = dot_nn(left, xh)
        out = both[:2 * BEAMS] + both[2 * BEAMS:] + dot_nn(vh, xl)
        top, low = out[:BEAMS], out[BEAMS:]
        beams[0].append(cat(*[top[:, c:c + CHUNK] + low[:, c + CHUNK:c + 2 * CHUNK] for c in (0, 2 * CHUNK)]))
        beams[1].append(cat(*[top[:, c + CHUNK:c + 2 * CHUNK] - low[:, c:c + CHUNK] for c in (0, 2 * CHUNK)]))

    def filtered(kind, frame):
        total = None
        for tap in range(TAPS):
            if 0 <= frame - tap < FRAMES:
                term = taps[tap:tap + 1, :] * beams[kind][frame - tap]
                total = term if total is None else total + term
        return total

    for kind in range(2):
        for frame in range(FRAMES):
            after[kind, frame] = filtered(kind, frame + FRAMES)

    def quarter(off):
        return aligned(lax.rem(me + off, GROUP) * QUARTER, QUARTER)

    def halo_copy(off):
        rows = quarter(off)
        return pltpu.make_async_remote_copy(
            src_ref=after.at[:, :, rows, :], dst_ref=halo.at[:, :, rows, :],
            send_sem=halo_send.at[off], recv_sem=halo_recv.at[off],
            device_id={"tm": tm + 1, "elem": me}, device_id_type=MESH)

    def cross_copy(off):
        return pltpu.make_async_remote_copy(
            src_ref=after.at[:, :, quarter(off), :], dst_ref=crossed.at[off],
            send_sem=cross_send.at[off], recv_sem=cross_recv.at[off],
            device_id={"tm": tm + 1, "elem": lax.rem(me + off, GROUP)}, device_id_type=MESH)

    def last_copy(off):
        return pltpu.make_async_remote_copy(
            src_ref=own.at[:, :, quarter(off), :], dst_ref=got.at[off],
            send_sem=last_send.at[off], recv_sem=last_recv.at[off],
            device_id={"elem": lax.rem(me + off, GROUP)}, device_id_type=MESH)

    order = (2, 1, 3, 0)

    @pl.when(near_out)
    def _():
        for off in order:
            halo_copy(off).start()

    @pl.when(cross_out)
    def _():
        for off in order:
            cross_copy(off).start()

    for kind in range(2):
        for frame in range(FRAMES):
            own[kind, frame] = filtered(kind, frame)

    for off in order:
        @pl.when(near_in)
        def _():
            halo_copy(off).wait_recv()
            rows = quarter(off)
            own[:, :, rows, :] += halo[:, :, rows, :]

        if off:
            last_copy(off).start()
        else:
            got[0] = own[:, :, quarter(0), :]

    table_copy.wait()
    rows = 2 * FRAMES * QUARTER
    half = FRAMES * QUARTER
    for position, off in enumerate((0, 1, 3, 2)):
        if off:
            last_copy(off).wait_recv()

        @pl.when(cross_in)
        def _():
            cross_copy(off).wait_recv()
            got[off] += crossed[off]

        high, low = split(got[off].reshape(rows, PART))
        left = jnp.concatenate([high, low], axis=0)
        where = aligned(lax.rem(me + GROUP - off, GROUP) * PART, PART)

        def times_table(index):
            both = dot_nn(left, table[index, where, :])
            return both[:rows] + both[rows:] + dot_nn(high, table[index + 1, where, :])

        with_cos = times_table(0)
        with_sin = times_table(2)
        real = with_cos[:half] + with_sin[half:]
        imag = with_cos[half:] - with_sin[:half]
        if position == 0:
            out_ref[0] = real
            out_ref[1] = imag
        else:
            out_ref[0] += real
            out_ref[1] += imag

    for off in range(1, GROUP):
        last_copy(off).wait_send()
        for group in range(2):
            start_copy(group, off).wait_send()
            for chunk in range(CHUNKS):
                sample_copy(group, chunk, off).wait_send()
        for part in range(2):
            for stage in range(2):
                for group in range(2):
                    rs_copy(group, part, stage, off).wait_send()
                    ag_copy(group, part, stage, off).wait_send()
    for off in range(1, 8):
        z_copy(off).wait_send()
        az_copy(off).wait_send()
    for part in range(2):
        for group in range(2):
            pair_copy(group, part).wait_send()
        for off in range(4):
            for group in range(2):
                forward_copy(group, part, off).wait_send()

    @pl.when(near_out)
    def _():
        for off in order:
            halo_copy(off).wait_send()

    @pl.when(cross_out)
    def _():
        for off in order:
            cross_copy(off).wait_send()


def finish_kernel(spectra_ref, weights_ref, spectra_out, weights_out):
    spectra_out[...] = spectra_ref[...]
    weights_out[...] = weights_ref[...]


def body(samples, shift_bin, start_vectors, tap_table):
    vmem = pl.BlockSpec(memory_space=pltpu.VMEM)
    smem = pl.BlockSpec(memory_space=pltpu.SMEM)
    hbm = pl.BlockSpec(memory_space=pl.ANY)
    dma = pltpu.SemaphoreType.DMA
    scratch = [
        ((2, BEAMS, OWN), jnp.int32),
        ((TAPS, CHANNELS), jnp.int32),
        ((CHUNKS, 2, ELEMS, CHUNK), F32),
        ((ELEMS, 2 * BEAMS), F32),
        ((2, 8, CHUNK), F32),
        ((CHUNKS, ELEMS, 2 * CHUNK), BF16),
        ((CHUNKS, ELEMS, 2 * CHUNK), BF16),
        ((CHUNKS, ELEMS, 2 * CHUNK), BF16),
        ((CHUNKS, ELEMS, 2 * CHUNK), BF16),
        ((2, 8, 3, BLOCK, BLOCK), F32),
        ((2, 8, 3, BLOCK, BLOCK), F32),
        ((8, 3, BLOCK, BLOCK), F32),
        ((4, 4, 2, 3, 32, BLOCK), F32),
        ((4, 4, 2, 3, 8, BLOCK), F32),
        ((8, 3, 8, BLOCK), F32),
        ((ELEMS, 2 * BEAMS), F32),
        ((ELEMS, 4 * ELEMS), BF16),
        ((ELEMS, 4 * ELEMS), BF16),
        ((ELEMS, 2 * ELEMS), BF16),
        ((ELEMS, 2 * ELEMS), BF16),
        ((4, CHANNELS, CHANNELS), BF16),
        ((2, FRAMES, BEAMS, PART), F32),
        ((2, FRAMES, BEAMS, PART), F32),
        ((2, FRAMES, BEAMS, PART), F32),
        ((GROUP, 2, FRAMES, QUARTER, PART), F32),
        ((GROUP, 2, FRAMES, QUARTER, PART), F32),
    ]
    semaphores = [
        (2 * CHUNKS, GROUP), (2 * CHUNKS, GROUP), (2 * CHUNKS,), (8,), (8,), None, (2,),
        (4,), (4,), (32,), (32,), (8,), (8,), (8,), (8,), (32,), (32,),
        (16,), (16,), (GROUP,), (GROUP,), (GROUP,), (GROUP,), (GROUP,), (GROUP,),
    ]
    spectra, weights = pl.pallas_call(
        kernel,
        out_shape=(
            jax.ShapeDtypeStruct((2, FRAMES * QUARTER, CHANNELS), F32),
            jax.ShapeDtypeStruct((2, BEAMS, OWN), F32),
        ),
        in_specs=[hbm, hbm, smem, hbm, hbm],
        out_specs=(vmem, vmem),
        scratch_shapes=[pltpu.VMEM(*entry) for entry in scratch]
        + [dma if shape is None else dma(shape) for shape in semaphores],
        compiler_params=pltpu.CompilerParams(
            collective_id=0, has_side_effects=True, vmem_limit_bytes=VMEM_LIMIT),
        name="beamformer",
    )(*[pltpu.with_memory_space_constraint(value, pltpu.HBM) for value in (samples, start_vectors.transpose(0, 2, 1))],
      shift_bin, pltpu.with_memory_space_constraint(tap_table, pltpu.HBM), jnp.asarray(dft_tables()))
    spectra, weights = pl.pallas_call(
        finish_kernel,
        out_shape=(
            jax.ShapeDtypeStruct((2, FRAMES * QUARTER, CHANNELS), F32),
            jax.ShapeDtypeStruct((2, BEAMS, OWN), F32),
        ),
        in_specs=[vmem, vmem],
        out_specs=(vmem, vmem),
        compiler_params=pltpu.CompilerParams(vmem_limit_bytes=4 * 1024 * 1024),
        name="finish",
    )(spectra, weights)
    spectra = spectra.reshape(2, FRAMES, QUARTER, CHANNELS).transpose(0, 2, 1, 3)
    return (spectra, weights.transpose(0, 2, 1))


def solution(mesh):
    return jax.shard_map(
        body,
        mesh=mesh,
        in_specs=(P(None, "elem", "tm"), P(), P(None, "elem", None), P()),
        out_specs=(P(None, "elem", "tm", None), P(None, "elem", None)),
        check_vma=False,
    )
```

```python
import math

import jax
import jax.numpy as jnp
import ml_dtypes
import numpy as np
from jax import lax
from jax.experimental import pallas as pl
from jax.experimental.pallas import tpu as pltpu
from jax.sharding import PartitionSpec as P

ELEMS = 512
BEAMS = 64
CHANNELS = 1024
TAPS = 4
ITERS = 3
SPAN = 3072
SAMPLES = 196608
FRAMES = SPAN // CHANNELS
GROUP = 4
OWN = ELEMS // GROUP
PART = CHANNELS // GROUP
TM = SAMPLES // SPAN
QUARTER = BEAMS // GROUP

EPS = 1e-06
F32 = jnp.float32
BF16 = jnp.bfloat16
MESH = pl.DeviceIdType.MESH
VMEM_LIMIT = 46 * 1024 * 1024

CHUNK = 128
EARLY = 96
LATE = OWN - EARLY
CHUNKS = SPAN // GROUP // CHUNK
BLOCK = 128
SIZES = {"core": 2, "x": 4, "y": 4, "z": 8}
PLANE = (("x", "y"), ("y", "x"))
SLOTS = (
    ((0, 0), (0, 2), (1, 1), (1, 3), (2, 0), (2, 2), (3, 1), (3, 3)),
    ((0, 1), (1, 0), (0, 3), (2, 3), (1, 2), (2, 1), (3, 0), (3, 2)),
)
SLOT_OF = {block: (parity, slot) for parity in range(2) for slot, block in enumerate(SLOTS[parity])}


def split(value):
    high = value.astype(BF16)
    return high, (value - high.astype(F32)).astype(BF16)


def dot_nt(left, right):
    return lax.dot_general(left, right, (((1,), (1,)), ((), ())), preferred_element_type=F32)


def dot_nn(left, right):
    return lax.dot_general(left, right, (((1,), (0,)), ((), ())), preferred_element_type=F32)


def cat(*pieces):
    return jnp.concatenate(pieces, axis=1)


def dft_tables():
    ids = np.arange(CHANNELS)
    angle = 2.0 * np.pi / CHANNELS * (ids[:, None] * ids[None, :] % CHANNELS)
    out = []
    for table in (np.cos(angle), np.sin(angle)):
        table = (table / math.sqrt(CHANNELS)).astype(np.float32)
        high = table.astype(ml_dtypes.bfloat16)
        out += [high, (table - high.astype(np.float32)).astype(ml_dtypes.bfloat16)]
    return np.stack(out)


def place():
    tm = lax.axis_index("tm")
    return {
        "core": lax.rem(tm, 2),
        "x": lax.rem(tm // 2, 4),
        "y": tm // 16,
        "z": lax.rem(tm // 8, 2) * 4 + lax.axis_index("elem"),
    }


def device_at(spot, axis, value):
    at = dict(spot)
    at[axis] = value
    tm = ((at["y"] * 2 + at["z"] // 4) * 4 + at["x"]) * 2 + at["core"]
    return {"tm": tm, "elem": lax.rem(at["z"], 4)}


def aligned(start, size):
    return pl.ds(pl.multiple_of(start, size), size)


def kernel(x_ref, start_hbm, shift_ref, tap_hbm, table_ref, out_ref, weights_ref,
           start_ref, tap_ref, xg, sg, phase, rh, rl, uh, ul, g, o, pair_got, first_got, second_got, z_got, v_ref, ah, al, bh, bl,
           table, own, after, halo, got, crossed,
           send_sem, recv_sem, own_sem, s_send, s_recv, table_sem, input_sem,
           pair_send, pair_recv, rs_send, rs_recv, z_send, z_recv, az_send, az_recv, ag_send, ag_recv,
           fw_send, fw_recv, halo_send, halo_recv, cross_send, cross_recv, last_send, last_recv):
    tm = lax.axis_index("tm")
    me = lax.axis_index("elem")
    spot = place()
    core = spot["core"]

    table_copy = pltpu.make_async_copy(table_ref, table, table_sem)
    start_fetch = pltpu.make_async_copy(start_hbm, start_ref, input_sem.at[0])
    tap_fetch = pltpu.make_async_copy(tap_hbm, tap_ref, input_sem.at[1])
    start_fetch.start()
    tap_fetch.start()

    barrier = pltpu.get_barrier_semaphore()
    count = 0
    for axis, size in SIZES.items():
        for off in range(1, size):
            pl.semaphore_signal(
                barrier, inc=1, device_id=device_at(spot, axis, lax.rem(spot[axis] + off, size)),
                device_id_type=MESH)
            count += 1
    turn = lax.rem(tm, 8)
    near_out = turn != 7
    near_in = turn != 0
    cross_out = jnp.logical_and(turn == 7, tm < TM - 1)
    cross_in = jnp.logical_and(turn == 0, tm > 0)

    @pl.when(near_out)
    def _():
        pl.semaphore_signal(barrier, inc=1, device_id={"tm": tm + 1, "elem": me}, device_id_type=MESH)

    @pl.when(near_in)
    def _():
        pl.semaphore_signal(barrier, inc=1, device_id={"tm": tm - 1, "elem": me}, device_id_type=MESH)

    @pl.when(cross_out)
    def _():
        for peer in range(GROUP):
            pl.semaphore_signal(barrier, inc=1, device_id={"tm": tm + 1, "elem": peer}, device_id_type=MESH)

    @pl.when(cross_in)
    def _():
        for peer in range(GROUP):
            pl.semaphore_signal(barrier, inc=1, device_id={"tm": tm - 1, "elem": peer}, device_id_type=MESH)

    number = lambda flag: flag.astype(jnp.int32)
    pl.semaphore_wait(
        barrier, count + number(near_out) + number(near_in) + GROUP * (number(cross_out) + number(cross_in)))

    firsts = (0, EARLY)
    counts = (EARLY, LATE)

    def virtual(group):
        return aligned(me * EARLY, EARLY) if group == 0 else aligned(GROUP * EARLY + me * LATE, LATE)

    def start_copy(group, off):
        where = sg.at[virtual(group), :]
        return pltpu.make_async_remote_copy(
            src_ref=where, dst_ref=where,
            send_sem=s_send.at[group * 4 + off], recv_sem=s_recv.at[group * 4 + off],
            device_id={"elem": lax.rem(me + off, GROUP)}, device_id_type=MESH)

    def columns(chunk, peer):
        return aligned(chunk // 2 * CHANNELS + peer * PART + lax.rem(chunk, 2) * CHUNK, CHUNK)

    def sample_copy(group, chunk, off):
        peer = lax.rem(me + off, GROUP)
        return pltpu.make_async_remote_copy(
            src_ref=x_ref.at[:, pl.ds(firsts[group], counts[group]), columns(chunk, peer)],
            dst_ref=xg.at[chunk, :, virtual(group), :],
            send_sem=send_sem.at[group * CHUNKS + chunk, off], recv_sem=recv_sem.at[group * CHUNKS + chunk, off],
            device_id={"elem": peer}, device_id_type=MESH)

    def own_copy(group, chunk):
        return pltpu.make_async_copy(
            x_ref.at[:, pl.ds(firsts[group], counts[group]), columns(chunk, me)],
            xg.at[chunk, :, virtual(group), :], own_sem.at[group * CHUNKS + chunk])

    def send_group(group):
        for chunk in range(CHUNKS):
            for off in (2, 1, 3):
                sample_copy(group, chunk, off).start()
            own_copy(group, chunk).start()

    send_group(0)
    send_group(1)
    table_copy.start()
    start_fetch.wait()
    starts = (start_ref[...].reshape(2 * BEAMS, OWN).astype(F32) - 4.5).T
    for group in range(2):
        sg[virtual(group), :] = starts[firsts[group]:firsts[group] + counts[group]]

    rows8 = lax.broadcasted_iota(jnp.int32, (8, CHUNK), 0)
    lanes = lax.broadcasted_iota(jnp.int32, (8, CHUNK), 1)
    times = tm * SPAN + rows8 // 2 * CHANNELS + me * PART + lax.rem(rows8, 2) * CHUNK + lanes
    turns = (times * shift_ref[0]).astype(F32)
    folded = turns - jnp.floor(turns * (1.0 / SAMPLES)) * SAMPLES
    folded = jnp.where(folded < 0.0, folded + SAMPLES, folded)
    folded = jnp.where(folded >= SAMPLES, folded - SAMPLES, folded)
    angle = 2.0 * math.pi / SAMPLES * folded
    phase[0] = jnp.cos(angle)
    phase[1] = jnp.sin(angle)
    g[...] = jnp.zeros_like(g)

    def triangle(size):
        return lax.broadcasted_iota(jnp.int32, (size, size), 0) <= lax.broadcasted_iota(jnp.int32, (size, size), 1)

    def left_of(high_ref, low_ref, chunk, rows, imag):
        high = high_ref[chunk, rows, :]
        low = low_ref[chunk, rows, :]
        if imag:
            high = cat(high[:, CHUNK:], -high[:, :CHUNK])
            low = cat(low[:, CHUNK:], -low[:, :CHUNK])
        return cat(high, high, low)

    def right_of(chunk, rows):
        high = rh[chunk, rows, :]
        return cat(high, rl[chunk, rows, :], high)

    def add_blocks(kind, first, first_col, value):
        for i in range(value.shape[0] // BLOCK):
            for j in range(value.shape[1] // BLOCK):
                parity, slot = SLOT_OF[(first + i, first_col + j)]
                g[parity, slot, kind] += value[i * BLOCK:(i + 1) * BLOCK, j * BLOCK:(j + 1) * BLOCK]

    def arrive(group, chunk):
        own_copy(group, chunk).wait()
        for off in range(1, GROUP):
            sample_copy(group, chunk, off).wait_recv()
        cos_row = phase[0, pl.ds(chunk, 1), :]
        sin_row = phase[1, pl.ds(chunk, 1), :]
        for block in ((0, 1, 2), (3,))[group]:
            rows = pl.ds(block * BLOCK, BLOCK)
            real = xg[chunk, 0, rows, :]
            imag = xg[chunk, 1, rows, :]
            rh[chunk, rows, :], rl[chunk, rows, :] = split(cat(real, imag))
            uh[chunk, rows, :], ul[chunk, rows, :] = split(
                cat(real * cos_row + imag * sin_row, imag * cos_row - real * sin_row))

    front = pl.ds(0, 3 * BLOCK)
    back = pl.ds(3 * BLOCK, BLOCK)

    def early_chunk(chunk, carry):
        arrive(0, chunk)
        out = dot_nt(jnp.concatenate(
            [left_of(uh, ul, chunk, front, 0), left_of(uh, ul, chunk, front, 1),
             left_of(rh, rl, chunk, front, 0), left_of(rh, rl, chunk, front, 1)], axis=0), right_of(chunk, front))
        size = 3 * BLOCK
        add_blocks(1, 0, 0, out[:size])
        add_blocks(2, 0, 0, out[size:2 * size])
        add_blocks(0, 0, 0, jnp.where(triangle(size), out[2 * size:3 * size], out[3 * size:]))
        return carry

    def late_columns(chunk):
        last = right_of(chunk, back)
        out = dot_nt(jnp.concatenate(
            [left_of(rh, rl, chunk, front, 0), left_of(uh, ul, chunk, front, 0), left_of(uh, ul, chunk, front, 1),
             left_of(rh, rl, chunk, back, 0)], axis=0), last)
        for kind in range(3):
            add_blocks(kind, 0, 3, out[kind * 3 * BLOCK:(kind + 1) * 3 * BLOCK])
        return out[9 * BLOCK:]

    def late_rows(chunk, corner):
        out = dot_nt(jnp.concatenate(
            [left_of(rh, rl, chunk, back, 1), left_of(uh, ul, chunk, back, 0), left_of(uh, ul, chunk, back, 1)],
            axis=0), right_of(chunk, pl.ds(0, ELEMS)))
        add_blocks(0, 3, 0, out[:BLOCK, :3 * BLOCK])
        add_blocks(0, 3, 3, jnp.where(triangle(BLOCK), corner, out[:BLOCK, 3 * BLOCK:]))
        for kind in (1, 2):
            add_blocks(kind, 3, 0, out[kind * BLOCK:(kind + 1) * BLOCK])

    def late_chunk(chunk, carry):
        arrive(1, chunk)
        late_rows(chunk, late_columns(chunk))
        return carry

    sibling = device_at(spot, "core", 1 - core)

    def slots_of(group, part):
        return pl.ds(part * 4 + group * 2, 2)

    def pair_copy(group, part):
        return pltpu.make_async_remote_copy(
            src_ref=g.at[1 - core, slots_of(group, part)], dst_ref=pair_got.at[slots_of(group, part)],
            send_sem=pair_send.at[group * 2 + part], recv_sem=pair_recv.at[group * 2 + part],
            device_id=sibling, device_id_type=MESH)

    def piece(part, stage, first, second):
        if stage == 0:
            return aligned(first * 32, 32)
        return aligned(first * 32 + second * 8, 8)

    def rs_copy(group, part, stage, off):
        axis = PLANE[part][stage]
        peer = lax.rem(spot[axis] + off, 4)
        rows = piece(part, 0, peer, 0) if stage == 0 else piece(part, 1, spot[PLANE[part][0]], peer)
        index = group * 16 + part * 8 + stage * 4 + off
        return pltpu.make_async_remote_copy(
            src_ref=g.at[core, slots_of(group, part), :, rows, :],
            dst_ref=(first_got if stage == 0 else second_got).at[group * 2 + part, off],
            send_sem=rs_send.at[index], recv_sem=rs_recv.at[index],
            device_id=device_at(spot, axis, peer), device_id_type=MESH)

    def rows_of(z):
        part = z // 4
        plane = (spot["x"] * 32 + spot["y"] * 8) * (1 - part) + (spot["y"] * 32 + spot["x"] * 8) * part
        return aligned(plane, 8)

    def z_copy(off):
        peer = lax.rem(spot["z"] + off, 8)
        return pltpu.make_async_remote_copy(
            src_ref=g.at[core, peer, :, rows_of(peer), :], dst_ref=z_got.at[off],
            send_sem=z_send.at[off], recv_sem=z_recv.at[off],
            device_id=device_at(spot, "z", peer), device_id_type=MESH)

    def az_copy(off):
        mine = spot["z"]
        where = o.at[core, mine, :, rows_of(mine), :]
        return pltpu.make_async_remote_copy(
            src_ref=where, dst_ref=where, send_sem=az_send.at[off], recv_sem=az_recv.at[off],
            device_id=device_at(spot, "z", lax.rem(mine + off, 8)), device_id_type=MESH)

    def ag_copy(group, part, stage, off):
        axis = PLANE[part][stage]
        peer = lax.rem(spot[axis] + off, 4)
        rows = piece(part, stage, spot[PLANE[part][0]], spot[PLANE[part][1]])
        where = o.at[core, slots_of(group, part), :, rows, :]
        index = group * 16 + part * 8 + stage * 4 + off
        return pltpu.make_async_remote_copy(
            src_ref=where, dst_ref=where, send_sem=ag_send.at[index], recv_sem=ag_recv.at[index],
            device_id=device_at(spot, axis, peer), device_id_type=MESH)

    def forward_copy(group, part, off):
        origin = lax.rem(spot[PLANE[part][0]] + 4 - off, 4)
        where = o.at[core, slots_of(group, part), :, aligned(origin * 32, 32), :]
        index = group * 8 + part * 4 + off
        return pltpu.make_async_remote_copy(
            src_ref=where, dst_ref=where, send_sem=fw_send.at[index], recv_sem=fw_recv.at[index],
            device_id=sibling, device_id_type=MESH)

    def pair_send_out(group):
        for part in range(2):
            pair_copy(group, part).start()

    def pair_add(group):
        for part in range(2):
            pair_copy(group, part).wait_recv()
            for slot in range(part * 4 + group * 2, part * 4 + group * 2 + 2):
                g[core, slot] += pair_got[slot]
            for off in (2, 1, 3):
                rs_copy(group, part, 0, off).start()

    def plane_add(group, stage):
        got_ref = first_got if stage == 0 else second_got
        for part in range(2):
            for off in (1, 3, 2):
                rs_copy(group, part, stage, off).wait_recv()
            rows = piece(part, stage, spot[PLANE[part][0]], spot[PLANE[part][1]])
            which = group * 2 + part
            g[core, slots_of(group, part), :, rows, :] += got_ref[which, 1] + got_ref[which, 2] + got_ref[which, 3]
            if stage == 0:
                for off in (2, 1, 3):
                    rs_copy(group, part, 1, off).start()

    z_order = (4, 3, 5, 2, 6, 1, 7)
    mine = spot["z"]

    def group_of(z):
        return lax.rem(z // 2, 2)

    def z_start(group):
        for off in z_order:
            @pl.when(group_of(lax.rem(mine + off, 8)) == group)
            def _():
                z_copy(off).start()

    def z_sum(group):
        @pl.when(group_of(mine) == group)
        def _():
            for off in range(1, 8):
                z_copy(off).wait_recv()
            total = g[core, mine, :, rows_of(mine), :]
            for off in range(1, 8):
                total = total + z_got[off]
            o[core, mine, :, rows_of(mine), :] = total
            for off in z_order:
                az_copy(off).start()

    def z_gather(group):
        for off in range(1, 8):
            @pl.when(group_of(lax.rem(mine + 8 - off, 8)) == group)
            def _():
                az_copy(off).wait_recv()
        for part in range(2):
            for off in (2, 1, 3):
                ag_copy(group, part, 1, off).start()

    def ag_middle(group):
        for part in range(2):
            for off in (1, 3, 2):
                ag_copy(group, part, 1, off).wait_recv()
            for off in (2, 1, 3):
                ag_copy(group, part, 0, off).start()
            forward_copy(group, part, 0).start()

    def ag_last(group):
        for off in (1, 3, 2):
            for part in range(2):
                ag_copy(group, part, 0, off).wait_recv()
                forward_copy(group, part, off).start()

    def ag_done(group):
        for part in range(2):
            for off in range(4):
                forward_copy(group, part, off).wait_recv()

    plain_scale = 1.0 / SAMPLES
    cyc_scale = 1.0 / math.sqrt(SAMPLES * ELEMS)

    def put(high_ref, low_ref, row, kind, col, value):
        rows = pl.ds(row * BLOCK, BLOCK)
        cols = pl.ds(kind * ELEMS + col * BLOCK, BLOCK)
        high_ref[rows, cols], low_ref[rows, cols] = split(value)

    def prepare(group):
        for parity in range(2):
            for slot in range(8):
                if slot // 2 % 2 != group:
                    continue
                i, j = SLOTS[parity][slot]
                for imag in (0, 1):
                    block = o[parity, slot, 1 + imag] * cyc_scale
                    put(ah, al, i, imag, j, block)
                    put(bh, bl, j, imag, i, -block.T if imag else block.T)
                block = o[parity, slot, 0] * plain_scale
                turned_block = block.T
                if i < j:
                    put(ah, al, i, 2, j, block)
                    put(ah, al, j, 2, i, turned_block)
                elif i > j:
                    put(ah, al, i, 3, j, block)
                    put(ah, al, j, 3, i, -turned_block)
                else:
                    row_ids = lax.broadcasted_iota(jnp.int32, (BLOCK, BLOCK), 0)
                    col_ids = lax.broadcasted_iota(jnp.int32, (BLOCK, BLOCK), 1)
                    put(ah, al, i, 2, i, jnp.where(row_ids <= col_ids, block, turned_block))
                    put(ah, al, i, 3, i, jnp.where(
                        row_ids > col_ids, block, jnp.where(row_ids < col_ids, -turned_block, 0.0)))

    lax.fori_loop(0, CHUNKS, early_chunk, 0)
    pair_send_out(0)
    late_chunk(0, 0)
    pair_add(0)
    lax.fori_loop(1, 4, late_chunk, 0)
    plane_add(0, 0)
    lax.fori_loop(4, CHUNKS - 1, late_chunk, 0)
    arrive(1, CHUNKS - 1)
    corner = late_columns(CHUNKS - 1)
    pair_copy(1, 0).start()
    late_rows(CHUNKS - 1, corner)
    pair_copy(1, 1).start()
    pair_add(1)
    plane_add(0, 1)
    z_start(0)
    for group in range(2):
        for off in range(1, GROUP):
            start_copy(group, off).start()
    z_sum(0)
    plane_add(1, 0)
    plane_add(1, 1)
    z_start(1)
    z_gather(0)
    ag_middle(0)
    z_sum(1)
    ag_last(0)
    z_gather(1)
    ag_done(0)
    ag_middle(1)
    prepare(0)
    for off in range(1, GROUP):
        for group in range(2):
            start_copy(group, off).wait_recv()
    ag_last(1)
    ag_done(1)
    prepare(1)

    lane = lax.broadcasted_iota(jnp.int32, (ELEMS, 2 * BEAMS), 1)

    def turned(vector):
        other = pltpu.roll(vector, BEAMS, 1)
        return jnp.where(lane < BEAMS, -other, other)

    def normalized(vector):
        squares = jnp.sum(vector * vector, axis=0, keepdims=True)
        squares = jnp.broadcast_to(squares, (8, 2 * BEAMS))
        squares = squares + pltpu.roll(squares, BEAMS, 1)
        return vector * (1.0 / jnp.sqrt(squares[:1] + EPS))

    def stacked(vector):
        high, low = split(jnp.concatenate([vector, turned(vector)], axis=0))
        return cat(high, low)

    def product(high, low, right):
        wide_out = dot_nn(high, right)
        return wide_out[:, :2 * BEAMS] + wide_out[:, 2 * BEAMS:] + dot_nn(low, right[:, :2 * BEAMS])

    v_ref[...] = normalized(sg[...])

    def step(iteration, carry):
        held = stacked(v_ref[...])
        mid = product(bh[...], bl[...], held)
        v_ref[...] = normalized(product(ah[...], al[...], jnp.concatenate([stacked(mid), held], axis=0)))
        return carry

    lax.fori_loop(0, ITERS, step, 0)
    mine = jnp.concatenate([v_ref[virtual(0), :], v_ref[virtual(1), :]], axis=0)
    weights_ref[...] = mine.T.reshape(2, BEAMS, OWN)

    vh, vl = split(v_ref[...].T)
    left = jnp.concatenate([vh, vl], axis=0)
    tap_fetch.wait()
    taps = tap_ref[:, aligned(me * PART, PART)].astype(F32) / 2048.0
    beams = ([], [])
    both = dot_nn(left, cat(*[rh[chunk] for chunk in range(CHUNKS)]))
    every = both[:2 * BEAMS] + both[2 * BEAMS:] + dot_nn(vh, cat(*[rl[chunk] for chunk in range(CHUNKS)]))
    for frame in range(FRAMES):
        out = every[:, frame * 4 * CHUNK:(frame + 1) * 4 * CHUNK]
        top, low = out[:BEAMS], out[BEAMS:]
        beams[0].append(cat(*[top[:, c:c + CHUNK] + low[:, c + CHUNK:c + 2 * CHUNK] for c in (0, 2 * CHUNK)]))
        beams[1].append(cat(*[top[:, c + CHUNK:c + 2 * CHUNK] - low[:, c:c + CHUNK] for c in (0, 2 * CHUNK)]))

    def filtered(kind, frame):
        total = None
        for tap in range(TAPS):
            if 0 <= frame - tap < FRAMES:
                term = taps[tap:tap + 1, :] * beams[kind][frame - tap]
                total = term if total is None else total + term
        return total

    for kind in range(2):
        for frame in range(FRAMES):
            after[kind, frame] = filtered(kind, frame + FRAMES)

    def quarter(off):
        return aligned(lax.rem(me + off, GROUP) * QUARTER, QUARTER)

    def halo_copy(off):
        rows = quarter(off)
        return pltpu.make_async_remote_copy(
            src_ref=after.at[:, :, rows, :], dst_ref=halo.at[:, :, rows, :],
            send_sem=halo_send.at[off], recv_sem=halo_recv.at[off],
            device_id={"tm": tm + 1, "elem": me}, device_id_type=MESH)

    def cross_copy(off):
        return pltpu.make_async_remote_copy(
            src_ref=after.at[:, :, quarter(off), :], dst_ref=crossed.at[off],
            send_sem=cross_send.at[off], recv_sem=cross_recv.at[off],
            device_id={"tm": tm + 1, "elem": lax.rem(me + off, GROUP)}, device_id_type=MESH)

    def last_copy(off):
        return pltpu.make_async_remote_copy(
            src_ref=own.at[:, :, quarter(off), :], dst_ref=got.at[off],
            send_sem=last_send.at[off], recv_sem=last_recv.at[off],
            device_id={"elem": lax.rem(me + off, GROUP)}, device_id_type=MESH)

    order = (2, 1, 3, 0)

    @pl.when(near_out)
    def _():
        for off in order:
            halo_copy(off).start()

    @pl.when(cross_out)
    def _():
        for off in order:
            cross_copy(off).start()

    for kind in range(2):
        for frame in range(FRAMES):
            own[kind, frame] = filtered(kind, frame)

    for off in order:
        @pl.when(near_in)
        def _():
            halo_copy(off).wait_recv()
            rows = quarter(off)
            own[:, :, rows, :] += halo[:, :, rows, :]

        if off:
            last_copy(off).start()
        else:
            got[0] = own[:, :, quarter(0), :]

    table_copy.wait()
    rows = 2 * FRAMES * QUARTER
    half = FRAMES * QUARTER
    for position, off in enumerate((0, 1, 3, 2)):
        if off:
            last_copy(off).wait_recv()

        @pl.when(cross_in)
        def _():
            cross_copy(off).wait_recv()
            got[off] += crossed[off]

        high, low = split(got[off].reshape(rows, PART))
        left = jnp.concatenate([high, low], axis=0)
        where = aligned(lax.rem(me + GROUP - off, GROUP) * PART, PART)

        def times_table(index):
            both = dot_nn(left, table[index, where, :])
            return both[:rows] + both[rows:] + dot_nn(high, table[index + 1, where, :])

        with_cos = times_table(0)
        with_sin = times_table(2)
        real = with_cos[:half] + with_sin[half:]
        imag = with_cos[half:] - with_sin[:half]
        if position == 0:
            out_ref[0] = real
            out_ref[1] = imag
        else:
            out_ref[0] += real
            out_ref[1] += imag

    for off in range(1, GROUP):
        last_copy(off).wait_send()
        for group in range(2):
            start_copy(group, off).wait_send()
            for chunk in range(CHUNKS):
                sample_copy(group, chunk, off).wait_send()
        for part in range(2):
            for stage in range(2):
                for group in range(2):
                    rs_copy(group, part, stage, off).wait_send()
                    ag_copy(group, part, stage, off).wait_send()
    for off in range(1, 8):
        z_copy(off).wait_send()
        az_copy(off).wait_send()
    for part in range(2):
        for group in range(2):
            pair_copy(group, part).wait_send()
        for off in range(4):
            for group in range(2):
                forward_copy(group, part, off).wait_send()

    @pl.when(near_out)
    def _():
        for off in order:
            halo_copy(off).wait_send()

    @pl.when(cross_out)
    def _():
        for off in order:
            cross_copy(off).wait_send()


def finish_kernel(spectra_ref, weights_ref, spectra_out, weights_out):
    spectra_out[...] = spectra_ref[...]
    weights_out[...] = weights_ref[...]


def body(samples, shift_bin, start_vectors, tap_table):
    vmem = pl.BlockSpec(memory_space=pltpu.VMEM)
    smem = pl.BlockSpec(memory_space=pltpu.SMEM)
    hbm = pl.BlockSpec(memory_space=pl.ANY)
    dma = pltpu.SemaphoreType.DMA
    scratch = [
        ((2, BEAMS, OWN), jnp.int32),
        ((TAPS, CHANNELS), jnp.int32),
        ((CHUNKS, 2, ELEMS, CHUNK), F32),
        ((ELEMS, 2 * BEAMS), F32),
        ((2, 8, CHUNK), F32),
        ((CHUNKS, ELEMS, 2 * CHUNK), BF16),
        ((CHUNKS, ELEMS, 2 * CHUNK), BF16),
        ((CHUNKS, ELEMS, 2 * CHUNK), BF16),
        ((CHUNKS, ELEMS, 2 * CHUNK), BF16),
        ((2, 8, 3, BLOCK, BLOCK), F32),
        ((2, 8, 3, BLOCK, BLOCK), F32),
        ((8, 3, BLOCK, BLOCK), F32),
        ((4, 4, 2, 3, 32, BLOCK), F32),
        ((4, 4, 2, 3, 8, BLOCK), F32),
        ((8, 3, 8, BLOCK), F32),
        ((ELEMS, 2 * BEAMS), F32),
        ((ELEMS, 4 * ELEMS), BF16),
        ((ELEMS, 4 * ELEMS), BF16),
        ((ELEMS, 2 * ELEMS), BF16),
        ((ELEMS, 2 * ELEMS), BF16),
        ((4, CHANNELS, CHANNELS), BF16),
        ((2, FRAMES, BEAMS, PART), F32),
        ((2, FRAMES, BEAMS, PART), F32),
        ((2, FRAMES, BEAMS, PART), F32),
        ((GROUP, 2, FRAMES, QUARTER, PART), F32),
        ((GROUP, 2, FRAMES, QUARTER, PART), F32),
    ]
    semaphores = [
        (2 * CHUNKS, GROUP), (2 * CHUNKS, GROUP), (2 * CHUNKS,), (8,), (8,), None, (2,),
        (4,), (4,), (32,), (32,), (8,), (8,), (8,), (8,), (32,), (32,),
        (16,), (16,), (GROUP,), (GROUP,), (GROUP,), (GROUP,), (GROUP,), (GROUP,),
    ]
    spectra, weights = pl.pallas_call(
        kernel,
        out_shape=(
            jax.ShapeDtypeStruct((2, FRAMES * QUARTER, CHANNELS), F32),
            jax.ShapeDtypeStruct((2, BEAMS, OWN), F32),
        ),
        in_specs=[hbm, hbm, smem, hbm, hbm],
        out_specs=(vmem, vmem),
        scratch_shapes=[pltpu.VMEM(*entry) for entry in scratch]
        + [dma if shape is None else dma(shape) for shape in semaphores],
        compiler_params=pltpu.CompilerParams(
            collective_id=0, has_side_effects=True, vmem_limit_bytes=VMEM_LIMIT),
        name="beamformer",
    )(*[pltpu.with_memory_space_constraint(value, pltpu.HBM) for value in (samples, start_vectors.transpose(0, 2, 1))],
      shift_bin, pltpu.with_memory_space_constraint(tap_table, pltpu.HBM), jnp.asarray(dft_tables()))
    spectra, weights = pl.pallas_call(
        finish_kernel,
        out_shape=(
            jax.ShapeDtypeStruct((2, FRAMES * QUARTER, CHANNELS), F32),
            jax.ShapeDtypeStruct((2, BEAMS, OWN), F32),
        ),
        in_specs=[vmem, vmem],
        out_specs=(vmem, vmem),
        compiler_params=pltpu.CompilerParams(vmem_limit_bytes=4 * 1024 * 1024),
        name="finish",
    )(spectra, weights)
    spectra = spectra.reshape(2, FRAMES, QUARTER, CHANNELS).transpose(0, 2, 1, 3)
    return (spectra, weights.transpose(0, 2, 1))


def solution(mesh):
    return jax.shard_map(
        body,
        mesh=mesh,
        in_specs=(P(None, "elem", "tm"), P(), P(None, "elem", None), P()),
        out_specs=(P(None, "elem", "tm", None), P(None, "elem", None)),
        check_vma=False,
    )
```
